128 devices in a mesh: vocab: 8 (over z, y_lo), rows: 16 (over y_hi, x, core).
Axes of the slice: x: 4, y: 4 (y_hi: 2, y_lo: 2; y = y_hi * 2 + y_lo), z: 4, core: 2. Of those that a mesh axis runs over, the one named last changes fastest.
Arguments:
- hidden_pass: bfloat16 [192, 64, 4096], P('rows', None, 'vocab'), may hold values from -6 to 6
- hidden_query: bfloat16 [192, 8, 4096], P('rows', None, 'vocab'), may hold values from -6 to 6
- mask_pass: int32 [192, 64], P('rows'), may hold values 0 or 1
- mask_query: int32 [192, 8], P('rows'), may hold values 0 or 1
- labels: int32 [192], P('rows'), may hold values from 0 to 191, each once
- head_weight: bfloat16 [4096, 16384], P('rows', 'vocab'), may hold values from -1 to 1
Outputs:
- grad_pass: bfloat16 [192, 64, 4096], P('rows', None, 'vocab')
- grad_query: bfloat16 [192, 8, 4096], P('rows', None, 'vocab')
The draws below stay inside these ranges and needn't reach their ends.
Inputs may be any that keep to these rules, and one draw needn't show every extreme that they name: `labels`: each passage is the positive of exactly one query.
All inputs are finite; a program needn't handle non-finite values. No bound on the sum of `mask_pass` or of `mask_query` on one device may be relied on, other than what follows from the above.
Results may differ from the reference program's by a relative error of at most 0.018.
The reference program's roundings to bfloat16 on the way count: a program that leaves them out, or rounds other values in their place, can miss the bound.
Values may be sent and summed in bfloat16 or wider, within the bound.
A program may use at most 128 MiB of HBM per device.

```python
import jax
import jax.numpy as jnp
from jax import lax

D = 4096
V = 16384
LP = 64
LQ = 8
ROW_DEV = 12
PASSAGES = 192
QUERIES = 192
N_VOCAB = 8


def draw_head_weight(key, part):
    entry_key = jax.random.fold_in(key, 11)
    column_key = jax.random.fold_in(key, 12)
    position = jnp.arange(V, dtype=jnp.float32)[None, :] / V
    rough = jnp.exp(jax.random.uniform(column_key, (1, V), jnp.float32, jnp.log(0.7), jnp.log(1.4)))
    entries = jnp.clip(jax.random.normal(entry_key, (D, V), jnp.float32), -6.0, 6.0)
    ramp = 0.5 * jnp.exp(position * jnp.log(8.0))
    values = jnp.clip(entries * D ** (-0.5) * ramp * rough, -1.0, 1.0)
    return values.astype(jnp.bfloat16)


def plant(values, stream_key, least, top_value):
    index_at = [jax.random.randint(jax.random.fold_in(stream_key, axis), (), 0, length) for axis, length in enumerate(values.shape)]
    main_axis = values.shape.index(max(values.shape))
    neighbour = index_at[:main_axis] + [(index_at[main_axis] + 1) % values.shape[main_axis]] + index_at[main_axis + 1:]
    return values.at[tuple(index_at)].set(least).at[tuple(neighbour)].set(top_value)


def steps_of(own_key, dims, cuts, least, high):
    gain = 1.0
    for dim, blocks in cuts:
        draws = jax.random.uniform(jax.random.fold_in(jax.random.fold_in(own_key, 6), dim), (blocks,), jnp.float32, least / len(cuts), high / len(cuts))
        gain = gain * jnp.repeat(jnp.exp(draws), dims[dim] // blocks).reshape((-1,) + (1,) * (len(dims) - 1 - dim))
    return gain


def bell_draw(own_key, extent, width, bound, pieces=(), kind=jnp.bfloat16):
    result = jax.random.normal(own_key, extent, jnp.float32) * width
    if len(pieces) > 0:
        result = steps_of(own_key, extent, pieces, -0.22, 0.18) * result
    return jnp.clip(result, min=-bound, max=bound).astype(kind)


def setup_inputs(seed: int = 0) -> dict:
    streams_of = jax.random.split(jax.random.key(seed), 7)
    return {
        "hidden_pass": bell_draw(streams_of[0], (PASSAGES, LP, D), 1.0, 6.0, ((0, 16), (2, 8))),
        "hidden_query": bell_draw(streams_of[1], (QUERIES, LQ, D), 1.0, 6.0, ((0, 16), (2, 8))),
        "mask_pass": plant((jax.random.randint(streams_of[2], (PASSAGES, LP), 0, 4) < 3).astype(jnp.int32), jax.random.fold_in(streams_of[2], 1), 0, 1),
        "mask_query": plant((jax.random.randint(streams_of[3], (QUERIES, LQ), 0, 4) < 3).astype(jnp.int32), jax.random.fold_in(streams_of[3], 1), 0, 1),
        "labels": jax.random.permutation(streams_of[4], PASSAGES).astype(jnp.int32),
        "head_weight": draw_head_weight(jax.random.fold_in(streams_of[6], 71), 0),
    }


MARGIN = 1.0
SHARPNESS = 16.0

def activate(logits):
    return jnp.log1p(jnp.maximum(logits, 0.0))

def pool_rows(logits, mask, groups, length):
    values = activate(logits).reshape(groups, length, -1)
    weight = mask.astype(jnp.float32)[:, :, None]
    totals = lax.optimization_barrier(jnp.sum(values ** 4 * weight, axis=1))
    sparse = (jnp.power(totals + 1.0, 0.25) - 1.0).astype(jnp.bfloat16)
    return (values, totals, sparse)

def logit_slopes(sparse_grad, values, totals, logits, mask, groups, length):
    weight = mask.astype(jnp.float32)[:, :, None]
    factor = sparse_grad * jnp.power(totals + 1.0, -0.75)
    slopes = 1.0 / (1.0 + jnp.maximum(logits, 0.0)).reshape(groups, length, -1)
    gradient = factor[:, None, :] * weight * values ** 3 * slopes
    return gradient.astype(jnp.bfloat16).reshape(groups * length, -1)

def side_logits(hidden, head_weight):
    return jnp.dot(hidden.reshape(hidden.shape[0] * hidden.shape[1], hidden.shape[2]), head_weight, preferred_element_type=jnp.float32)

def side_sparse(hidden, mask, head_weight):
    blocks = hidden.shape[0] // ROW_DEV

    def single(bundle):
        block_hidden, block_mask = bundle
        logits = side_logits(block_hidden, head_weight)
        return pool_rows(logits, block_mask, ROW_DEV, block_hidden.shape[1])[2]
    stacked = lax.map(single, (hidden.reshape(blocks, ROW_DEV, hidden.shape[1], hidden.shape[2]), mask.reshape(blocks, ROW_DEV, mask.shape[1])))
    return stacked.reshape(hidden.shape[0], -1)

def side_grad(hidden, mask, sparse_grad, head_weight):
    blocks = hidden.shape[0] // ROW_DEV
    slice_width = V // N_VOCAB

    def single(bundle):
        block_hidden, block_mask, block_grad = bundle
        length = block_hidden.shape[1]
        logits = side_logits(block_hidden, head_weight)
        values, totals, unused_sparse = pool_rows(logits, block_mask, ROW_DEV, length)
        slopes = logit_slopes(block_grad, values, totals, logits, block_mask, ROW_DEV, length)
        summed = jnp.zeros((ROW_DEV * length, D), jnp.float32)
        for slice_index in range(N_VOCAB):
            lower = slice_index * slice_width
            upper = lower + slice_width
            partial_value = lax.dot_general(slopes[:, lower:upper], head_weight[:, lower:upper], (((1,), (1,)), ((), ())), preferred_element_type=jnp.float32)
            summed = summed + lax.optimization_barrier(partial_value.astype(jnp.bfloat16)).astype(jnp.float32)
        return summed.astype(jnp.bfloat16).reshape(ROW_DEV, length, D)
    stacked = lax.map(single, (hidden.reshape(blocks, ROW_DEV, hidden.shape[1], hidden.shape[2]), mask.reshape(blocks, ROW_DEV, mask.shape[1]), sparse_grad.reshape(blocks, ROW_DEV, sparse_grad.shape[1])))
    return stacked.reshape(hidden.shape)

def reference(hidden_pass, hidden_query, mask_pass, mask_query, labels, head_weight):
    sparse_pass = side_sparse(hidden_pass, mask_pass, head_weight)
    sparse_query = side_sparse(hidden_query, mask_query, head_weight)
    scaling = SHARPNESS * V ** (-0.5)
    scores = jnp.dot(sparse_query, sparse_pass.T, preferred_element_type=jnp.float32) * scaling
    onehot = (labels[:, None] == jnp.arange(sparse_pass.shape[0], dtype=jnp.int32)[None, :]).astype(jnp.float32)
    positive = lax.optimization_barrier(jnp.sum(scores * onehot, axis=1, keepdims=True))
    weights = jax.nn.sigmoid(MARGIN + scores - positive) * (1.0 - onehot)
    score_grad = ((weights - onehot * lax.optimization_barrier(jnp.sum(weights, axis=1, keepdims=True))) * scaling).astype(jnp.bfloat16)
    query_sparse_grad = jnp.dot(score_grad, sparse_pass, preferred_element_type=jnp.float32)
    pass_sparse_grad = jnp.dot(score_grad.T, sparse_query, preferred_element_type=jnp.float32)
    grad_pass = side_grad(hidden_pass, mask_pass, pass_sparse_grad, head_weight)
    grad_query = side_grad(hidden_query, mask_query, query_sparse_grad, head_weight)
    return (grad_pass, grad_query)
```

```python
import jax
import jax.numpy as jnp
from jax import lax
from jax.experimental import pallas as pl
from jax.experimental.pallas import tpu as pltpu
from jax.sharding import PartitionSpec as P

MESH = pl.DeviceIdType.MESH
MARGIN = 1.0
SHARPNESS = 16.0
V = 16384
SCALING = SHARPNESS * V ** (-0.5)

G = 12
LP = 64
LQ = 8
PR = G * LP
QR = G * LQ
R = PR + QR
RH = R // 2
F = 512
W = 2048
HD = 256
HH = HD // 2
PAD = 16
ROWS = 16
VOCAB = 8
BF = jnp.bfloat16
F32 = jnp.float32

RELATIVE = [(1, 0), (3, 0), (2, 0), (0, 1), (1, 1), (3, 1), (2, 1)]


def where_am_i():
    v = lax.axis_index("vocab")
    r = lax.axis_index("rows")
    return v // 2, v % 2, r // 8, (r // 2) % 4, r % 2


def device(z, yl, yh, x, c):
    return (z * 2 + yl, (yh * 4 + x) * 2 + c)


def kernel(
    hp_ref,
    hq_ref,
    mp_ref,
    mq_ref,
    lab_ref,
    hw_ref,
    gp_ref,
    gq_ref,
    tok,
    head,
    acc,
    slopes,
    totals,
    factor,
    allp,
    allq,
    sbuf,
    gbuf,
    rhalf,
    rfull,
    ybuf,
    lsem,
    ssem,
    rsem,
):
    z, yl, yh, x, c = where_am_i()
    v = z * 2 + yl
    r = (yh * 4 + x) * 2 + c
    zs = [z, (z + 1) % 4, (z + 2) % 4, (z + 3) % 4]
    xs = [x, (x + 1) % 4, (x + 2) % 4, (x + 3) % 4]
    yls = [yl, 1 - yl]
    yhs = [yh, 1 - yh]
    cs = [c, 1 - c]
    zdev = [device(k, yl, yh, x, c) for k in zs]
    xdev = [device(z, yl, yh, k, c) for k in xs]
    yldev = device(z, 1 - yl, yh, x, c)
    yhdev = device(z, yl, 1 - yh, x, c)
    cdev = device(z, yl, yh, x, 1 - c)

    own_head = yh * 4 + x
    local = [
        pltpu.make_async_copy(hp_ref, tok.at[v, pl.ds(0, PR)], lsem.at[0]),
        pltpu.make_async_copy(hq_ref, tok.at[v, pl.ds(PR, QR)], lsem.at[1]),
        pltpu.make_async_copy(hw_ref, head.at[own_head, pl.ds(c * HD, HD)], lsem.at[2]),
    ]
    for copy in local:
        copy.start()

    peers = [device(zs[d], yls[e], yh, x, c) for d, e in RELATIVE]
    peers += [device(z, yl, yhs[e], xs[d], c) for d, e in RELATIVE]
    peers += [device(z, yl, yhs[e], xs[d], 1 - c) for d, e in [(0, 0)] + RELATIVE]
    barrier = pltpu.get_barrier_semaphore()
    for peer in peers:
        pl.semaphore_signal(barrier, inc=1, device_id=peer, device_id_type=MESH)
    pl.semaphore_wait(barrier, len(peers))
    for copy in local:
        copy.wait()

    counter = [0]
    sent = []

    def remote(src, dst, dev):
        k = counter[0]
        counter[0] += 1
        copy = pltpu.make_async_remote_copy(
            src_ref=src,
            dst_ref=dst,
            send_sem=ssem.at[k],
            recv_sem=rsem.at[k],
            device_id=dev,
            device_id_type=MESH,
        )
        copy.start()
        return copy

    def send(ref, dev):
        copy = remote(ref, ref, dev)
        sent.append(copy)
        return copy

    def hid(dz, dy, h):
        return tok.at[zs[dz] * 2 + yls[dy], pl.ds(h * RH, RH)]

    def hed(dx, dy, h):
        return head.at[yhs[dy] * 4 + xs[dx], pl.ds(c * HD + h * HH, HH)]

    a, b, s = {}, {}, {}
    tok_sent = []

    def a_send(key, ref, dev):
        copy = remote(ref, ref, dev)
        a[key] = copy
        tok_sent.append(copy)

    def b_send(key, ref, dev):
        b[key] = send(ref, dev)

    def to_core(dx, dy, h):
        s[(dx, dy, h)] = send(hed(dx, dy, h), cdev)

    a_send(("y", 0), hid(0, 0, 0), yldev)
    b_send(("y", 0), hed(0, 0, 0), yhdev)
    a_send(("+", 0), hid(0, 0, 0), zdev[1])
    a_send(("-", 1), hid(0, 0, 1), zdev[3])
    b_send(("+", 0), hed(0, 0, 0), xdev[1])
    b_send(("-", 1), hed(0, 0, 1), xdev[3])
    a_send(("y", 1), hid(0, 0, 1), yldev)
    b_send(("y", 1), hed(0, 0, 1), yhdev)
    a_send(("+", 1), hid(0, 0, 1), zdev[1])
    a_send(("-", 0), hid(0, 0, 0), zdev[3])
    b_send(("+", 1), hed(0, 0, 1), xdev[1])
    b_send(("-", 0), hed(0, 0, 0), xdev[3])
    to_core(0, 0, 0)
    to_core(0, 0, 1)

    a[("+", 0)].wait_recv()
    a_send("f+", hid(3, 0, 0), zdev[1])
    a[("-", 1)].wait_recv()
    a_send("f-", hid(1, 0, 1), zdev[3])
    b[("+", 0)].wait_recv()
    b_send("f+", hed(3, 0, 0), xdev[1])
    b[("-", 1)].wait_recv()
    b_send("f-", hed(1, 0, 1), xdev[3])
    to_core(3, 0, 0)
    to_core(1, 0, 1)

    a[("y", 0)].wait_recv()
    a_send(("o+", 0), hid(0, 1, 0), zdev[1])
    a_send(("o-", 0), hid(0, 1, 0), zdev[3])
    b[("y", 0)].wait_recv()
    b_send(("o+", 0), hed(0, 1, 0), xdev[1])
    b_send(("o-", 0), hed(0, 1, 0), xdev[3])
    a[("y", 1)].wait_recv()
    a_send(("o-", 1), hid(0, 1, 1), zdev[3])
    a_send(("o+", 1), hid(0, 1, 1), zdev[1])
    b[("y", 1)].wait_recv()
    b_send(("o-", 1), hed(0, 1, 1), xdev[3])
    b_send(("o+", 1), hed(0, 1, 1), xdev[1])
    to_core(0, 1, 0)
    to_core(0, 1, 1)
    b[("+", 1)].wait_recv()
    to_core(3, 0, 1)
    b[("-", 0)].wait_recv()
    to_core(1, 0, 0)
    a[("o+", 0)].wait_recv()
    a_send("g+", hid(3, 1, 0), zdev[1])
    b[("o+", 0)].wait_recv()
    b_send("g+", hed(3, 1, 0), xdev[1])
    to_core(3, 1, 0)
    a[("o-", 1)].wait_recv()
    a_send("g-", hid(1, 1, 1), zdev[3])
    b[("o-", 1)].wait_recv()
    b_send("g-", hed(1, 1, 1), xdev[3])
    to_core(1, 1, 1)
    b["f+"].wait_recv()
    to_core(2, 0, 0)
    b["f-"].wait_recv()
    to_core(2, 0, 1)
    for key in [("+", 1), ("-", 0), "f+", "f-", ("o-", 0), ("o+", 1), "g+", "g-"]:
        a[key].wait_recv()

    def mm1(dx, dy, first):
        slot = yhs[dy] * 4 + xs[dx]
        for h in (0, 1):
            s[(dx, dy, h)].wait_recv()

        @pl.loop(0, W // 256)
        def _(n):
            cols = pl.ds(pl.multiple_of(n * 256, 256), 256)
            product = jnp.dot(tok[slot], head[slot, :, cols], preferred_element_type=F32)
            if first:
                acc[:, cols] = product
            else:
                acc[:, cols] += product

    mm1(0, 0, True)
    mm1(1, 0, False)
    mm1(3, 0, False)
    b[("o+", 1)].wait_recv()
    to_core(3, 1, 1)
    b[("o-", 0)].wait_recv()
    to_core(1, 1, 0)
    mm1(0, 1, False)
    mm1(2, 0, False)
    mm1(1, 1, False)
    mm1(3, 1, False)
    b["g+"].wait_recv()
    to_core(2, 1, 0)
    b["g-"].wait_recv()
    to_core(2, 1, 1)
    mm1(2, 1, False)

    totals[...] = jnp.zeros_like(totals)

    def pool(base, length, mask_ref, k, side):
        rows = pl.ds(pl.multiple_of(base + k * length, 8), length)
        line = mask_ref[pl.ds(k, 1), :].astype(F32)
        eye = lax.broadcasted_iota(jnp.int32, (length, length), 0) == lax.broadcasted_iota(
            jnp.int32, (length, length), 1
        )
        weight = jnp.sum(
            jnp.where(eye, jnp.broadcast_to(line, (length, length)), 0.0), axis=1, keepdims=True
        )
        for n in range(W // 256):
            cols = pl.ds(n * 256, 256)
            high = jnp.maximum(acc[rows, cols], 0.0)
            act = jnp.log1p(high)
            square = act * act
            totals[side, pl.ds(k, 1), cols] = jnp.sum(
                square * square * weight, axis=0, keepdims=True
            )
            acc[rows, cols] = weight * (square * act) / (1.0 + high)

    @pl.loop(0, G)
    def _(k):
        pool(0, LP, mp_ref, k, 0)
        pool(PR, LQ, mq_ref, k, 1)

    def fourth_root(t):
        return jnp.sqrt(jnp.sqrt(t))

    allp[r] = (fourth_root(totals[0] + 1.0) - 1.0).astype(BF)
    allq[r] = (fourth_root(totals[1] + 1.0) - 1.0).astype(BF)

    def spread(ref):
        copies = [send(ref.at[r], device(z, yl, yhs[e], xs[d], c)) for d, e in RELATIVE]
        copies.append(send(ref.at[r], cdev))
        return copies

    def hand_on(ref, copies):
        handed = []
        for (d, e), copy in zip(RELATIVE, copies):
            copy.wait_recv()
            came = (yhs[e] * 4 + xs[(4 - d) % 4]) * 2 + c
            handed.append(send(ref.at[came], cdev))
        return handed

    spread_p = spread(allp)
    spread_q = spread(allq)
    handed_p = hand_on(allp, spread_p)
    spread_p[7].wait_recv()
    for copy in handed_p:
        copy.wait_recv()

    every_pass = allp[...].reshape(ROWS * PAD, W)
    sbuf[v] = lax.dot_general(
        allq[r], every_pass, (((1,), (1,)), ((), ())), preferred_element_type=F32
    )
    shared = [send(sbuf.at[v], device(zs[d], yls[e], yh, x, c)) for d, e in RELATIVE]
    handed_q = hand_on(allq, spread_q)
    row_at = lax.broadcasted_iota(jnp.int32, (PAD, ROWS * PAD), 0)
    col_at = lax.broadcasted_iota(jnp.int32, (PAD, ROWS * PAD), 1)
    passage = (col_at // PAD) * G + col_at % PAD
    real = (col_at % PAD < G) & (row_at < G)
    label = jnp.full((PAD, ROWS * PAD), -1, jnp.int32)
    for q in range(G):
        label = jnp.where(row_at == q, lab_ref[q], label)
    chosen = (label == passage) & real
    for copy in shared:
        copy.wait_recv()
    scores = sbuf[0]
    for k in range(1, VOCAB):
        scores = scores + sbuf[k]
    scores = scores * SCALING
    onehot = jnp.where(chosen, 1.0, 0.0)
    positive = jnp.sum(scores * onehot, axis=1, keepdims=True)
    weights = jnp.where(
        real & jnp.logical_not(chosen), jax.nn.sigmoid(MARGIN + scores - positive), 0.0
    )
    score_grad = (
        (weights - onehot * jnp.sum(weights, axis=1, keepdims=True)) * SCALING
    ).astype(BF)
    gbuf[r] = score_grad
    group = [send(gbuf.at[r], device(z, yl, yhs[e], xs[d], cs[f])) for d, e in RELATIVE for f in (0, 1)]
    group.append(send(gbuf.at[r], cdev))

    def tail(t):
        root = jnp.sqrt(t)
        return 1.0 / (root * jnp.sqrt(root))

    query_grad = jnp.dot(score_grad, every_pass, preferred_element_type=F32)
    factor[1] = query_grad * tail(totals[1] + 1.0)

    @pl.loop(0, G // 2)
    def _(k):
        rows = pl.ds(pl.multiple_of(PR + k * 2 * LQ, 2 * LQ), 2 * LQ)
        upper = lax.broadcasted_iota(jnp.int32, (2 * LQ, W), 0) < LQ
        gain = jnp.where(
            upper,
            jnp.broadcast_to(factor[1, pl.ds(2 * k, 1), :], (2 * LQ, W)),
            jnp.broadcast_to(factor[1, pl.ds(2 * k + 1, 1), :], (2 * LQ, W)),
        )
        slopes[rows, :] = (acc[rows, :] * gain).astype(BF)

    spread_q[7].wait_recv()
    for copy in handed_q:
        copy.wait_recv()
    for copy in group:
        copy.wait_recv()
    pick = jnp.where(
        lax.broadcasted_iota(jnp.int32, (ROWS * PAD, PAD), 0)
        == r * PAD + lax.broadcasted_iota(jnp.int32, (ROWS * PAD, PAD), 1),
        1.0,
        0.0,
    ).astype(BF)
    mine = jnp.dot(
        gbuf[...].reshape(ROWS * PAD, ROWS * PAD), pick, preferred_element_type=F32
    ).astype(BF)
    pass_grad = lax.dot_general(
        mine,
        allq[...].reshape(ROWS * PAD, W),
        (((0,), (0,)), ((), ())),
        preferred_element_type=F32,
    )
    factor[0] = pass_grad * tail(totals[0] + 1.0)

    @pl.loop(0, G)
    def _(k):
        rows = pl.ds(pl.multiple_of(k * LP, LP), LP)
        slopes[rows, :] = (acc[rows, :] * factor[0, pl.ds(k, 1), :]).astype(BF)

    for copy in tok_sent:
        copy.wait_send()

    def mm2(dz, dy):
        slot = zs[dz] * 2 + yls[dy]

        @pl.loop(0, F // 256)
        def _(n):
            cols = pl.ds(pl.multiple_of(n * 256, 256), 256)
            tok[slot, :, cols] = lax.dot_general(
                slopes[...],
                head[slot, cols, :],
                (((1,), (1,)), ((), ())),
                preferred_element_type=F32,
            ).astype(BF)

    def add_into(slot, h, other):
        @pl.loop(0, RH // 48)
        def _(k):
            rows = pl.ds(pl.multiple_of(h * RH + k * 48, 16), 48)
            some = pl.ds(pl.multiple_of(k * 48, 16), 48)
            tok[slot, rows, :] = (
                tok[slot, rows, :].astype(F32) + other[some, :].astype(F32)
            ).astype(BF)

    def out(src, dst, dev):
        copy = remote(src, dst, dev)
        sent.append(copy)
        return copy

    arrivals = {}
    for dy in (1, 0):
        mm2(2, dy)
        up = out(hid(2, dy, 0), rhalf.at[dy, 0], zdev[1])
        down = out(hid(2, dy, 1), rhalf.at[dy, 1], zdev[3])
        mm2(1, dy)
        arrivals[(dy, 0, 1)] = out(hid(1, dy, 1), rfull.at[dy, 0, pl.ds(RH, RH)], zdev[1])
        mm2(3, dy)
        arrivals[(dy, 1, 0)] = out(hid(3, dy, 0), rfull.at[dy, 1, pl.ds(0, RH)], zdev[3])
        up.wait_recv()
        add_into(zs[1] * 2 + yls[dy], 0, rhalf.at[dy, 0])
        arrivals[(dy, 0, 0)] = out(hid(1, dy, 0), rfull.at[dy, 0, pl.ds(0, RH)], zdev[1])
        down.wait_recv()
        add_into(zs[3] * 2 + yls[dy], 1, rhalf.at[dy, 1])
        arrivals[(dy, 1, 1)] = out(hid(3, dy, 1), rfull.at[dy, 1, pl.ds(RH, RH)], zdev[3])
    mm2(0, 1)
    mm2(0, 0)

    slot = z * 2 + (1 - yl)
    across = []
    for h in (0, 1):
        arrivals[(1, 0, h)].wait_recv()
        arrivals[(1, 1, h)].wait_recv()

        @pl.loop(0, RH // 48)
        def _(k):
            rows = pl.ds(pl.multiple_of(h * RH + k * 48, 16), 48)
            tok[slot, rows, :] = (
                tok[slot, rows, :].astype(F32)
                + rfull[1, 0, rows, :].astype(F32)
                + rfull[1, 1, rows, :].astype(F32)
            ).astype(BF)

        across.append(out(hid(0, 1, h), ybuf.at[pl.ds(h * RH, RH)], yldev))
    for copy in across:
        copy.wait_recv()
    for key in [(0, 0, 0), (0, 0, 1), (0, 1, 0), (0, 1, 1)]:
        arrivals[key].wait_recv()

    def total(rows):
        return (
            tok[v, rows, :].astype(F32)
            + rfull[0, 0, rows, :].astype(F32)
            + rfull[0, 1, rows, :].astype(F32)
            + ybuf[rows, :].astype(F32)
        ).astype(BF)

    @pl.loop(0, PR // 48)
    def _(k):
        rows = pl.ds(pl.multiple_of(k * 48, 16), 48)
        gp_ref[rows, :] = total(rows)

    for k in range(QR // 48):
        gq_ref[pl.ds(k * 48, 48), :] = total(pl.ds(PR + k * 48, 48))

    for copy in sent:
        copy.wait_send()


COPIES = 150


def shards(hidden_pass, hidden_query, mask_pass, mask_query, labels, head_weight):
    anywhere = pl.BlockSpec(memory_space=pl.ANY)
    vmem = pl.BlockSpec(memory_space=pltpu.VMEM)
    smem = pl.BlockSpec(memory_space=pltpu.SMEM)
    grad_pass, grad_query = pl.pallas_call(
        kernel,
        out_shape=(
            jax.ShapeDtypeStruct((PR, F), BF),
            jax.ShapeDtypeStruct((QR, F), BF),
        ),
        in_specs=[anywhere, anywhere, vmem, vmem, smem, anywhere],
        out_specs=(vmem, vmem),
        scratch_shapes=[
            pltpu.VMEM((VOCAB, R, F), BF),
            pltpu.VMEM((VOCAB, 2 * HD, W), BF),
            pltpu.VMEM((R, W), F32),
            pltpu.VMEM((R, W), BF),
            pltpu.VMEM((2, PAD, W), F32),
            pltpu.VMEM((2, PAD, W), F32),
            pltpu.VMEM((ROWS, PAD, W), BF),
            pltpu.VMEM((ROWS, PAD, W), BF),
            pltpu.VMEM((VOCAB, PAD, ROWS * PAD), F32),
            pltpu.VMEM((ROWS, PAD, ROWS * PAD), BF),
            pltpu.VMEM((2, 2, RH, F), BF),
            pltpu.VMEM((2, 2, R, F), BF),
            pltpu.VMEM((R, F), BF),
            pltpu.SemaphoreType.DMA((3,)),
            pltpu.SemaphoreType.DMA((COPIES,)),
            pltpu.SemaphoreType.DMA((COPIES,)),
        ],
        compiler_params=pltpu.CompilerParams(
            collective_id=0, has_side_effects=True, vmem_limit_bytes=60 * 1024 * 1024
        ),
        name="step",
    )(
        hidden_pass.reshape(PR, F),
        hidden_query.reshape(QR, F),
        mask_pass,
        mask_query,
        labels,
        head_weight,
    )
    return (
        grad_pass.reshape(G, LP, F),
        grad_query.reshape(G, LQ, F),
    )


def solution(mesh):
    return jax.shard_map(
        shards,
        mesh=mesh,
        in_specs=(
            P("rows", None, "vocab"),
            P("rows", None, "vocab"),
            P("rows", None),
            P("rows", None),
            P("rows"),
            P("rows", "vocab"),
        ),
        out_specs=(P("rows", None, "vocab"), P("rows", None, "vocab")),
        check_vma=False,
    )
```

```python
import jax
import jax.numpy as jnp
from jax import lax
from jax.experimental import pallas as pl
from jax.experimental.pallas import tpu as pltpu
from jax.sharding import PartitionSpec as P

MESH = pl.DeviceIdType.MESH
MARGIN = 1.0
SHARPNESS = 16.0
V = 16384
SCALING = SHARPNESS * V ** (-0.5)

G = 12
LP = 64
LQ = 8
PR = G * LP
QR = G * LQ
R = PR + QR
RH = R // 2
ZR = 480
ZH = ((0, 240), (240, 240))
YR = R - ZR
YH = ((480, 192), (672, 192))
F = 512
W = 2048
HD = 256
HH = HD // 2
HY = 96
HX = HD - 2 * HY
PAD = 16
ROWS = 16
VOCAB = 8
BF = jnp.bfloat16
F32 = jnp.float32

RELATIVE = [(1, 0), (3, 0), (2, 0), (0, 1), (1, 1), (3, 1), (2, 1)]


def where_am_i():
    v = lax.axis_index("vocab")
    r = lax.axis_index("rows")
    return v // 2, v % 2, r // 8, (r // 2) % 4, r % 2


def device(z, yl, yh, x, c):
    return (z * 2 + yl, (yh * 4 + x) * 2 + c)


def kernel(
    hp_ref,
    hq_ref,
    mp_ref,
    mq_ref,
    lab_ref,
    hw_ref,
    gp_ref,
    gq_ref,
    tok,
    head,
    acc,
    slopes,
    totals,
    factor,
    allp,
    allq,
    sbuf,
    gbuf,
    rhalf,
    rfull,
    ybuf,
    yb,
    lsem,
    ssem,
    rsem,
):
    z, yl, yh, x, c = where_am_i()
    v = z * 2 + yl
    r = (yh * 4 + x) * 2 + c
    zs = [z, (z + 1) % 4, (z + 2) % 4, (z + 3) % 4]
    xs = [x, (x + 1) % 4, (x + 2) % 4, (x + 3) % 4]
    yls = [yl, 1 - yl]
    yhs = [yh, 1 - yh]
    cs = [c, 1 - c]
    zdev = [device(k, yl, yh, x, c) for k in zs]
    xdev = [device(z, yl, yh, k, c) for k in xs]
    yldev = device(z, 1 - yl, yh, x, c)
    yhdev = device(z, yl, 1 - yh, x, c)
    cdev = device(z, yl, yh, x, 1 - c)

    own_head = yh * 4 + x
    local = [
        pltpu.make_async_copy(hp_ref, tok.at[v, pl.ds(0, PR)], lsem.at[0]),
        pltpu.make_async_copy(hq_ref, tok.at[v, pl.ds(PR, QR)], lsem.at[1]),
        pltpu.make_async_copy(hw_ref, head.at[own_head, pl.ds(c * HD, HD)], lsem.at[2]),
    ]
    for copy in local:
        copy.start()

    acc[...] = jnp.zeros_like(acc)
    totals[...] = jnp.zeros_like(totals)
    peers = [zdev[1], zdev[3], yldev, xdev[1], xdev[3], yhdev, cdev]
    barrier = pltpu.get_barrier_semaphore()
    for peer in peers:
        pl.semaphore_signal(barrier, inc=1, device_id=peer, device_id_type=MESH)
    pl.semaphore_wait(barrier, len(peers))
    for copy in local:
        copy.wait()

    counter = [0]
    sent = []

    def remote(src, dst, dev):
        k = counter[0]
        counter[0] += 1
        copy = pltpu.make_async_remote_copy(
            src_ref=src,
            dst_ref=dst,
            send_sem=ssem.at[k],
            recv_sem=rsem.at[k],
            device_id=dev,
            device_id_type=MESH,
        )
        copy.start()
        return copy

    def send(ref, dev):
        copy = remote(ref, ref, dev)
        sent.append(copy)
        return copy

    def hid(dz, dy, h):
        return tok.at[zs[dz] * 2 + yls[dy], pl.ds(h * RH, RH)]

    def hed(dx, dy, lo, n):
        return head.at[yhs[dy] * 4 + xs[dx], pl.ds(c * HD + lo, n)]

    halves = ((0, HH), (HH, HH))
    ring = ((0, HY), (HY, HY))
    rest = (2 * HY, HX)
    a, b, s = {}, {}, {}
    tok_sent = []

    def a_send(key, ref, dev):
        copy = remote(ref, ref, dev)
        a[key] = copy
        tok_sent.append(copy)

    def b_send(key, dx, dy, part, dev):
        b[key] = send(hed(dx, dy, *part), dev)

    def to_core(dx, dy, part):
        s.setdefault((dx, dy), []).append(send(hed(dx, dy, *part), cdev))

    def b_took(key, dx, dy, part):
        b[key].wait_recv()
        to_core(dx, dy, part)

    a_send(("y", 0), hid(0, 0, 0), yldev)
    a_send(("+", 0), hid(0, 0, 0), zdev[1])
    a_send(("-", 1), hid(0, 0, 1), zdev[3])
    b_send(("+", 0), 0, 0, halves[0], xdev[1])
    b_send(("-", 1), 0, 0, halves[1], xdev[3])
    a_send(("y", 1), hid(0, 0, 1), yldev)
    b_send(("y", 0), 0, 0, ring[0], yhdev)
    b_send(("y", 1), 0, 0, ring[1], yhdev)
    a_send(("+", 1), hid(0, 0, 1), zdev[1])
    a_send(("-", 0), hid(0, 0, 0), zdev[3])
    b_send(("+", 1), 0, 0, halves[1], xdev[1])
    b_send(("-", 0), 0, 0, halves[0], xdev[3])
    b_send(("r", 0), 0, 0, rest, yhdev)
    to_core(0, 0, halves[0])
    to_core(0, 0, halves[1])

    a[("+", 0)].wait_recv()
    a_send("f+", hid(3, 0, 0), zdev[1])
    a[("-", 1)].wait_recv()
    a_send("f-", hid(1, 0, 1), zdev[3])
    b_took(("+", 0), 3, 0, halves[0])
    b_send("f+", 3, 0, halves[0], xdev[1])
    b_took(("-", 1), 1, 0, halves[1])
    b_send("f-", 1, 0, halves[1], xdev[3])
    b_send(("r", 1), 1, 0, rest, yhdev)

    a[("y", 0)].wait_recv()
    a_send(("o+", 0), hid(0, 1, 0), zdev[1])
    b_took(("+", 1), 3, 0, halves[1])
    b_send(("r", 3), 3, 0, rest, yhdev)
    b_took(("-", 0), 1, 0, halves[0])
    a[("y", 1)].wait_recv()
    a_send(("o-", 1), hid(0, 1, 1), zdev[3])
    a_send(("o-", 0), hid(0, 1, 0), zdev[3])
    a_send(("o+", 1), hid(0, 1, 1), zdev[1])
    b_took(("y", 0), 0, 1, ring[0])
    b_send(("o+", 0), 0, 1, ring[0], xdev[1])
    b_took(("y", 1), 0, 1, ring[1])
    b_send(("o-", 1), 0, 1, ring[1], xdev[3])
    b_send(("o-", 0), 0, 1, ring[0], xdev[3])
    b_send(("o+", 1), 0, 1, ring[1], xdev[1])
    b_took("f+", 2, 0, halves[0])
    b_took("f-", 2, 0, halves[1])
    b_send(("r", 2), 2, 0, rest, yhdev)

    def core_took(dx, dy):
        for copy in s[(dx, dy)]:
            copy.wait_recv()

    def mm1(ready):
        @pl.loop(0, VOCAB)
        def _(slot):
            @pl.when(ready(slot))
            def _():
                @pl.loop(0, 2)
                def _(n):
                    cols = pl.ds(pl.multiple_of(n * (W // 2), W // 2), W // 2)
                    acc[:, cols] += jnp.dot(
                        tok[slot], head[slot, :, cols], preferred_element_type=F32
                    )

    def near_head(slot):
        return slot // 4 == yh

    def near_hidden(slot):
        return slot % 2 == yl

    def far(slot):
        return (jnp.logical_not(near_head(slot)) & (slot % 4 == xs[2])) | (
            jnp.logical_not(near_hidden(slot)) & (slot // 2 == zs[2])
        )

    for key in [("+", 1), ("-", 0), "f+", "f-"]:
        a[key].wait_recv()
    for dx in range(4):
        core_took(dx, 0)
    mm1(lambda slot: near_head(slot) & near_hidden(slot))
    a[("o+", 0)].wait_recv()
    a_send("g+", hid(3, 1, 0), zdev[1])
    a[("o-", 1)].wait_recv()
    a_send("g-", hid(1, 1, 1), zdev[3])
    b_took(("o+", 0), 3, 1, ring[0])
    b_send("g+", 3, 1, ring[0], xdev[1])
    b_took(("o-", 1), 1, 1, ring[1])
    b_send("g-", 1, 1, ring[1], xdev[3])
    a[("o+", 1)].wait_recv()
    a[("o-", 0)].wait_recv()
    b_took(("r", 0), 0, 1, rest)
    mm1(
        lambda slot: near_head(slot)
        & jnp.logical_not(near_hidden(slot))
        & jnp.logical_not(far(slot))
    )
    b_took(("o+", 1), 3, 1, ring[1])
    b_took(("o-", 0), 1, 1, ring[0])
    b_took(("r", 1), 1, 1, rest)
    b_took(("r", 3), 3, 1, rest)
    for dx in (0, 1, 3):
        core_took(dx, 1)
    mm1(lambda slot: jnp.logical_not(near_head(slot)) & jnp.logical_not(far(slot)))
    b_took(("r", 2), 2, 1, rest)
    b_took("g+", 2, 1, ring[0])
    b_took("g-", 2, 1, ring[1])
    a["g+"].wait_recv()
    a["g-"].wait_recv()
    core_took(2, 1)
    mm1(far)

    def pool(base, length, weight, k, side, first):
        rows = pl.ds(pl.multiple_of(base + k * length, 8), length)
        for n in range(first, first + W // 2, 256):
            cols = pl.ds(n, 256)
            high = jnp.maximum(acc[rows, cols], 0.0)
            act = jnp.log1p(high)
            square = act * act
            totals[side, pl.ds(k, 1), cols] = jnp.sum(
                square * square * weight, axis=0, keepdims=True
            )
            acc[rows, cols] = weight * (square * act) / (1.0 + high)

    def line_weight(k):
        line = mp_ref[pl.ds(k, 1), :].astype(F32)
        shape = (LP, LP)
        eye = lax.broadcasted_iota(jnp.int32, shape, 0) == lax.broadcasted_iota(jnp.int32, shape, 1)
        return jnp.sum(jnp.where(eye, jnp.broadcast_to(line, shape), 0.0), axis=1, keepdims=True)

    def query_weight(k):
        shape = (LQ, G)
        here = lax.broadcasted_iota(jnp.int32, shape, 1) == k
        return jnp.sum(jnp.where(here, mq_ref[...].astype(F32), 0.0), axis=1, keepdims=True)

    def fourth_root(t):
        return jnp.sqrt(jnp.sqrt(t))

    def spread(ref, cols):
        mine = ref.at[r, :, cols]
        copies = [send(mine, device(z, yl, yhs[e], xs[d], c)) for d, e in RELATIVE]
        copies.append(send(mine, cdev))
        return copies

    def hand_on(ref, cols, copies):
        handed = []
        for (d, e), copy in zip(RELATIVE, copies):
            copy.wait_recv()
            came = (yhs[e] * 4 + xs[(4 - d) % 4]) * 2 + c
            handed.append(send(ref.at[came, :, cols], cdev))
        return handed

    spread_p = []
    for first in (0, W // 2):
        cols = pl.ds(first, W // 2)

        @pl.loop(0, G)
        def _(k):
            pool(0, LP, line_weight(k), k, 0, first)

        allp[r, :, cols] = (fourth_root(totals[0, :, cols] + 1.0) - 1.0).astype(BF)
        spread_p.append((cols, spread(allp, cols)))

    @pl.loop(0, G)
    def _(k):
        pool(PR, LQ, query_weight(k), k, 1, 0)
        pool(PR, LQ, query_weight(k), k, 1, W // 2)

    whole = pl.ds(0, W)
    allq[r] = (fourth_root(totals[1] + 1.0) - 1.0).astype(BF)
    handed_p = []
    for cols, copies in spread_p:
        handed_p += hand_on(allp, cols, copies)
        handed_p.append(copies[7])
    spread_q = spread(allq, whole)
    for copy in handed_p:
        copy.wait_recv()

    every_pass = allp[...].reshape(ROWS * PAD, W)
    sbuf[v] = lax.dot_general(
        allq[r], every_pass, (((1,), (1,)), ((), ())), preferred_element_type=F32
    )
    shared = [send(sbuf.at[v], device(zs[d], yls[e], yh, x, c)) for d, e in RELATIVE]
    row_at = lax.broadcasted_iota(jnp.int32, (PAD, ROWS * PAD), 0)
    col_at = lax.broadcasted_iota(jnp.int32, (PAD, ROWS * PAD), 1)
    passage = (col_at // PAD) * G + col_at % PAD
    real = (col_at % PAD < G) & (row_at < G)
    label = jnp.full((PAD, ROWS * PAD), -1, jnp.int32)
    for q in range(G):
        label = jnp.where(row_at == q, lab_ref[q], label)
    chosen = (label == passage) & real
    for copy in shared:
        copy.wait_recv()
    scores = sbuf[0]
    for k in range(1, VOCAB):
        scores = scores + sbuf[k]
    scores = scores * SCALING
    onehot = jnp.where(chosen, 1.0, 0.0)
    positive = jnp.sum(scores * onehot, axis=1, keepdims=True)
    weights = jnp.where(
        real & jnp.logical_not(chosen), jax.nn.sigmoid(MARGIN + scores - positive), 0.0
    )
    score_grad = (
        (weights - onehot * jnp.sum(weights, axis=1, keepdims=True)) * SCALING
    ).astype(BF)
    gbuf[r] = score_grad
    group = [send(gbuf.at[r], device(z, yl, yhs[e], xs[d], cs[f])) for d, e in RELATIVE for f in (0, 1)]
    group.append(send(gbuf.at[r], cdev))

    def tail(t):
        root = jnp.sqrt(t)
        return 1.0 / (root * jnp.sqrt(root))

    query_grad = jnp.dot(score_grad, every_pass, preferred_element_type=F32)
    factor[1] = query_grad * tail(totals[1] + 1.0)

    @pl.loop(0, G // 2)
    def _(k):
        rows = pl.ds(pl.multiple_of(PR + k * 2 * LQ, 2 * LQ), 2 * LQ)
        upper = lax.broadcasted_iota(jnp.int32, (2 * LQ, W), 0) < LQ
        gain = jnp.where(
            upper,
            jnp.broadcast_to(factor[1, pl.ds(2 * k, 1), :], (2 * LQ, W)),
            jnp.broadcast_to(factor[1, pl.ds(2 * k + 1, 1), :], (2 * LQ, W)),
        )
        slopes[rows, :] = (acc[rows, :] * gain).astype(BF)

    handed_q = hand_on(allq, whole, spread_q)
    spread_q[7].wait_recv()
    for copy in handed_q:
        copy.wait_recv()
    for copy in group:
        copy.wait_recv()
    pick = jnp.where(
        lax.broadcasted_iota(jnp.int32, (ROWS * PAD, PAD), 0)
        == r * PAD + lax.broadcasted_iota(jnp.int32, (ROWS * PAD, PAD), 1),
        1.0,
        0.0,
    ).astype(BF)
    mine = jnp.dot(
        gbuf[...].reshape(ROWS * PAD, ROWS * PAD), pick, preferred_element_type=F32
    ).astype(BF)
    pass_grad = lax.dot_general(
        mine,
        allq[...].reshape(ROWS * PAD, W),
        (((0,), (0,)), ((), ())),
        preferred_element_type=F32,
    )
    factor[0] = pass_grad * tail(totals[0] + 1.0)

    @pl.loop(0, G)
    def _(k):
        rows = pl.ds(pl.multiple_of(k * LP, LP), LP)
        slopes[rows, :] = (acc[rows, :] * factor[0, pl.ds(k, 1), :]).astype(BF)

    for copy in tok_sent:
        copy.wait_send()

    def part(dz, dy, lo, n):
        return tok.at[zs[dz] * 2 + yls[dy], pl.ds(lo, n)]

    def mm2(dz, dy):
        slot = zs[dz] * 2 + yls[dy]

        @pl.loop(0, F // 256)
        def _(n):
            cols = pl.ds(pl.multiple_of(n * 256, 256), 256)
            tok[slot, :, cols] = lax.dot_general(
                slopes[...],
                head[slot, cols, :],
                (((1,), (1,)), ((), ())),
                preferred_element_type=F32,
            ).astype(BF)

    def add_into(dz, dy, lo, size, *others):
        slot = zs[dz] * 2 + yls[dy]

        @pl.loop(0, size // 48)
        def _(k):
            rows = pl.ds(pl.multiple_of(lo + k * 48, 16), 48)
            total = tok[slot, rows, :].astype(F32)
            for other in others:
                total = total + other[rows, :].astype(F32)
            tok[slot, rows, :] = total.astype(BF)

    def out(src, dst, dev):
        copy = remote(src, dst, dev)
        sent.append(copy)
        return copy

    def to_ring(dz, dy, lo, n, ref):
        dev = zdev[1] if ref == 0 else zdev[3]
        return out(part(dz, dy, lo, n), rfull.at[dy, ref, pl.ds(lo, n)], dev)

    def to_half(dy, lo, n, ref):
        dev = zdev[1] if ref == 0 else zdev[3]
        return out(part(2, dy, lo, n), rhalf.at[dy, ref, pl.ds(lo, n)], dev)

    def to_pair(dz):
        return out(part(dz, 1, ZR, YR), yb.at[dz], yldev)

    mm2(2, 1)
    up = to_half(1, *ZH[0], 0)
    down = to_half(1, *ZH[1], 1)
    pair = {2: to_pair(2)}
    mm2(1, 1)
    other_plane = [to_ring(1, 1, *ZH[1], 0)]
    pair[1] = to_pair(1)
    mm2(3, 1)
    other_plane.append(to_ring(3, 1, *ZH[0], 1))
    pair[3] = to_pair(3)
    up.wait_recv()
    add_into(1, 1, *ZH[0], rhalf.at[1, 0])
    other_plane.append(to_ring(1, 1, *ZH[0], 0))
    down.wait_recv()
    add_into(3, 1, *ZH[1], rhalf.at[1, 1])
    other_plane.append(to_ring(3, 1, *ZH[1], 1))
    mm2(0, 1)
    last = [out(part(0, 1, ZR, YR), ybuf.at[pl.ds(ZR, YR)], yldev)]

    def add_pair(dz):
        slot = zs[dz] * 2 + yl
        pair[dz].wait_recv()

        @pl.loop(0, YR // 48)
        def _(k):
            rows = pl.ds(pl.multiple_of(ZR + k * 48, 16), 48)
            some = pl.ds(pl.multiple_of(k * 48, 16), 48)
            tok[slot, rows, :] = (
                tok[slot, rows, :].astype(F32) + yb[dz, some, :].astype(F32)
            ).astype(BF)

    mm2(2, 0)
    up = to_half(0, *ZH[0], 0)
    down = to_half(0, *ZH[1], 1)
    add_pair(2)
    up_y = to_half(0, *YH[0], 0)
    down_y = to_half(0, *YH[1], 1)
    mm2(1, 0)
    last.append(to_ring(1, 0, *ZH[1], 0))
    mm2(3, 0)
    last.append(to_ring(3, 0, *ZH[0], 1))
    for copy in other_plane:
        copy.wait_recv()
    add_into(0, 1, 0, ZR, rfull.at[1, 0], rfull.at[1, 1])
    last.append(out(part(0, 1, 0, ZR), ybuf.at[pl.ds(0, ZR)], yldev))
    up.wait_recv()
    add_into(1, 0, *ZH[0], rhalf.at[0, 0])
    last.append(to_ring(1, 0, *ZH[0], 0))
    down.wait_recv()
    add_into(3, 0, *ZH[1], rhalf.at[0, 1])
    last.append(to_ring(3, 0, *ZH[1], 1))
    add_pair(1)
    last.append(to_ring(1, 0, *YH[1], 0))
    add_pair(3)
    last.append(to_ring(3, 0, *YH[0], 1))
    mm2(0, 0)
    up_y.wait_recv()
    add_into(1, 0, *YH[0], rhalf.at[0, 0])
    last.append(to_ring(1, 0, *YH[0], 0))
    down_y.wait_recv()
    add_into(3, 0, *YH[1], rhalf.at[0, 1])
    last.append(to_ring(3, 0, *YH[1], 1))
    for copy in last:
        copy.wait_recv()

    def total(rows):
        return (
            tok[v, rows, :].astype(F32)
            + rfull[0, 0, rows, :].astype(F32)
            + rfull[0, 1, rows, :].astype(F32)
            + ybuf[rows, :].astype(F32)
        ).astype(BF)

    @pl.loop(0, PR // 48)
    def _(k):
        rows = pl.ds(pl.multiple_of(k * 48, 16), 48)
        gp_ref[rows, :] = total(rows)

    for k in range(QR // 48):
        gq_ref[pl.ds(k * 48, 48), :] = total(pl.ds(PR + k * 48, 48))

    for copy in sent:
        copy.wait_send()


COPIES = 192


def shards(hidden_pass, hidden_query, mask_pass, mask_query, labels, head_weight):
    anywhere = pl.BlockSpec(memory_space=pl.ANY)
    vmem = pl.BlockSpec(memory_space=pltpu.VMEM)
    smem = pl.BlockSpec(memory_space=pltpu.SMEM)
    grad_pass, grad_query = pl.pallas_call(
        kernel,
        out_shape=(
            jax.ShapeDtypeStruct((PR, F), BF),
            jax.ShapeDtypeStruct((QR, F), BF),
        ),
        in_specs=[anywhere, anywhere, vmem, vmem, smem, anywhere],
        out_specs=(vmem, vmem),
        scratch_shapes=[
            pltpu.VMEM((VOCAB, R, F), BF),
            pltpu.VMEM((VOCAB, 2 * HD, W), BF),
            pltpu.VMEM((R, W), F32),
            pltpu.VMEM((R, W), BF),
            pltpu.VMEM((2, PAD, W), F32),
            pltpu.VMEM((2, PAD, W), F32),
            pltpu.VMEM((ROWS, PAD, W), BF),
            pltpu.VMEM((ROWS, PAD, W), BF),
            pltpu.VMEM((VOCAB, PAD, ROWS * PAD), F32),
            pltpu.VMEM((ROWS, PAD, ROWS * PAD), BF),
            pltpu.VMEM((2, 2, R, F), BF),
            pltpu.VMEM((2, 2, R, F), BF),
            pltpu.VMEM((R, F), BF),
            pltpu.VMEM((4, YR, F), BF),
            pltpu.SemaphoreType.DMA((3,)),
            pltpu.SemaphoreType.DMA((COPIES,)),
            pltpu.SemaphoreType.DMA((COPIES,)),
        ],
        compiler_params=pltpu.CompilerParams(
            collective_id=0, has_side_effects=True, vmem_limit_bytes=60 * 1024 * 1024
        ),
        name="step",
    )(
        hidden_pass.reshape(PR, F),
        hidden_query.reshape(QR, F),
        mask_pass,
        mask_query.T,
        labels,
        head_weight,
    )
    return (
        grad_pass.reshape(G, LP, F),
        grad_query.reshape(G, LQ, F),
    )


def solution(mesh):
    return jax.shard_map(
        shards,
        mesh=mesh,
        in_specs=(
            P("rows", None, "vocab"),
            P("rows", None, "vocab"),
            P("rows", None),
            P("rows", None),
            P("rows"),
            P("rows", "vocab"),
        ),
        out_specs=(P("rows", None, "vocab"), P("rows", None, "vocab")),
        check_vma=False,
    )
```

```python
import jax
import jax.numpy as jnp
from jax import lax
from jax.experimental import pallas as pl
from jax.experimental.pallas import tpu as pltpu
from jax.sharding import PartitionSpec as P

MESH = pl.DeviceIdType.MESH
MARGIN = 1.0
SHARPNESS = 16.0
V = 16384
SCALING = SHARPNESS * V ** (-0.5)

G = 12
LP = 64
LQ = 8
PR = G * LP
QR = G * LQ
R = PR + QR
RH = R // 2
ZR = 480
ZH = ((0, 240), (240, 240))
YR = R - ZR
YH = ((480, 192), (672, 192))
F = 512
W = 2048
HD = 256
HH = HD // 2
HY = 96
HX = HD - 2 * HY
PAD = 16
ROWS = 16
VOCAB = 8
BF = jnp.bfloat16
F32 = jnp.float32

RELATIVE = [(1, 0), (3, 0), (2, 0), (0, 1), (1, 1), (3, 1), (2, 1)]


def where_am_i():
    v = lax.axis_index("vocab")
    r = lax.axis_index("rows")
    return v // 2, v % 2, r // 8, (r // 2) % 4, r % 2


def device(z, yl, yh, x, c):
    return (z * 2 + yl, (yh * 4 + x) * 2 + c)


def kernel(
    hp_ref,
    hq_ref,
    mp_ref,
    mq_ref,
    lab_ref,
    hw_ref,
    gp_ref,
    gq_ref,
    tok,
    head,
    acc,
    slopes,
    totals,
    factor,
    allp,
    allq,
    sbuf,
    gbuf,
    rhalf,
    rfull,
    ybuf,
    yb,
    lsem,
    ssem,
    rsem,
):
    z, yl, yh, x, c = where_am_i()
    v = z * 2 + yl
    r = (yh * 4 + x) * 2 + c
    zs = [z, (z + 1) % 4, (z + 2) % 4, (z + 3) % 4]
    xs = [x, (x + 1) % 4, (x + 2) % 4, (x + 3) % 4]
    yls = [yl, 1 - yl]
    yhs = [yh, 1 - yh]
    cs = [c, 1 - c]
    zdev = [device(k, yl, yh, x, c) for k in zs]
    xdev = [device(z, yl, yh, k, c) for k in xs]
    yldev = device(z, 1 - yl, yh, x, c)
    yhdev = device(z, yl, 1 - yh, x, c)
    cdev = device(z, yl, yh, x, 1 - c)

    own_head = yh * 4 + x
    local = [
        pltpu.make_async_copy(hp_ref, tok.at[v, pl.ds(0, PR)], lsem.at[0]),
        pltpu.make_async_copy(hq_ref, tok.at[v, pl.ds(PR, QR)], lsem.at[1]),
        pltpu.make_async_copy(hw_ref, head.at[own_head, pl.ds(c * HD, HD)], lsem.at[2]),
    ]
    for copy in local:
        copy.start()

    acc[...] = jnp.zeros_like(acc)
    totals[...] = jnp.zeros_like(totals)
    peers = [zdev[1], zdev[3], yldev, xdev[1], xdev[3], yhdev, cdev]
    barrier = pltpu.get_barrier_semaphore()
    for peer in peers:
        pl.semaphore_signal(barrier, inc=1, device_id=peer, device_id_type=MESH)
    pl.semaphore_wait(barrier, len(peers))
    for copy in local:
        copy.wait()

    counter = [0]
    sent = []

    def remote(src, dst, dev):
        k = counter[0]
        counter[0] += 1
        copy = pltpu.make_async_remote_copy(
            src_ref=src,
            dst_ref=dst,
            send_sem=ssem.at[k],
            recv_sem=rsem.at[k],
            device_id=dev,
            device_id_type=MESH,
        )
        copy.start()
        return copy

    def send(ref, dev):
        copy = remote(ref, ref, dev)
        sent.append(copy)
        return copy

    def hid(dz, dy, h):
        return tok.at[zs[dz] * 2 + yls[dy], pl.ds(h * RH, RH)]

    def hed(dx, dy, lo, n):
        return head.at[yhs[dy] * 4 + xs[dx], pl.ds(c * HD + lo, n)]

    halves = ((0, HH), (HH, HH))
    ring = ((0, HY), (HY, HY))
    rest = (2 * HY, HX)
    a, b, s = {}, {}, {}
    tok_sent = []

    def a_send(key, ref, dev):
        copy = remote(ref, ref, dev)
        a[key] = copy
        tok_sent.append(copy)

    def b_send(key, dx, dy, part, dev):
        b[key] = send(hed(dx, dy, *part), dev)

    def to_core(dx, dy, part):
        s.setdefault((dx, dy), []).append(send(hed(dx, dy, *part), cdev))

    def b_took(key, dx, dy, part):
        b[key].wait_recv()
        to_core(dx, dy, part)

    a_send(("y", 0), hid(0, 0, 0), yldev)
    a_send(("+", 0), hid(0, 0, 0), zdev[1])
    a_send(("-", 1), hid(0, 0, 1), zdev[3])
    b_send(("+", 0), 0, 0, halves[0], xdev[1])
    b_send(("-", 1), 0, 0, halves[1], xdev[3])
    a_send(("y", 1), hid(0, 0, 1), yldev)
    b_send(("y", 0), 0, 0, ring[0], yhdev)
    b_send(("y", 1), 0, 0, ring[1], yhdev)
    a_send(("+", 1), hid(0, 0, 1), zdev[1])
    a_send(("-", 0), hid(0, 0, 0), zdev[3])
    b_send(("+", 1), 0, 0, halves[1], xdev[1])
    b_send(("-", 0), 0, 0, halves[0], xdev[3])
    b_send(("r", 0), 0, 0, rest, yhdev)
    to_core(0, 0, halves[0])
    to_core(0, 0, halves[1])

    a[("+", 0)].wait_recv()
    a_send("f+", hid(3, 0, 0), zdev[1])
    a[("-", 1)].wait_recv()
    a_send("f-", hid(1, 0, 1), zdev[3])
    b[("+", 0)].wait_recv()
    b_send("f+", 3, 0, halves[0], xdev[1])
    b[("-", 1)].wait_recv()
    b_send("f-", 1, 0, halves[1], xdev[3])
    b_send(("r", 1), 1, 0, rest, yhdev)
    to_core(3, 0, halves[0])
    to_core(1, 0, halves[1])

    a[("y", 0)].wait_recv()
    a_send(("o+", 0), hid(0, 1, 0), zdev[1])
    b_took(("+", 1), 3, 0, halves[1])
    b_send(("r", 3), 3, 0, rest, yhdev)
    b_took(("-", 0), 1, 0, halves[0])
    a[("y", 1)].wait_recv()
    a_send(("o-", 1), hid(0, 1, 1), zdev[3])
    a_send(("o-", 0), hid(0, 1, 0), zdev[3])
    a_send(("o+", 1), hid(0, 1, 1), zdev[1])
    b[("y", 0)].wait_recv()
    b_send(("o+", 0), 0, 1, ring[0], xdev[1])
    b[("y", 1)].wait_recv()
    b_send(("o-", 1), 0, 1, ring[1], xdev[3])
    b_send(("o-", 0), 0, 1, ring[0], xdev[3])
    b_send(("o+", 1), 0, 1, ring[1], xdev[1])
    to_core(0, 1, ring[0])
    to_core(0, 1, ring[1])
    b_took("f+", 2, 0, halves[0])
    b_took("f-", 2, 0, halves[1])
    b_send(("r", 2), 2, 0, rest, yhdev)

    def core_took(dx, dy):
        for copy in s[(dx, dy)]:
            copy.wait_recv()

    def mm1(ready):
        @pl.loop(0, VOCAB)
        def _(slot):
            @pl.when(ready(slot))
            def _():
                @pl.loop(0, 2)
                def _(n):
                    cols = pl.ds(pl.multiple_of(n * (W // 2), W // 2), W // 2)
                    acc[:, cols] += jnp.dot(
                        tok[slot], head[slot, :, cols], preferred_element_type=F32
                    )

    def near_head(slot):
        return slot // 4 == yh

    def near_hidden(slot):
        return slot % 2 == yl

    def far_head(slot):
        return jnp.logical_not(near_head(slot)) & (slot % 4 == xs[2])

    def far_hidden(slot):
        return jnp.logical_not(near_hidden(slot)) & (slot // 2 == zs[2])

    def far(slot):
        return far_head(slot) | far_hidden(slot)

    for key in [("+", 1), ("-", 0), "f+", "f-"]:
        a[key].wait_recv()
    for dx in range(4):
        core_took(dx, 0)
    mm1(lambda slot: near_head(slot) & near_hidden(slot))
    a[("o+", 0)].wait_recv()
    a_send("g+", hid(3, 1, 0), zdev[1])
    a[("o-", 1)].wait_recv()
    a_send("g-", hid(1, 1, 1), zdev[3])
    b[("o+", 0)].wait_recv()
    b_send("g+", 3, 1, ring[0], xdev[1])
    b[("o-", 1)].wait_recv()
    b_send("g-", 1, 1, ring[1], xdev[3])
    to_core(3, 1, ring[0])
    to_core(1, 1, ring[1])
    a[("o+", 1)].wait_recv()
    a[("o-", 0)].wait_recv()
    b_took(("r", 0), 0, 1, rest)
    mm1(
        lambda slot: near_head(slot)
        & jnp.logical_not(near_hidden(slot))
        & jnp.logical_not(far(slot))
    )
    b_took(("o+", 1), 3, 1, ring[1])
    b_took(("o-", 0), 1, 1, ring[0])
    b_took(("r", 1), 1, 1, rest)
    b_took(("r", 3), 3, 1, rest)
    for dx in (0, 1, 3):
        core_took(dx, 1)
    mm1(lambda slot: jnp.logical_not(near_head(slot)) & jnp.logical_not(far(slot)))
    a["g+"].wait_recv()
    a["g-"].wait_recv()
    b_took(("r", 2), 2, 1, rest)
    mm1(lambda slot: far_hidden(slot) & jnp.logical_not(far_head(slot)))
    b_took("g+", 2, 1, ring[0])
    b_took("g-", 2, 1, ring[1])
    core_took(2, 1)
    mm1(far_head)

    def pool(base, length, weight, k, side, first):
        rows = pl.ds(pl.multiple_of(base + k * length, 8), length)
        for n in range(first, first + W // 2, 256):
            cols = pl.ds(n, 256)
            high = jnp.maximum(acc[rows, cols], 0.0)
            act = jnp.log1p(high)
            square = act * act
            totals[side, pl.ds(k, 1), cols] = jnp.sum(
                square * square * weight, axis=0, keepdims=True
            )

    def slope(base, length, weight, k):
        rows = pl.ds(pl.multiple_of(base + k * length, 8), length)
        for n in range(0, W, 256):
            cols = pl.ds(n, 256)
            high = jnp.maximum(acc[rows, cols], 0.0)
            act = jnp.log1p(high)
            acc[rows, cols] = weight * (act * act * act) / (1.0 + high)

    def line_weight(k):
        line = mp_ref[pl.ds(k, 1), :].astype(F32)
        shape = (LP, LP)
        eye = lax.broadcasted_iota(jnp.int32, shape, 0) == lax.broadcasted_iota(jnp.int32, shape, 1)
        return jnp.sum(jnp.where(eye, jnp.broadcast_to(line, shape), 0.0), axis=1, keepdims=True)

    def query_weight(k):
        shape = (LQ, G)
        here = lax.broadcasted_iota(jnp.int32, shape, 1) == k
        return jnp.sum(jnp.where(here, mq_ref[...].astype(F32), 0.0), axis=1, keepdims=True)

    def fourth_root(t):
        return jnp.sqrt(jnp.sqrt(t))

    def spread(ref, cols):
        mine = ref.at[r, :, cols]
        copies = [send(mine, device(z, yl, yhs[e], xs[d], c)) for d, e in RELATIVE]
        copies.append(send(mine, cdev))
        return copies

    def hand_on(ref, cols, copies):
        handed = []
        for (d, e), copy in zip(RELATIVE, copies):
            copy.wait_recv()
            came = (yhs[e] * 4 + xs[(4 - d) % 4]) * 2 + c
            handed.append(send(ref.at[came, :, cols], cdev))
        return handed

    spread_p = []
    for first in (0, W // 2):
        cols = pl.ds(first, W // 2)

        @pl.loop(0, G)
        def _(k):
            pool(0, LP, line_weight(k), k, 0, first)

        allp[r, :, cols] = (fourth_root(totals[0, :, cols] + 1.0) - 1.0).astype(BF)
        spread_p.append((cols, spread(allp, cols)))

    @pl.loop(0, G)
    def _(k):
        pool(PR, LQ, query_weight(k), k, 1, 0)
        pool(PR, LQ, query_weight(k), k, 1, W // 2)

    whole = pl.ds(0, W)
    allq[r] = (fourth_root(totals[1] + 1.0) - 1.0).astype(BF)

    @pl.loop(0, G)
    def _(k):
        slope(0, LP, line_weight(k), k)

    handed_p = []
    for cols, copies in spread_p:
        handed_p += hand_on(allp, cols, copies)
        handed_p.append(copies[7])
    spread_q = spread(allq, whole)
    for copy in handed_p:
        copy.wait_recv()

    every_pass = allp[...].reshape(ROWS * PAD, W)
    sbuf[v] = lax.dot_general(
        allq[r], every_pass, (((1,), (1,)), ((), ())), preferred_element_type=F32
    )
    shared = [send(sbuf.at[v], device(zs[d], yls[e], yh, x, c)) for d, e in RELATIVE]

    @pl.loop(0, G)
    def _(k):
        slope(PR, LQ, query_weight(k), k)

    row_at = lax.broadcasted_iota(jnp.int32, (PAD, ROWS * PAD), 0)
    col_at = lax.broadcasted_iota(jnp.int32, (PAD, ROWS * PAD), 1)
    passage = (col_at // PAD) * G + col_at % PAD
    real = (col_at % PAD < G) & (row_at < G)
    label = jnp.full((PAD, ROWS * PAD), -1, jnp.int32)
    for q in range(G):
        label = jnp.where(row_at == q, lab_ref[q], label)
    chosen = (label == passage) & real
    for copy in shared:
        copy.wait_recv()
    scores = sbuf[0]
    for k in range(1, VOCAB):
        scores = scores + sbuf[k]
    scores = scores * SCALING
    onehot = jnp.where(chosen, 1.0, 0.0)
    positive = jnp.sum(scores * onehot, axis=1, keepdims=True)
    weights = jnp.where(
        real & jnp.logical_not(chosen), jax.nn.sigmoid(MARGIN + scores - positive), 0.0
    )
    score_grad = (
        (weights - onehot * jnp.sum(weights, axis=1, keepdims=True)) * SCALING
    ).astype(BF)
    gbuf[r] = score_grad
    group = [send(gbuf.at[r], device(z, yl, yhs[e], xs[d], cs[f])) for d, e in RELATIVE for f in (0, 1)]
    group.append(send(gbuf.at[r], cdev))

    def tail(t):
        root = jnp.sqrt(t)
        return 1.0 / (root * jnp.sqrt(root))

    query_grad = jnp.dot(score_grad, every_pass, preferred_element_type=F32)
    factor[1] = query_grad * tail(totals[1] + 1.0)

    @pl.loop(0, G // 2)
    def _(k):
        rows = pl.ds(pl.multiple_of(PR + k * 2 * LQ, 2 * LQ), 2 * LQ)
        upper = lax.broadcasted_iota(jnp.int32, (2 * LQ, W), 0) < LQ
        gain = jnp.where(
            upper,
            jnp.broadcast_to(factor[1, pl.ds(2 * k, 1), :], (2 * LQ, W)),
            jnp.broadcast_to(factor[1, pl.ds(2 * k + 1, 1), :], (2 * LQ, W)),
        )
        slopes[rows, :] = (acc[rows, :] * gain).astype(BF)

    handed_q = hand_on(allq, whole, spread_q)
    spread_q[7].wait_recv()
    for copy in handed_q:
        copy.wait_recv()
    for copy in group:
        copy.wait_recv()
    pick = jnp.where(
        lax.broadcasted_iota(jnp.int32, (ROWS * PAD, PAD), 0)
        == r * PAD + lax.broadcasted_iota(jnp.int32, (ROWS * PAD, PAD), 1),
        1.0,
        0.0,
    ).astype(BF)
    mine = jnp.dot(
        gbuf[...].reshape(ROWS * PAD, ROWS * PAD), pick, preferred_element_type=F32
    ).astype(BF)
    pass_grad = lax.dot_general(
        mine,
        allq[...].reshape(ROWS * PAD, W),
        (((0,), (0,)), ((), ())),
        preferred_element_type=F32,
    )
    factor[0] = pass_grad * tail(totals[0] + 1.0)

    def pass_slopes(lo, n):
        @pl.loop(lo // 16, (lo + n) // 16)
        def _(k):
            rows = pl.ds(pl.multiple_of(k * 16, 16), 16)
            slopes[rows, :] = (acc[rows, :] * factor[0, pl.ds(k // (LP // 16), 1), :]).astype(BF)

    for copy in tok_sent:
        copy.wait_send()

    def part(dz, dy, lo, n):
        return tok.at[zs[dz] * 2 + yls[dy], pl.ds(lo, n)]

    def mm2(dz, dy):
        slot = zs[dz] * 2 + yls[dy]

        @pl.loop(0, F // 256)
        def _(n):
            cols = pl.ds(pl.multiple_of(n * 256, 256), 256)
            tok[slot, :, cols] = lax.dot_general(
                slopes[...],
                head[slot, cols, :],
                (((1,), (1,)), ((), ())),
                preferred_element_type=F32,
            ).astype(BF)

    def mm2_rows(dz, dy, lo, n):
        slot = zs[dz] * 2 + yls[dy]
        rows = pl.ds(lo, n)
        tok[slot, rows, :] = lax.dot_general(
            slopes[rows, :],
            head[slot],
            (((1,), (1,)), ((), ())),
            preferred_element_type=F32,
        ).astype(BF)

    def add_into(dz, dy, lo, size, *others):
        slot = zs[dz] * 2 + yls[dy]

        @pl.loop(0, size // 48)
        def _(k):
            rows = pl.ds(pl.multiple_of(lo + k * 48, 16), 48)
            total = tok[slot, rows, :].astype(F32)
            for other in others:
                total = total + other[rows, :].astype(F32)
            tok[slot, rows, :] = total.astype(BF)

    def out(src, dst, dev):
        copy = remote(src, dst, dev)
        sent.append(copy)
        return copy

    def to_ring(dz, dy, lo, n, ref):
        dev = zdev[1] if ref == 0 else zdev[3]
        return out(part(dz, dy, lo, n), rfull.at[dy, ref, pl.ds(lo, n)], dev)

    def to_half(dy, lo, n, ref):
        dev = zdev[1] if ref == 0 else zdev[3]
        return out(part(2, dy, lo, n), rhalf.at[dy, ref, pl.ds(lo, n)], dev)

    def to_pair(dz):
        return out(part(dz, 1, ZR, YR), yb.at[dz], yldev)

    pass_slopes(*ZH[0])
    mm2_rows(2, 1, *ZH[0])
    up = to_half(1, *ZH[0], 0)
    pass_slopes(*ZH[1])
    mm2_rows(2, 1, *ZH[1])
    down = to_half(1, *ZH[1], 1)
    pass_slopes(ZR, PR - ZR)
    mm2_rows(2, 1, ZR, YR)
    pair = {2: to_pair(2)}
    mm2(1, 1)
    other_plane = [to_ring(1, 1, *ZH[1], 0)]
    pair[1] = to_pair(1)
    mm2(3, 1)
    other_plane.append(to_ring(3, 1, *ZH[0], 1))
    pair[3] = to_pair(3)
    up.wait_recv()
    add_into(1, 1, *ZH[0], rhalf.at[1, 0])
    other_plane.append(to_ring(1, 1, *ZH[0], 0))
    down.wait_recv()
    add_into(3, 1, *ZH[1], rhalf.at[1, 1])
    other_plane.append(to_ring(3, 1, *ZH[1], 1))
    mm2(0, 1)
    last = [out(part(0, 1, ZR, YR), ybuf.at[pl.ds(ZR, YR)], yldev)]

    def add_pair(dz):
        slot = zs[dz] * 2 + yl
        pair[dz].wait_recv()

        @pl.loop(0, YR // 48)
        def _(k):
            rows = pl.ds(pl.multiple_of(ZR + k * 48, 16), 48)
            some = pl.ds(pl.multiple_of(k * 48, 16), 48)
            tok[slot, rows, :] = (
                tok[slot, rows, :].astype(F32) + yb[dz, some, :].astype(F32)
            ).astype(BF)

    mm2(2, 0)
    up = to_half(0, *ZH[0], 0)
    down = to_half(0, *ZH[1], 1)
    add_pair(2)
    up_y = to_half(0, *YH[0], 0)
    down_y = to_half(0, *YH[1], 1)
    mm2(1, 0)
    last.append(to_ring(1, 0, *ZH[1], 0))
    mm2(3, 0)
    last.append(to_ring(3, 0, *ZH[0], 1))
    for copy in other_plane:
        copy.wait_recv()
    add_into(0, 1, 0, ZR, rfull.at[1, 0], rfull.at[1, 1])
    last.append(out(part(0, 1, 0, ZR), ybuf.at[pl.ds(0, ZR)], yldev))
    up.wait_recv()
    add_into(1, 0, *ZH[0], rhalf.at[0, 0])
    last.append(to_ring(1, 0, *ZH[0], 0))
    down.wait_recv()
    add_into(3, 0, *ZH[1], rhalf.at[0, 1])
    last.append(to_ring(3, 0, *ZH[1], 1))
    add_pair(1)
    last.append(to_ring(1, 0, *YH[1], 0))
    add_pair(3)
    last.append(to_ring(3, 0, *YH[0], 1))
    mm2(0, 0)
    up_y.wait_recv()
    add_into(1, 0, *YH[0], rhalf.at[0, 0])
    last.append(to_ring(1, 0, *YH[0], 0))
    down_y.wait_recv()
    add_into(3, 0, *YH[1], rhalf.at[0, 1])
    last.append(to_ring(3, 0, *YH[1], 1))
    for copy in last:
        copy.wait_recv()

    def total(rows):
        return (
            tok[v, rows, :].astype(F32)
            + rfull[0, 0, rows, :].astype(F32)
            + rfull[0, 1, rows, :].astype(F32)
            + ybuf[rows, :].astype(F32)
        ).astype(BF)

    @pl.loop(0, PR // 48)
    def _(k):
        rows = pl.ds(pl.multiple_of(k * 48, 16), 48)
        gp_ref[rows, :] = total(rows)

    for k in range(QR // 48):
        gq_ref[pl.ds(k * 48, 48), :] = total(pl.ds(PR + k * 48, 48))

    for copy in sent:
        copy.wait_send()


COPIES = 192


def shards(hidden_pass, hidden_query, mask_pass, mask_query, labels, head_weight):
    anywhere = pl.BlockSpec(memory_space=pl.ANY)
    vmem = pl.BlockSpec(memory_space=pltpu.VMEM)
    smem = pl.BlockSpec(memory_space=pltpu.SMEM)
    grad_pass, grad_query = pl.pallas_call(
        kernel,
        out_shape=(
            jax.ShapeDtypeStruct((PR, F), BF),
            jax.ShapeDtypeStruct((QR, F), BF),
        ),
        in_specs=[anywhere, anywhere, vmem, vmem, smem, anywhere],
        out_specs=(vmem, vmem),
        scratch_shapes=[
            pltpu.VMEM((VOCAB, R, F), BF),
            pltpu.VMEM((VOCAB, 2 * HD, W), BF),
            pltpu.VMEM((R, W), F32),
            pltpu.VMEM((R, W), BF),
            pltpu.VMEM((2, PAD, W), F32),
            pltpu.VMEM((2, PAD, W), F32),
            pltpu.VMEM((ROWS, PAD, W), BF),
            pltpu.VMEM((ROWS, PAD, W), BF),
            pltpu.VMEM((VOCAB, PAD, ROWS * PAD), F32),
            pltpu.VMEM((ROWS, PAD, ROWS * PAD), BF),
            pltpu.VMEM((2, 2, R, F), BF),
            pltpu.VMEM((2, 2, R, F), BF),
            pltpu.VMEM((R, F), BF),
            pltpu.VMEM((4, YR, F), BF),
            pltpu.SemaphoreType.DMA((3,)),
            pltpu.SemaphoreType.DMA((COPIES,)),
            pltpu.SemaphoreType.DMA((COPIES,)),
        ],
        compiler_params=pltpu.CompilerParams(
            collective_id=0, has_side_effects=True, vmem_limit_bytes=52 * 1024 * 1024
        ),
        name="step",
    )(
        hidden_pass.reshape(PR, F),
        hidden_query.reshape(QR, F),
        mask_pass,
        mask_query.T,
        labels,
        head_weight,
    )
    return (
        grad_pass.reshape(G, LP, F),
        grad_query.reshape(G, LQ, F),
    )


def solution(mesh):
    return jax.shard_map(
        shards,
        mesh=mesh,
        in_specs=(
            P("rows", None, "vocab"),
            P("rows", None, "vocab"),
            P("rows", None),
            P("rows", None),
            P("rows"),
            P("rows", "vocab"),
        ),
        out_specs=(P("rows", None, "vocab"), P("rows", None, "vocab")),
        check_vma=False,
    )
```

```python
import jax
import jax.numpy as jnp
from jax import lax
from jax.experimental import pallas as pl
from jax.experimental.pallas import tpu as pltpu
from jax.sharding import PartitionSpec as P

MESH = pl.DeviceIdType.MESH
MARGIN = 1.0
SHARPNESS = 16.0
V = 16384
SCALING = SHARPNESS * V ** (-0.5)

G = 12
LP = 64
LQ = 8
PR = G * LP
QR = G * LQ
R = PR + QR
RH = R // 2
ZR = 512
ZH = ((0, 256), (256, 256))
YR = R - ZR
YH = ((512, 176), (688, 176))
F = 512
W = 2048
HD = 256
HH = HD // 2
HY = 96
HX = HD - 2 * HY
PAD = 16
ROWS = 16
VOCAB = 8
BF = jnp.bfloat16
F32 = jnp.float32

RELATIVE = [(1, 0), (3, 0), (2, 0), (0, 1), (1, 1), (3, 1), (2, 1)]


def where_am_i():
    v = lax.axis_index("vocab")
    r = lax.axis_index("rows")
    return v // 2, v % 2, r // 8, (r // 2) % 4, r % 2


def device(z, yl, yh, x, c):
    return (z * 2 + yl, (yh * 4 + x) * 2 + c)


def kernel(
    hp_ref,
    hq_ref,
    mp_ref,
    mq_ref,
    lab_ref,
    hw_ref,
    gp_ref,
    gq_ref,
    tok,
    head,
    acc,
    slopes,
    totals,
    factor,
    allp,
    allq,
    sbuf,
    gbuf,
    rhalf,
    rfull,
    ybuf,
    yb,
    lsem,
    ssem,
    rsem,
):
    z, yl, yh, x, c = where_am_i()
    v = z * 2 + yl
    r = (yh * 4 + x) * 2 + c
    zs = [z, (z + 1) % 4, (z + 2) % 4, (z + 3) % 4]
    xs = [x, (x + 1) % 4, (x + 2) % 4, (x + 3) % 4]
    yls = [yl, 1 - yl]
    yhs = [yh, 1 - yh]
    cs = [c, 1 - c]
    zdev = [device(k, yl, yh, x, c) for k in zs]
    xdev = [device(z, yl, yh, k, c) for k in xs]
    yldev = device(z, 1 - yl, yh, x, c)
    yhdev = device(z, yl, 1 - yh, x, c)
    cdev = device(z, yl, yh, x, 1 - c)

    own_head = yh * 4 + x
    local = [
        pltpu.make_async_copy(hp_ref, tok.at[v, pl.ds(0, PR)], lsem.at[0]),
        pltpu.make_async_copy(hq_ref, tok.at[v, pl.ds(PR, QR)], lsem.at[1]),
        pltpu.make_async_copy(hw_ref, head.at[own_head, pl.ds(c * HD, HD)], lsem.at[2]),
    ]
    for copy in local:
        copy.start()

    peers = [zdev[1], zdev[3], yldev, xdev[1], xdev[3], yhdev, cdev]
    barrier = pltpu.get_barrier_semaphore()
    for peer in peers:
        pl.semaphore_signal(barrier, inc=1, device_id=peer, device_id_type=MESH)
    for copy in local:
        copy.wait()
    pl.semaphore_wait(barrier, len(peers))

    counter = [0]
    sent = []

    def remote(src, dst, dev):
        k = counter[0]
        counter[0] += 1
        copy = pltpu.make_async_remote_copy(
            src_ref=src,
            dst_ref=dst,
            send_sem=ssem.at[k],
            recv_sem=rsem.at[k],
            device_id=dev,
            device_id_type=MESH,
        )
        copy.start()
        return copy

    def send(ref, dev):
        copy = remote(ref, ref, dev)
        sent.append(copy)
        return copy

    def hid(dz, dy, h):
        return tok.at[zs[dz] * 2 + yls[dy], pl.ds(h * RH, RH)]

    def hed(dx, dy, lo, n):
        return head.at[yhs[dy] * 4 + xs[dx], pl.ds(c * HD + lo, n)]

    halves = ((0, HH), (HH, HH))
    ring = ((0, HY), (HY, HY))
    rest = (2 * HY, HX)
    a, b, s = {}, {}, {}
    tok_sent = []

    def a_send(key, ref, dev):
        copy = remote(ref, ref, dev)
        a[key] = copy
        tok_sent.append(copy)

    def b_send(key, dx, dy, part, dev):
        b[key] = send(hed(dx, dy, *part), dev)

    def to_core(dx, dy, part):
        s.setdefault((dx, dy), []).append(send(hed(dx, dy, *part), cdev))

    def b_took(key, dx, dy, part):
        b[key].wait_recv()
        to_core(dx, dy, part)

    a_send(("y", 0), hid(0, 0, 0), yldev)
    a_send(("+", 0), hid(0, 0, 0), zdev[1])
    a_send(("-", 1), hid(0, 0, 1), zdev[3])
    b_send(("+", 0), 0, 0, halves[0], xdev[1])
    b_send(("-", 1), 0, 0, halves[1], xdev[3])
    a_send(("y", 1), hid(0, 0, 1), yldev)
    b_send(("y", 0), 0, 0, ring[0], yhdev)
    b_send(("y", 1), 0, 0, ring[1], yhdev)
    a_send(("+", 1), hid(0, 0, 1), zdev[1])
    a_send(("-", 0), hid(0, 0, 0), zdev[3])
    b_send(("+", 1), 0, 0, halves[1], xdev[1])
    b_send(("-", 0), 0, 0, halves[0], xdev[3])
    b_send(("r", 0), 0, 0, rest, yhdev)
    to_core(0, 0, halves[0])
    to_core(0, 0, halves[1])

    acc[...] = jnp.zeros_like(acc)
    totals[...] = jnp.zeros_like(totals)

    a[("+", 0)].wait_recv()
    a_send("f+", hid(3, 0, 0), zdev[1])
    a[("-", 1)].wait_recv()
    a_send("f-", hid(1, 0, 1), zdev[3])
    b[("+", 0)].wait_recv()
    b_send("f+", 3, 0, halves[0], xdev[1])
    b[("-", 1)].wait_recv()
    b_send("f-", 1, 0, halves[1], xdev[3])
    b_send(("r", 1), 1, 0, rest, yhdev)
    to_core(3, 0, halves[0])
    to_core(1, 0, halves[1])

    a[("y", 0)].wait_recv()
    a_send(("o+", 0), hid(0, 1, 0), zdev[1])
    b_took(("+", 1), 3, 0, halves[1])
    b_send(("r", 3), 3, 0, rest, yhdev)
    b_took(("-", 0), 1, 0, halves[0])
    a[("y", 1)].wait_recv()
    a_send(("o-", 1), hid(0, 1, 1), zdev[3])
    a_send(("o-", 0), hid(0, 1, 0), zdev[3])
    a_send(("o+", 1), hid(0, 1, 1), zdev[1])
    b[("y", 0)].wait_recv()
    b_send(("o+", 0), 0, 1, ring[0], xdev[1])
    b_send(("o-", 0), 0, 1, (0, HY // 2), xdev[3])
    b[("y", 1)].wait_recv()
    b_send(("o-", 1), 0, 1, ring[1], xdev[3])
    b_send(("o-", 2), 0, 1, (HY // 2, HY // 2), xdev[3])
    b_send(("o+", 1), 0, 1, ring[1], xdev[1])
    to_core(0, 1, ring[0])
    to_core(0, 1, ring[1])
    b_took("f+", 2, 0, halves[0])
    b_took("f-", 2, 0, halves[1])
    b_send(("r", 2), 2, 0, rest, yhdev)

    def core_took(dx, dy):
        for copy in s[(dx, dy)]:
            copy.wait_recv()

    def mm1(ready):
        @pl.loop(0, VOCAB)
        def _(slot):
            @pl.when(ready(slot))
            def _():
                @pl.loop(0, 2)
                def _(n):
                    cols = pl.ds(pl.multiple_of(n * (W // 2), W // 2), W // 2)
                    acc[:, cols] += jnp.dot(
                        tok[slot], head[slot, :, cols], preferred_element_type=F32
                    )

    def near_head(slot):
        return slot // 4 == yh

    def near_hidden(slot):
        return slot % 2 == yl

    def far_head(slot):
        return jnp.logical_not(near_head(slot)) & (slot % 4 == xs[2])

    def far_hidden(slot):
        return jnp.logical_not(near_hidden(slot)) & (slot // 2 == zs[2])

    def far(slot):
        return far_head(slot) | far_hidden(slot)

    for key in [("+", 1), ("-", 0), "f+", "f-"]:
        a[key].wait_recv()
    for dx in range(4):
        core_took(dx, 0)
    mm1(lambda slot: near_head(slot) & near_hidden(slot))
    a[("o+", 0)].wait_recv()
    a_send("g+", hid(3, 1, 0), zdev[1])
    a[("o-", 1)].wait_recv()
    a_send("g-", hid(1, 1, 1), zdev[3])
    b[("o+", 0)].wait_recv()
    b_send("g+", 3, 1, ring[0], xdev[1])
    b[("o-", 1)].wait_recv()
    b_send("g-", 1, 1, ring[1], xdev[3])
    to_core(3, 1, ring[0])
    to_core(1, 1, ring[1])
    a[("o+", 1)].wait_recv()
    a[("o-", 0)].wait_recv()
    b_took(("r", 0), 0, 1, rest)
    core_took(0, 1)
    mm1(
        lambda slot: (
            (near_head(slot) & jnp.logical_not(near_hidden(slot)))
            | (slot == (1 - yh) * 4 + x)
        )
        & jnp.logical_not(far_hidden(slot))
    )
    b_took(("o+", 1), 3, 1, ring[1])
    b_took(("o-", 0), 1, 1, (0, HY // 2))
    b_took(("o-", 2), 1, 1, (HY // 2, HY // 2))
    b_took(("r", 1), 1, 1, rest)
    b_took(("r", 3), 3, 1, rest)
    for dx in (1, 3):
        core_took(dx, 1)
    mm1(
        lambda slot: jnp.logical_not(near_head(slot))
        & (slot % 4 != x)
        & jnp.logical_not(far(slot))
    )
    b_took(("r", 2), 2, 1, rest)
    b_took("g+", 2, 1, ring[0])
    b_took("g-", 2, 1, ring[1])
    a["g+"].wait_recv()
    a["g-"].wait_recv()
    mm1(lambda slot: far_hidden(slot) & jnp.logical_not(far_head(slot)))
    core_took(2, 1)
    mm1(far_head)

    def pool(base, length, weight, k, side, first):
        rows = pl.ds(pl.multiple_of(base + k * length, 8), length)
        for n in range(first, first + W // 2, 256):
            cols = pl.ds(n, 256)
            high = jnp.maximum(acc[rows, cols], 0.0)
            act = jnp.log1p(high)
            square = act * act
            totals[side, pl.ds(k, 1), cols] = jnp.sum(
                square * square * weight, axis=0, keepdims=True
            )

    def slope(base, length, weight, k):
        rows = pl.ds(pl.multiple_of(base + k * length, 8), length)
        for n in range(0, W, 256):
            cols = pl.ds(n, 256)
            high = jnp.maximum(acc[rows, cols], 0.0)
            act = jnp.log1p(high)
            acc[rows, cols] = weight * (act * act * act) / (1.0 + high)

    def line_weight(k):
        line = mp_ref[pl.ds(k, 1), :].astype(F32)
        shape = (LP, LP)
        eye = lax.broadcasted_iota(jnp.int32, shape, 0) == lax.broadcasted_iota(jnp.int32, shape, 1)
        return jnp.sum(jnp.where(eye, jnp.broadcast_to(line, shape), 0.0), axis=1, keepdims=True)

    def query_weight(k):
        shape = (LQ, G)
        here = lax.broadcasted_iota(jnp.int32, shape, 1) == k
        return jnp.sum(jnp.where(here, mq_ref[...].astype(F32), 0.0), axis=1, keepdims=True)

    def fourth_root(t):
        return jnp.sqrt(jnp.sqrt(t))

    def spread(ref, cols):
        mine = ref.at[r, :, cols]
        copies = [send(mine, device(z, yl, yhs[e], xs[d], c)) for d, e in RELATIVE]
        copies.append(send(mine, cdev))
        return copies

    def hand_on(ref, cols, copies):
        handed = []
        for (d, e), copy in zip(RELATIVE, copies):
            copy.wait_recv()
            came = (yhs[e] * 4 + xs[(4 - d) % 4]) * 2 + c
            handed.append(send(ref.at[came, :, cols], cdev))
        return handed

    spread_p = []
    for first in (0, W // 2):
        cols = pl.ds(first, W // 2)

        @pl.loop(0, G)
        def _(k):
            pool(0, LP, line_weight(k), k, 0, first)

        allp[r, :, cols] = (fourth_root(totals[0, :, cols] + 1.0) - 1.0).astype(BF)
        spread_p.append((cols, spread(allp, cols)))

    @pl.loop(0, G)
    def _(k):
        pool(PR, LQ, query_weight(k), k, 1, 0)
        pool(PR, LQ, query_weight(k), k, 1, W // 2)

    whole = pl.ds(0, W)
    allq[r] = (fourth_root(totals[1] + 1.0) - 1.0).astype(BF)

    @pl.loop(0, G)
    def _(k):
        slope(0, LP, line_weight(k), k)

    spread_q = spread(allq, whole)
    handed_p = []
    for cols, copies in spread_p:
        handed_p += hand_on(allp, cols, copies)
        handed_p.append(copies[7])
    for copy in handed_p:
        copy.wait_recv()

    every_pass = allp[...].reshape(ROWS * PAD, W)
    sbuf[v] = lax.dot_general(
        allq[r], every_pass, (((1,), (1,)), ((), ())), preferred_element_type=F32
    )
    shared = [send(sbuf.at[v], device(zs[d], yls[e], yh, x, c)) for d, e in RELATIVE]

    @pl.loop(0, G)
    def _(k):
        slope(PR, LQ, query_weight(k), k)

    row_at = lax.broadcasted_iota(jnp.int32, (PAD, ROWS * PAD), 0)
    col_at = lax.broadcasted_iota(jnp.int32, (PAD, ROWS * PAD), 1)
    passage = (col_at // PAD) * G + col_at % PAD
    real = (col_at % PAD < G) & (row_at < G)
    label = jnp.full((PAD, ROWS * PAD), -1, jnp.int32)
    for q in range(G):
        label = jnp.where(row_at == q, lab_ref[q], label)
    chosen = (label == passage) & real
    for copy in shared:
        copy.wait_recv()
    scores = sbuf[0]
    for k in range(1, VOCAB):
        scores = scores + sbuf[k]
    scores = scores * SCALING
    onehot = jnp.where(chosen, 1.0, 0.0)
    positive = jnp.sum(scores * onehot, axis=1, keepdims=True)
    weights = jnp.where(
        real & jnp.logical_not(chosen), jax.nn.sigmoid(MARGIN + scores - positive), 0.0
    )
    score_grad = (
        (weights - onehot * jnp.sum(weights, axis=1, keepdims=True)) * SCALING
    ).astype(BF)
    gbuf[r] = score_grad
    group = [send(gbuf.at[r], device(z, yl, yhs[e], xs[d], cs[f])) for d, e in RELATIVE for f in (0, 1)]
    group.append(send(gbuf.at[r], cdev))
    handed_q = hand_on(allq, whole, spread_q)

    def tail(t):
        root = jnp.sqrt(t)
        return 1.0 / (root * jnp.sqrt(root))

    query_grad = jnp.dot(score_grad, every_pass, preferred_element_type=F32)
    factor[1] = query_grad * tail(totals[1] + 1.0)

    @pl.loop(0, G // 2)
    def _(k):
        rows = pl.ds(pl.multiple_of(PR + k * 2 * LQ, 2 * LQ), 2 * LQ)
        upper = lax.broadcasted_iota(jnp.int32, (2 * LQ, W), 0) < LQ
        gain = jnp.where(
            upper,
            jnp.broadcast_to(factor[1, pl.ds(2 * k, 1), :], (2 * LQ, W)),
            jnp.broadcast_to(factor[1, pl.ds(2 * k + 1, 1), :], (2 * LQ, W)),
        )
        slopes[rows, :] = (acc[rows, :] * gain).astype(BF)

    spread_q[7].wait_recv()
    for copy in handed_q:
        copy.wait_recv()
    for copy in group:
        copy.wait_recv()
    pick = jnp.where(
        lax.broadcasted_iota(jnp.int32, (ROWS * PAD, PAD), 0)
        == r * PAD + lax.broadcasted_iota(jnp.int32, (ROWS * PAD, PAD), 1),
        1.0,
        0.0,
    ).astype(BF)
    mine = jnp.dot(
        gbuf[...].reshape(ROWS * PAD, ROWS * PAD), pick, preferred_element_type=F32
    ).astype(BF)
    pass_grad = lax.dot_general(
        mine,
        allq[...].reshape(ROWS * PAD, W),
        (((0,), (0,)), ((), ())),
        preferred_element_type=F32,
    )
    factor[0] = pass_grad * tail(totals[0] + 1.0)

    def pass_slopes(lo, n):
        @pl.loop(lo // 16, (lo + n) // 16)
        def _(k):
            rows = pl.ds(pl.multiple_of(k * 16, 16), 16)
            slopes[rows, :] = (acc[rows, :] * factor[0, pl.ds(k // (LP // 16), 1), :]).astype(BF)

    for copy in tok_sent:
        copy.wait_send()

    def part(dz, dy, lo, n):
        return tok.at[zs[dz] * 2 + yls[dy], pl.ds(lo, n)]

    def mm2(dz, dy):
        slot = zs[dz] * 2 + yls[dy]

        @pl.loop(0, F // 256)
        def _(n):
            cols = pl.ds(pl.multiple_of(n * 256, 256), 256)
            tok[slot, :, cols] = lax.dot_general(
                slopes[...],
                head[slot, cols, :],
                (((1,), (1,)), ((), ())),
                preferred_element_type=F32,
            ).astype(BF)

    def mm2_rows(dz, dy, lo, n):
        slot = zs[dz] * 2 + yls[dy]
        rows = pl.ds(lo, n)
        tok[slot, rows, :] = lax.dot_general(
            slopes[rows, :],
            head[slot],
            (((1,), (1,)), ((), ())),
            preferred_element_type=F32,
        ).astype(BF)

    def add_into(dz, dy, lo, size, *others):
        slot = zs[dz] * 2 + yls[dy]

        @pl.loop(0, size // 16)
        def _(k):
            rows = pl.ds(pl.multiple_of(lo + k * 16, 16), 16)
            total = tok[slot, rows, :].astype(F32)
            for other in others:
                total = total + other[rows, :].astype(F32)
            tok[slot, rows, :] = total.astype(BF)

    def out(src, dst, dev):
        copy = remote(src, dst, dev)
        sent.append(copy)
        return copy

    def to_ring(dz, dy, lo, n, ref):
        dev = zdev[1] if ref == 0 else zdev[3]
        return out(part(dz, dy, lo, n), rfull.at[dy, ref, pl.ds(lo, n)], dev)

    def to_half(dy, lo, n, ref):
        dev = zdev[1] if ref == 0 else zdev[3]
        return out(part(2, dy, lo, n), rhalf.at[dy, ref, pl.ds(lo, n)], dev)

    def to_pair(dz):
        return out(part(dz, 1, ZR, YR), yb.at[dz], yldev)

    pass_slopes(*ZH[0])
    mm2_rows(2, 1, *ZH[0])
    up = to_half(1, *ZH[0], 0)
    pass_slopes(*ZH[1])
    mm2_rows(2, 1, *ZH[1])
    down = to_half(1, *ZH[1], 1)
    pass_slopes(ZR, PR - ZR)
    mm2_rows(2, 1, ZR, YR)
    pair = {2: to_pair(2)}
    mm2(1, 1)
    other_plane = [to_ring(1, 1, *ZH[1], 0)]
    pair[1] = to_pair(1)
    mm2(3, 1)
    other_plane.append(to_ring(3, 1, *ZH[0], 1))
    pair[3] = to_pair(3)
    up.wait_recv()
    add_into(1, 1, *ZH[0], rhalf.at[1, 0])
    other_plane.append(to_ring(1, 1, *ZH[0], 0))
    down.wait_recv()
    add_into(3, 1, *ZH[1], rhalf.at[1, 1])
    other_plane.append(to_ring(3, 1, *ZH[1], 1))
    mm2(0, 1)
    last = [out(part(0, 1, ZR, YR), ybuf.at[pl.ds(ZR, YR)], yldev)]

    def add_pair(dz):
        slot = zs[dz] * 2 + yl
        pair[dz].wait_recv()

        @pl.loop(0, YR // 32)
        def _(k):
            rows = pl.ds(pl.multiple_of(ZR + k * 32, 16), 32)
            some = pl.ds(pl.multiple_of(k * 32, 16), 32)
            tok[slot, rows, :] = (
                tok[slot, rows, :].astype(F32) + yb[dz, some, :].astype(F32)
            ).astype(BF)

    mm2(2, 0)
    up = to_half(0, *ZH[0], 0)
    down = to_half(0, *ZH[1], 1)
    add_pair(2)
    up_y = to_half(0, *YH[0], 0)
    down_y = to_half(0, *YH[1], 1)
    mm2(1, 0)
    last.append(to_ring(1, 0, *ZH[1], 0))
    mm2(3, 0)
    last.append(to_ring(3, 0, *ZH[0], 1))
    for copy in other_plane:
        copy.wait_recv()
    add_into(0, 1, 0, ZR, rfull.at[1, 0], rfull.at[1, 1])
    last.append(out(part(0, 1, 0, ZR), ybuf.at[pl.ds(0, ZR)], yldev))
    up.wait_recv()
    add_into(1, 0, *ZH[0], rhalf.at[0, 0])
    last.append(to_ring(1, 0, *ZH[0], 0))
    down.wait_recv()
    add_into(3, 0, *ZH[1], rhalf.at[0, 1])
    last.append(to_ring(3, 0, *ZH[1], 1))
    add_pair(1)
    last.append(to_ring(1, 0, *YH[1], 0))
    add_pair(3)
    last.append(to_ring(3, 0, *YH[0], 1))
    mm2(0, 0)
    up_y.wait_recv()
    add_into(1, 0, *YH[0], rhalf.at[0, 0])
    last.append(to_ring(1, 0, *YH[0], 0))
    down_y.wait_recv()
    add_into(3, 0, *YH[1], rhalf.at[0, 1])
    last.append(to_ring(3, 0, *YH[1], 1))
    for copy in last:
        copy.wait_recv()

    def total(rows):
        return (
            tok[v, rows, :].astype(F32)
            + rfull[0, 0, rows, :].astype(F32)
            + rfull[0, 1, rows, :].astype(F32)
            + ybuf[rows, :].astype(F32)
        ).astype(BF)

    @pl.loop(0, PR // 48)
    def _(k):
        rows = pl.ds(pl.multiple_of(k * 48, 16), 48)
        gp_ref[rows, :] = total(rows)

    for k in range(QR // 48):
        gq_ref[pl.ds(k * 48, 48), :] = total(pl.ds(PR + k * 48, 48))

    for copy in sent:
        copy.wait_send()


COPIES = 192


def shards(hidden_pass, hidden_query, mask_pass, mask_query, labels, head_weight):
    anywhere = pl.BlockSpec(memory_space=pl.ANY)
    vmem = pl.BlockSpec(memory_space=pltpu.VMEM)
    smem = pl.BlockSpec(memory_space=pltpu.SMEM)
    grad_pass, grad_query = pl.pallas_call(
        kernel,
        out_shape=(
            jax.ShapeDtypeStruct((PR, F), BF),
            jax.ShapeDtypeStruct((QR, F), BF),
        ),
        in_specs=[anywhere, anywhere, vmem, vmem, smem, anywhere],
        out_specs=(vmem, vmem),
        scratch_shapes=[
            pltpu.VMEM((VOCAB, R, F), BF),
            pltpu.VMEM((VOCAB, 2 * HD, W), BF),
            pltpu.VMEM((R, W), F32),
            pltpu.VMEM((R, W), BF),
            pltpu.VMEM((2, PAD, W), F32),
            pltpu.VMEM((2, PAD, W), F32),
            pltpu.VMEM((ROWS, PAD, W), BF),
            pltpu.VMEM((ROWS, PAD, W), BF),
            pltpu.VMEM((VOCAB, PAD, ROWS * PAD), F32),
            pltpu.VMEM((ROWS, PAD, ROWS * PAD), BF),
            pltpu.VMEM((2, 2, R, F), BF),
            pltpu.VMEM((2, 2, R, F), BF),
            pltpu.VMEM((R, F), BF),
            pltpu.VMEM((4, YR, F), BF),
            pltpu.SemaphoreType.DMA((3,)),
            pltpu.SemaphoreType.DMA((COPIES,)),
            pltpu.SemaphoreType.DMA((COPIES,)),
        ],
        compiler_params=pltpu.CompilerParams(
            collective_id=0, has_side_effects=True, vmem_limit_bytes=60 * 1024 * 1024
        ),
        name="step",
    )(
        hidden_pass.reshape(PR, F),
        hidden_query.reshape(QR, F),
        mask_pass,
        mask_query.T,
        labels,
        head_weight,
    )
    return (
        grad_pass.reshape(G, LP, F),
        grad_query.reshape(G, LQ, F),
    )


def solution(mesh):
    return jax.shard_map(
        shards,
        mesh=mesh,
        in_specs=(
            P("rows", None, "vocab"),
            P("rows", None, "vocab"),
            P("rows", None),
            P("rows", None),
            P("rows"),
            P("rows", "vocab"),
        ),
        out_specs=(P("rows", None, "vocab"), P("rows", None, "vocab")),
        check_vma=False,
    )
```

```python
import jax
import jax.numpy as jnp
from jax import lax
from jax.experimental import pallas as pl
from jax.experimental.pallas import tpu as pltpu
from jax.sharding import PartitionSpec as P

MESH = pl.DeviceIdType.MESH
MARGIN = 1.0
SHARPNESS = 16.0
V = 16384
SCALING = SHARPNESS * V ** (-0.5)

G = 12
LP = 64
LQ = 8
PR = G * LP
QR = G * LQ
R = PR + QR
RH = R // 2
ZR = 512
ZH = ((0, 256), (256, 256))
YR = R - ZR
YH = ((512, 176), (688, 176))
F = 512
W = 2048
HD = 256
HH = HD // 2
HY = 96
HX = HD - 2 * HY
PAD = 16
ROWS = 16
VOCAB = 8
BF = jnp.bfloat16
F32 = jnp.float32

RELATIVE = [(1, 0), (3, 0), (2, 0), (0, 1), (1, 1), (3, 1), (2, 1)]


def where_am_i():
    v = lax.axis_index("vocab")
    r = lax.axis_index("rows")
    return v // 2, v % 2, r // 8, (r // 2) % 4, r % 2


def device(z, yl, yh, x, c):
    return (z * 2 + yl, (yh * 4 + x) * 2 + c)


def kernel(
    hp_ref,
    hq_ref,
    mp_ref,
    mq_ref,
    lab_ref,
    hw_ref,
    gp_ref,
    gq_ref,
    tok,
    head,
    acc,
    slopes,
    totals,
    factor,
    allp,
    allq,
    sbuf,
    gbuf,
    rhalf,
    rfull,
    ybuf,
    yb,
    lsem,
    ssem,
    rsem,
):
    z, yl, yh, x, c = where_am_i()
    v = z * 2 + yl
    r = (yh * 4 + x) * 2 + c
    zs = [z, (z + 1) % 4, (z + 2) % 4, (z + 3) % 4]
    xs = [x, (x + 1) % 4, (x + 2) % 4, (x + 3) % 4]
    yls = [yl, 1 - yl]
    yhs = [yh, 1 - yh]
    cs = [c, 1 - c]
    zdev = [device(k, yl, yh, x, c) for k in zs]
    xdev = [device(z, yl, yh, k, c) for k in xs]
    yldev = device(z, 1 - yl, yh, x, c)
    yhdev = device(z, yl, 1 - yh, x, c)
    cdev = device(z, yl, yh, x, 1 - c)

    own_head = yh * 4 + x
    local = [
        pltpu.make_async_copy(hp_ref, tok.at[v, pl.ds(0, PR)], lsem.at[0]),
        pltpu.make_async_copy(hq_ref, tok.at[v, pl.ds(PR, QR)], lsem.at[1]),
        pltpu.make_async_copy(hw_ref, head.at[own_head, pl.ds(c * HD, HD)], lsem.at[2]),
    ]
    for copy in local:
        copy.start()

    peers = [zdev[1], zdev[3], yldev, xdev[1], xdev[3], yhdev, cdev]
    barrier = pltpu.get_barrier_semaphore()
    for peer in peers:
        pl.semaphore_signal(barrier, inc=1, device_id=peer, device_id_type=MESH)
    for copy in local:
        copy.wait()
    pl.semaphore_wait(barrier, len(peers))

    counter = [0]
    sent = []

    def remote(src, dst, dev):
        k = counter[0]
        counter[0] += 1
        copy = pltpu.make_async_remote_copy(
            src_ref=src,
            dst_ref=dst,
            send_sem=ssem.at[k],
            recv_sem=rsem.at[k],
            device_id=dev,
            device_id_type=MESH,
        )
        copy.start()
        return copy

    def send(ref, dev):
        copy = remote(ref, ref, dev)
        sent.append(copy)
        return copy

    def hid(dz, dy, h):
        return tok.at[zs[dz] * 2 + yls[dy], pl.ds(h * RH, RH)]

    def hed(dx, dy, lo, n):
        return head.at[yhs[dy] * 4 + xs[dx], pl.ds(c * HD + lo, n)]

    halves = ((0, HH), (HH, HH))
    ring = ((0, HY), (HY, HY))
    rest = (2 * HY, HX)
    a, b, s = {}, {}, {}
    tok_sent = []

    def a_send(key, ref, dev):
        copy = remote(ref, ref, dev)
        a[key] = copy
        tok_sent.append(copy)

    def b_send(key, dx, dy, part, dev):
        b[key] = send(hed(dx, dy, *part), dev)

    def to_core(dx, dy, part):
        s.setdefault((dx, dy), []).append(send(hed(dx, dy, *part), cdev))

    def b_took(key, dx, dy, part):
        b[key].wait_recv()
        to_core(dx, dy, part)

    a_send(("y", 0), hid(0, 0, 0), yldev)
    a_send(("+", 0), hid(0, 0, 0), zdev[1])
    a_send(("-", 1), hid(0, 0, 1), zdev[3])
    b_send(("+", 0), 0, 0, halves[0], xdev[1])
    b_send(("-", 1), 0, 0, halves[1], xdev[3])
    a_send(("y", 1), hid(0, 0, 1), yldev)
    b_send(("y", 0), 0, 0, ring[0], yhdev)
    b_send(("y", 1), 0, 0, ring[1], yhdev)
    a_send(("+", 1), hid(0, 0, 1), zdev[1])
    a_send(("-", 0), hid(0, 0, 0), zdev[3])
    b_send(("+", 1), 0, 0, halves[1], xdev[1])
    b_send(("-", 0), 0, 0, halves[0], xdev[3])
    b_send(("r", 0), 0, 0, rest, yhdev)
    to_core(0, 0, halves[0])
    to_core(0, 0, halves[1])

    acc[...] = jnp.zeros_like(acc)
    totals[...] = jnp.zeros_like(totals)

    a[("+", 0)].wait_recv()
    a_send("f+", hid(3, 0, 0), zdev[1])
    a[("-", 1)].wait_recv()
    a_send("f-", hid(1, 0, 1), zdev[3])
    b[("+", 0)].wait_recv()
    b_send("f+", 3, 0, halves[0], xdev[1])
    b[("-", 1)].wait_recv()
    b_send("f-", 1, 0, halves[1], xdev[3])
    b_send(("r", 1), 1, 0, rest, yhdev)
    to_core(3, 0, halves[0])
    to_core(1, 0, halves[1])

    a[("y", 0)].wait_recv()
    a_send(("o+", 0), hid(0, 1, 0), zdev[1])
    b_took(("+", 1), 3, 0, halves[1])
    b_send(("r", 3), 3, 0, rest, yhdev)
    b_took(("-", 0), 1, 0, halves[0])
    a[("y", 1)].wait_recv()
    a_send(("o-", 1), hid(0, 1, 1), zdev[3])
    a_send(("o-", 0), hid(0, 1, 0), zdev[3])
    a_send(("o+", 1), hid(0, 1, 1), zdev[1])
    b[("y", 0)].wait_recv()
    b_send(("o+", 0), 0, 1, ring[0], xdev[1])
    b_send(("o-", 0), 0, 1, (0, HY // 2), xdev[3])
    b[("y", 1)].wait_recv()
    b_send(("o-", 1), 0, 1, ring[1], xdev[3])
    b_send(("o-", 2), 0, 1, (HY // 2, HY // 2), xdev[3])
    b_send(("o+", 1), 0, 1, ring[1], xdev[1])
    to_core(0, 1, ring[0])
    to_core(0, 1, ring[1])
    b_took("f+", 2, 0, halves[0])
    b_took("f-", 2, 0, halves[1])
    b_send(("r", 2), 2, 0, rest, yhdev)

    def core_took(dx, dy):
        for copy in s[(dx, dy)]:
            copy.wait_recv()

    def mm1_part(slot, half):
        feats = pl.ds(pl.multiple_of(half * HD, HD), HD)

        @pl.loop(0, 2)
        def _(n):
            cols = pl.ds(pl.multiple_of(n * (W // 2), W // 2), W // 2)
            acc[:, cols] += jnp.dot(
                tok[slot, :, feats], head[slot, feats, cols], preferred_element_type=F32
            )

    def mm1(ready):
        @pl.loop(0, VOCAB)
        def _(slot):
            @pl.when(ready(slot))
            def _():
                @pl.loop(0, 2)
                def _(n):
                    cols = pl.ds(pl.multiple_of(n * (W // 2), W // 2), W // 2)
                    acc[:, cols] += jnp.dot(
                        tok[slot], head[slot, :, cols], preferred_element_type=F32
                    )

    def near_head(slot):
        return slot // 4 == yh

    def near_hidden(slot):
        return slot % 2 == yl

    def early(slot):
        return near_hidden(slot) | (slot // 2 == z)

    def far_head(slot):
        return slot == yhs[1] * 4 + xs[2]

    def far_hidden(slot):
        return jnp.logical_not(near_hidden(slot)) & (slot // 2 == zs[2])

    for key in [("+", 1), ("-", 0), "f+", "f-"]:
        a[key].wait_recv()
    for dx in range(4):
        core_took(dx, 0)
    mm1(lambda slot: near_head(slot) & early(slot))
    a[("o+", 0)].wait_recv()
    a_send("g+", hid(3, 1, 0), zdev[1])
    a[("o-", 1)].wait_recv()
    a_send("g-", hid(1, 1, 1), zdev[3])
    b[("o+", 0)].wait_recv()
    b_send("g+", 3, 1, ring[0], xdev[1])
    to_core(3, 1, ring[0])
    b_took(("r", 0), 0, 1, rest)
    b_took(("o-", 0), 1, 1, (0, HY // 2))
    core_took(0, 1)
    mm1(lambda slot: (slot == yhs[1] * 4 + x) & early(slot))
    b[("o-", 1)].wait_recv()
    b_send("g-", 1, 1, ring[1], xdev[3])
    to_core(1, 1, ring[1])
    a[("o+", 1)].wait_recv()
    a[("o-", 0)].wait_recv()
    mm1(
        lambda slot: (near_head(slot) | (slot == yhs[1] * 4 + x))
        & jnp.logical_not(early(slot))
        & jnp.logical_not(far_hidden(slot))
    )
    b_took(("r", 1), 1, 1, rest)
    b_took(("o-", 2), 1, 1, (HY // 2, HY // 2))
    b_took(("o+", 1), 3, 1, ring[1])
    b_took(("r", 3), 3, 1, rest)
    core_took(1, 1)
    mm1(lambda slot: (slot == yhs[1] * 4 + xs[1]) & jnp.logical_not(far_hidden(slot)))
    core_took(3, 1)
    mm1(lambda slot: (slot == yhs[1] * 4 + xs[3]) & jnp.logical_not(far_hidden(slot)))
    b_took(("r", 2), 2, 1, rest)
    b_took("g+", 2, 1, ring[0])
    b_took("g-", 2, 1, ring[1])
    a["g+"].wait_recv()
    a["g-"].wait_recv()
    mm1(lambda slot: far_hidden(slot) & jnp.logical_not(far_head(slot)))
    mm1_part(yhs[1] * 4 + xs[2], c)
    core_took(2, 1)
    mm1_part(yhs[1] * 4 + xs[2], 1 - c)

    def pool(base, length, weight, k, side, first):
        rows = pl.ds(pl.multiple_of(base + k * length, 8), length)
        for n in range(first, first + W // 2, 256):
            cols = pl.ds(n, 256)
            high = jnp.maximum(acc[rows, cols], 0.0)
            act = jnp.log1p(high)
            square = act * act
            totals[side, pl.ds(k, 1), cols] = jnp.sum(
                square * square * weight, axis=0, keepdims=True
            )

    def slope(base, length, weight, k):
        rows = pl.ds(pl.multiple_of(base + k * length, 8), length)
        for n in range(0, W, 256):
            cols = pl.ds(n, 256)
            high = jnp.maximum(acc[rows, cols], 0.0)
            act = jnp.log1p(high)
            acc[rows, cols] = weight * (act * act * act) / (1.0 + high)

    def line_weight(k):
        line = mp_ref[pl.ds(k, 1), :].astype(F32)
        shape = (LP, LP)
        eye = lax.broadcasted_iota(jnp.int32, shape, 0) == lax.broadcasted_iota(jnp.int32, shape, 1)
        return jnp.sum(jnp.where(eye, jnp.broadcast_to(line, shape), 0.0), axis=1, keepdims=True)

    def query_weight(k):
        shape = (LQ, G)
        here = lax.broadcasted_iota(jnp.int32, shape, 1) == k
        return jnp.sum(jnp.where(here, mq_ref[...].astype(F32), 0.0), axis=1, keepdims=True)

    def fourth_root(t):
        return jnp.sqrt(jnp.sqrt(t))

    def spread(ref, cols):
        mine = ref.at[r, :, cols]
        copies = [send(mine, device(z, yl, yhs[e], xs[d], c)) for d, e in RELATIVE]
        copies.append(send(mine, cdev))
        return copies

    def hand_on(ref, cols, copies):
        handed = []
        for (d, e), copy in zip(RELATIVE, copies):
            copy.wait_recv()
            came = (yhs[e] * 4 + xs[(4 - d) % 4]) * 2 + c
            handed.append(send(ref.at[came, :, cols], cdev))
        return handed

    spread_p = []
    for first in (0, W // 2):
        cols = pl.ds(first, W // 2)

        @pl.loop(0, G)
        def _(k):
            pool(0, LP, line_weight(k), k, 0, first)

        allp[r, :, cols] = (fourth_root(totals[0, :, cols] + 1.0) - 1.0).astype(BF)
        spread_p.append((cols, spread(allp, cols)))

    @pl.loop(0, G)
    def _(k):
        pool(PR, LQ, query_weight(k), k, 1, 0)
        pool(PR, LQ, query_weight(k), k, 1, W // 2)

    whole = pl.ds(0, W)
    allq[r] = (fourth_root(totals[1] + 1.0) - 1.0).astype(BF)

    @pl.loop(0, G)
    def _(k):
        slope(0, LP, line_weight(k), k)

    spread_q = spread(allq, whole)
    handed_p = []
    for cols, copies in spread_p:
        handed_p += hand_on(allp, cols, copies)
        handed_p.append(copies[7])
    for copy in handed_p:
        copy.wait_recv()

    every_pass = allp[...].reshape(ROWS * PAD, W)
    sbuf[v] = lax.dot_general(
        allq[r], every_pass, (((1,), (1,)), ((), ())), preferred_element_type=F32
    )
    shared = [send(sbuf.at[v], device(zs[d], yls[e], yh, x, c)) for d, e in RELATIVE]

    @pl.loop(0, G)
    def _(k):
        slope(PR, LQ, query_weight(k), k)

    row_at = lax.broadcasted_iota(jnp.int32, (PAD, ROWS * PAD), 0)
    col_at = lax.broadcasted_iota(jnp.int32, (PAD, ROWS * PAD), 1)
    passage = (col_at // PAD) * G + col_at % PAD
    real = (col_at % PAD < G) & (row_at < G)
    label = jnp.full((PAD, ROWS * PAD), -1, jnp.int32)
    for q in range(G):
        label = jnp.where(row_at == q, lab_ref[q], label)
    chosen = (label == passage) & real
    for copy in shared:
        copy.wait_recv()
    scores = sbuf[0]
    for k in range(1, VOCAB):
        scores = scores + sbuf[k]
    scores = scores * SCALING
    onehot = jnp.where(chosen, 1.0, 0.0)
    positive = jnp.sum(scores * onehot, axis=1, keepdims=True)
    weights = jnp.where(
        real & jnp.logical_not(chosen), jax.nn.sigmoid(MARGIN + scores - positive), 0.0
    )
    score_grad = (
        (weights - onehot * jnp.sum(weights, axis=1, keepdims=True)) * SCALING
    ).astype(BF)
    gbuf[r] = score_grad
    group = [send(gbuf.at[r], device(z, yl, yhs[e], xs[d], cs[f])) for d, e in RELATIVE for f in (0, 1)]
    group.append(send(gbuf.at[r], cdev))
    handed_q = hand_on(allq, whole, spread_q)

    def tail(t):
        root = jnp.sqrt(t)
        return 1.0 / (root * jnp.sqrt(root))

    query_grad = jnp.dot(score_grad, every_pass, preferred_element_type=F32)
    factor[1] = query_grad * tail(totals[1] + 1.0)

    @pl.loop(0, G // 2)
    def _(k):
        rows = pl.ds(pl.multiple_of(PR + k * 2 * LQ, 2 * LQ), 2 * LQ)
        upper = lax.broadcasted_iota(jnp.int32, (2 * LQ, W), 0) < LQ
        gain = jnp.where(
            upper,
            jnp.broadcast_to(factor[1, pl.ds(2 * k, 1), :], (2 * LQ, W)),
            jnp.broadcast_to(factor[1, pl.ds(2 * k + 1, 1), :], (2 * LQ, W)),
        )
        slopes[rows, :] = (acc[rows, :] * gain).astype(BF)

    spread_q[7].wait_recv()
    for copy in handed_q:
        copy.wait_recv()
    for copy in group:
        copy.wait_recv()
    pick = jnp.where(
        lax.broadcasted_iota(jnp.int32, (ROWS * PAD, PAD), 0)
        == r * PAD + lax.broadcasted_iota(jnp.int32, (ROWS * PAD, PAD), 1),
        1.0,
        0.0,
    ).astype(BF)
    mine = jnp.dot(
        gbuf[...].reshape(ROWS * PAD, ROWS * PAD), pick, preferred_element_type=F32
    ).astype(BF)
    pass_grad = lax.dot_general(
        mine,
        allq[...].reshape(ROWS * PAD, W),
        (((0,), (0,)), ((), ())),
        preferred_element_type=F32,
    )
    factor[0] = pass_grad * tail(totals[0] + 1.0)

    def pass_slopes(lo, n):
        @pl.loop(lo // 16, (lo + n) // 16)
        def _(k):
            rows = pl.ds(pl.multiple_of(k * 16, 16), 16)
            slopes[rows, :] = (acc[rows, :] * factor[0, pl.ds(k // (LP // 16), 1), :]).astype(BF)

    for copy in tok_sent:
        copy.wait_send()

    def part(dz, dy, lo, n):
        return tok.at[zs[dz] * 2 + yls[dy], pl.ds(lo, n)]

    def mm2(dz, dy):
        slot = zs[dz] * 2 + yls[dy]

        @pl.loop(0, F // 256)
        def _(n):
            cols = pl.ds(pl.multiple_of(n * 256, 256), 256)
            tok[slot, :, cols] = lax.dot_general(
                slopes[...],
                head[slot, cols, :],
                (((1,), (1,)), ((), ())),
                preferred_element_type=F32,
            ).astype(BF)

    def mm2_rows(dz, dy, lo, n):
        slot = zs[dz] * 2 + yls[dy]
        rows = pl.ds(lo, n)
        tok[slot, rows, :] = lax.dot_general(
            slopes[rows, :],
            head[slot],
            (((1,), (1,)), ((), ())),
            preferred_element_type=F32,
        ).astype(BF)

    def add_into(dz, dy, lo, size, *others):
        slot = zs[dz] * 2 + yls[dy]

        @pl.loop(0, size // 16)
        def _(k):
            rows = pl.ds(pl.multiple_of(lo + k * 16, 16), 16)
            total = tok[slot, rows, :].astype(F32)
            for other in others:
                total = total + other[rows, :].astype(F32)
            tok[slot, rows, :] = total.astype(BF)

    def out(src, dst, dev):
        copy = remote(src, dst, dev)
        sent.append(copy)
        return copy

    def to_ring(dz, dy, lo, n, ref):
        dev = zdev[1] if ref == 0 else zdev[3]
        return out(part(dz, dy, lo, n), rfull.at[dy, ref, pl.ds(lo, n)], dev)

    def to_half(dy, lo, n, ref):
        dev = zdev[1] if ref == 0 else zdev[3]
        return out(part(2, dy, lo, n), rhalf.at[dy, ref, pl.ds(lo, n)], dev)

    def to_pair(dz):
        return out(part(dz, 1, ZR, YR), yb.at[dz], yldev)

    pass_slopes(*ZH[0])
    mm2_rows(2, 1, *ZH[0])
    up = to_half(1, *ZH[0], 0)
    pass_slopes(*ZH[1])
    mm2_rows(2, 1, *ZH[1])
    down = to_half(1, *ZH[1], 1)
    pass_slopes(ZR, PR - ZR)
    mm2_rows(2, 1, ZR, YR)
    pair = {2: to_pair(2)}
    mm2(1, 1)
    other_plane = [to_ring(1, 1, *ZH[1], 0)]
    pair[1] = to_pair(1)
    mm2(3, 1)
    other_plane.append(to_ring(3, 1, *ZH[0], 1))
    pair[3] = to_pair(3)
    up.wait_recv()
    add_into(1, 1, *ZH[0], rhalf.at[1, 0])
    other_plane.append(to_ring(1, 1, *ZH[0], 0))
    down.wait_recv()
    add_into(3, 1, *ZH[1], rhalf.at[1, 1])
    other_plane.append(to_ring(3, 1, *ZH[1], 1))
    mm2(0, 1)
    last = [out(part(0, 1, ZR, YR), ybuf.at[pl.ds(ZR, YR)], yldev)]

    def add_pair(dz):
        slot = zs[dz] * 2 + yl
        pair[dz].wait_recv()

        @pl.loop(0, YR // 32)
        def _(k):
            rows = pl.ds(pl.multiple_of(ZR + k * 32, 16), 32)
            some = pl.ds(pl.multiple_of(k * 32, 16), 32)
            tok[slot, rows, :] = (
                tok[slot, rows, :].astype(F32) + yb[dz, some, :].astype(F32)
            ).astype(BF)

    mm2(2, 0)
    up = to_half(0, *ZH[0], 0)
    down = to_half(0, *ZH[1], 1)
    add_pair(2)
    up_y = to_half(0, *YH[0], 0)
    down_y = to_half(0, *YH[1], 1)
    mm2(1, 0)
    last.append(to_ring(1, 0, *ZH[1], 0))
    mm2(3, 0)
    last.append(to_ring(3, 0, *ZH[0], 1))
    for copy in other_plane:
        copy.wait_recv()
    add_into(0, 1, 0, ZR, rfull.at[1, 0], rfull.at[1, 1])
    last.append(out(part(0, 1, 0, ZR), ybuf.at[pl.ds(0, ZR)], yldev))
    up.wait_recv()
    add_into(1, 0, *ZH[0], rhalf.at[0, 0])
    last.append(to_ring(1, 0, *ZH[0], 0))
    down.wait_recv()
    add_into(3, 0, *ZH[1], rhalf.at[0, 1])
    last.append(to_ring(3, 0, *ZH[1], 1))
    add_pair(1)
    last.append(to_ring(1, 0, *YH[1], 0))
    add_pair(3)
    last.append(to_ring(3, 0, *YH[0], 1))
    mm2(0, 0)
    up_y.wait_recv()
    add_into(1, 0, *YH[0], rhalf.at[0, 0])
    last.append(to_ring(1, 0, *YH[0], 0))
    down_y.wait_recv()
    add_into(3, 0, *YH[1], rhalf.at[0, 1])
    last.append(to_ring(3, 0, *YH[1], 1))
    for copy in last:
        copy.wait_recv()

    def total(rows):
        return (
            tok[v, rows, :].astype(F32)
            + rfull[0, 0, rows, :].astype(F32)
            + rfull[0, 1, rows, :].astype(F32)
            + ybuf[rows, :].astype(F32)
        ).astype(BF)

    @pl.loop(0, PR // 48)
    def _(k):
        rows = pl.ds(pl.multiple_of(k * 48, 16), 48)
        gp_ref[rows, :] = total(rows)

    for k in range(QR // 48):
        gq_ref[pl.ds(k * 48, 48), :] = total(pl.ds(PR + k * 48, 48))

    for copy in sent:
        copy.wait_send()


COPIES = 192


def shards(hidden_pass, hidden_query, mask_pass, mask_query, labels, head_weight):
    anywhere = pl.BlockSpec(memory_space=pl.ANY)
    vmem = pl.BlockSpec(memory_space=pltpu.VMEM)
    smem = pl.BlockSpec(memory_space=pltpu.SMEM)
    grad_pass, grad_query = pl.pallas_call(
        kernel,
        out_shape=(
            jax.ShapeDtypeStruct((PR, F), BF),
            jax.ShapeDtypeStruct((QR, F), BF),
        ),
        in_specs=[anywhere, anywhere, vmem, vmem, smem, anywhere],
        out_specs=(vmem, vmem),
        scratch_shapes=[
            pltpu.VMEM((VOCAB, R, F), BF),
            pltpu.VMEM((VOCAB, 2 * HD, W), BF),
            pltpu.VMEM((R, W), F32),
            pltpu.VMEM((R, W), BF),
            pltpu.VMEM((2, PAD, W), F32),
            pltpu.VMEM((2, PAD, W), F32),
            pltpu.VMEM((ROWS, PAD, W), BF),
            pltpu.VMEM((ROWS, PAD, W), BF),
            pltpu.VMEM((VOCAB, PAD, ROWS * PAD), F32),
            pltpu.VMEM((ROWS, PAD, ROWS * PAD), BF),
            pltpu.VMEM((2, 2, R, F), BF),
            pltpu.VMEM((2, 2, R, F), BF),
            pltpu.VMEM((R, F), BF),
            pltpu.VMEM((4, YR, F), BF),
            pltpu.SemaphoreType.DMA((3,)),
            pltpu.SemaphoreType.DMA((COPIES,)),
            pltpu.SemaphoreType.DMA((COPIES,)),
        ],
        compiler_params=pltpu.CompilerParams(
            collective_id=0, has_side_effects=True, vmem_limit_bytes=60 * 1024 * 1024
        ),
        name="step",
    )(
        hidden_pass.reshape(PR, F),
        hidden_query.reshape(QR, F),
        mask_pass,
        mask_query.T,
        labels,
        head_weight,
    )
    return (
        grad_pass.reshape(G, LP, F),
        grad_query.reshape(G, LQ, F),
    )


def solution(mesh):
    return jax.shard_map(
        shards,
        mesh=mesh,
        in_specs=(
            P("rows", None, "vocab"),
            P("rows", None, "vocab"),
            P("rows", None),
            P("rows", None),
            P("rows"),
            P("rows", "vocab"),
        ),
        out_specs=(P("rows", None, "vocab"), P("rows", None, "vocab")),
        check_vma=False,
    )
```

```python
import jax
import jax.numpy as jnp
from jax import lax
from jax.experimental import pallas as pl
from jax.experimental.pallas import tpu as pltpu
from jax.sharding import PartitionSpec as P

MESH = pl.DeviceIdType.MESH
MARGIN = 1.0
SHARPNESS = 16.0
V = 16384
SCALING = SHARPNESS * V ** (-0.5)

G = 12
LP = 64
LQ = 8
PR = G * LP
QR = G * LQ
R = PR + QR
RH = R // 2
ZR = 464
ZH = ((0, 240), (240, 224))
YR = R - ZR
YH = ((464, 208), (672, 192))
F = 512
W = 2048
HD = 256
HH = HD // 2
HY = 96
HX = HD - 2 * HY
PAD = 16
ROWS = 16
VOCAB = 8
BF = jnp.bfloat16
F32 = jnp.float32

RELATIVE = [(1, 0), (3, 0), (2, 0), (0, 1), (1, 1), (3, 1), (2, 1)]


def where_am_i():
    v = lax.axis_index("vocab")
    r = lax.axis_index("rows")
    return v // 2, v % 2, r // 8, (r // 2) % 4, r % 2


def device(z, yl, yh, x, c):
    return (z * 2 + yl, (yh * 4 + x) * 2 + c)


def kernel(
    hp_ref,
    hq_ref,
    mp_hbm,
    mq_hbm,
    lab_hbm,
    hw_ref,
    gp_ref,
    gq_ref,
    tok,
    head,
    acc,
    slopes,
    totals,
    factor,
    allp,
    allq,
    sbuf,
    gbuf,
    rhalf,
    rfull,
    ybuf,
    yb,
    mp_ref,
    mq_ref,
    lab_ref,
    lsem,
    ssem,
    rsem,
):
    z, yl, yh, x, c = where_am_i()
    v = z * 2 + yl
    r = (yh * 4 + x) * 2 + c
    zs = [z, (z + 1) % 4, (z + 2) % 4, (z + 3) % 4]
    xs = [x, (x + 1) % 4, (x + 2) % 4, (x + 3) % 4]
    yls = [yl, 1 - yl]
    yhs = [yh, 1 - yh]
    cs = [c, 1 - c]
    zdev = [device(k, yl, yh, x, c) for k in zs]
    xdev = [device(z, yl, yh, k, c) for k in xs]
    yldev = device(z, 1 - yl, yh, x, c)
    yhdev = device(z, yl, 1 - yh, x, c)
    cdev = device(z, yl, yh, x, 1 - c)

    own_head = yh * 4 + x
    local = [
        pltpu.make_async_copy(hp_ref, tok.at[v, pl.ds(0, PR)], lsem.at[0]),
        pltpu.make_async_copy(hq_ref, tok.at[v, pl.ds(PR, QR)], lsem.at[1]),
        pltpu.make_async_copy(hw_ref, head.at[own_head, pl.ds(c * HD, HD)], lsem.at[2]),
        pltpu.make_async_copy(mp_hbm, mp_ref, lsem.at[3]),
        pltpu.make_async_copy(mq_hbm, mq_ref, lsem.at[4]),
        pltpu.make_async_copy(lab_hbm, lab_ref, lsem.at[5]),
    ]
    for copy in local:
        copy.start()

    peers = [zdev[1], zdev[3], yldev, xdev[1], xdev[3], yhdev, cdev]
    barrier = pltpu.get_barrier_semaphore()
    for peer in peers:
        pl.semaphore_signal(barrier, inc=1, device_id=peer, device_id_type=MESH)
    for copy in local:
        copy.wait()
    pl.semaphore_wait(barrier, len(peers))

    counter = [0]
    sent = []

    def remote(src, dst, dev):
        k = counter[0]
        counter[0] += 1
        copy = pltpu.make_async_remote_copy(
            src_ref=src,
            dst_ref=dst,
            send_sem=ssem.at[k],
            recv_sem=rsem.at[k],
            device_id=dev,
            device_id_type=MESH,
        )
        copy.start()
        return copy

    def send(ref, dev):
        copy = remote(ref, ref, dev)
        sent.append(copy)
        return copy

    def hid(dz, dy, h):
        return tok.at[zs[dz] * 2 + yls[dy], pl.ds(h * RH, RH)]

    def hed(dx, dy, lo, n):
        return head.at[yhs[dy] * 4 + xs[dx], pl.ds(c * HD + lo, n)]

    halves = ((0, HH), (HH, HH))
    ring = ((0, HY), (HY, HY))
    rest = (2 * HY, HX)
    a, b, s = {}, {}, {}
    tok_sent = []

    def a_send(key, ref, dev):
        copy = remote(ref, ref, dev)
        a[key] = copy
        tok_sent.append(copy)

    def b_send(key, dx, dy, part, dev):
        b[key] = send(hed(dx, dy, *part), dev)

    def to_core(dx, dy, part):
        s.setdefault((dx, dy), []).append(send(hed(dx, dy, *part), cdev))

    def b_took(key, dx, dy, part):
        b[key].wait_recv()
        to_core(dx, dy, part)

    a_send(("y", 0), hid(0, 0, 0), yldev)
    a_send(("+", 0), hid(0, 0, 0), zdev[1])
    a_send(("-", 1), hid(0, 0, 1), zdev[3])
    b_send(("+", 0), 0, 0, halves[0], xdev[1])
    b_send(("-", 1), 0, 0, halves[1], xdev[3])
    a_send(("y", 1), hid(0, 0, 1), yldev)
    b_send(("y", 0), 0, 0, ring[0], yhdev)
    b_send(("y", 1), 0, 0, ring[1], yhdev)
    a_send(("+", 1), hid(0, 0, 1), zdev[1])
    a_send(("-", 0), hid(0, 0, 0), zdev[3])
    b_send(("+", 1), 0, 0, halves[1], xdev[1])
    b_send(("-", 0), 0, 0, halves[0], xdev[3])
    b_send(("r", 0), 0, 0, rest, yhdev)
    to_core(0, 0, halves[0])
    to_core(0, 0, halves[1])

    acc[...] = jnp.zeros_like(acc)
    totals[...] = jnp.zeros_like(totals)

    a[("+", 0)].wait_recv()
    a_send("f+", hid(3, 0, 0), zdev[1])
    a[("-", 1)].wait_recv()
    a_send("f-", hid(1, 0, 1), zdev[3])
    b[("+", 0)].wait_recv()
    b_send("f+", 3, 0, halves[0], xdev[1])
    b[("-", 1)].wait_recv()
    b_send("f-", 1, 0, halves[1], xdev[3])
    b_send(("r", 1), 1, 0, rest, yhdev)
    to_core(3, 0, halves[0])
    to_core(1, 0, halves[1])

    a[("y", 0)].wait_recv()
    a_send(("o+", 0), hid(0, 1, 0), zdev[1])
    b_took(("+", 1), 3, 0, halves[1])
    b_send(("r", 3), 3, 0, rest, yhdev)
    b_took(("-", 0), 1, 0, halves[0])
    a[("y", 1)].wait_recv()
    a_send(("o-", 1), hid(0, 1, 1), zdev[3])
    a_send(("o-", 0), hid(0, 1, 0), zdev[3])
    a_send(("o+", 1), hid(0, 1, 1), zdev[1])
    b[("y", 0)].wait_recv()
    b_send(("o+", 0), 0, 1, ring[0], xdev[1])
    b_send(("o-", 0), 0, 1, (0, HY // 2), xdev[3])
    b[("y", 1)].wait_recv()
    b_send(("o-", 1), 0, 1, ring[1], xdev[3])
    b_send(("o-", 2), 0, 1, (HY // 2, HY // 2), xdev[3])
    b_send(("o+", 1), 0, 1, ring[1], xdev[1])
    to_core(0, 1, ring[0])
    to_core(0, 1, ring[1])
    b_took("f+", 2, 0, halves[0])
    b_took("f-", 2, 0, halves[1])
    b_send(("r", 2), 2, 0, rest, yhdev)

    def core_took(dx, dy):
        for copy in s[(dx, dy)]:
            copy.wait_recv()

    def mm1_part(slot, half):
        feats = pl.ds(pl.multiple_of(half * HD, HD), HD)

        @pl.loop(0, 2)
        def _(n):
            cols = pl.ds(pl.multiple_of(n * (W // 2), W // 2), W // 2)
            acc[:, cols] += jnp.dot(
                tok[slot, :, feats], head[slot, feats, cols], preferred_element_type=F32
            )

    def mm1(ready):
        @pl.loop(0, VOCAB)
        def _(slot):
            @pl.when(ready(slot))
            def _():
                @pl.loop(0, 2)
                def _(n):
                    cols = pl.ds(pl.multiple_of(n * (W // 2), W // 2), W // 2)
                    acc[:, cols] += jnp.dot(
                        tok[slot], head[slot, :, cols], preferred_element_type=F32
                    )

    def near_head(slot):
        return slot // 4 == yh

    def near_hidden(slot):
        return slot % 2 == yl

    def early(slot):
        return near_hidden(slot) | (slot // 2 == z)

    def far_head(slot):
        return slot == yhs[1] * 4 + xs[2]

    def far_hidden(slot):
        return jnp.logical_not(near_hidden(slot)) & (slot // 2 == zs[2])

    for key in [("+", 1), ("-", 0), "f+", "f-"]:
        a[key].wait_recv()
    for dx in range(4):
        core_took(dx, 0)
    mm1(lambda slot: near_head(slot) & early(slot))
    a[("o+", 0)].wait_recv()
    a_send("g+", hid(3, 1, 0), zdev[1])
    a[("o-", 1)].wait_recv()
    a_send("g-", hid(1, 1, 1), zdev[3])
    b[("o+", 0)].wait_recv()
    b_send("g+", 3, 1, ring[0], xdev[1])
    to_core(3, 1, ring[0])
    b_took(("r", 0), 0, 1, rest)
    b_took(("o-", 0), 1, 1, (0, HY // 2))
    core_took(0, 1)
    mm1(lambda slot: (slot == yhs[1] * 4 + x) & early(slot))
    b[("o-", 1)].wait_recv()
    b_send("g-", 1, 1, ring[1], xdev[3])
    to_core(1, 1, ring[1])
    a[("o+", 1)].wait_recv()
    a[("o-", 0)].wait_recv()
    mm1(
        lambda slot: (near_head(slot) | (slot == yhs[1] * 4 + x))
        & jnp.logical_not(early(slot))
        & jnp.logical_not(far_hidden(slot))
    )
    b_took(("r", 1), 1, 1, rest)
    b_took(("o-", 2), 1, 1, (HY // 2, HY // 2))
    b_took(("o+", 1), 3, 1, ring[1])
    b_took(("r", 3), 3, 1, rest)
    core_took(1, 1)
    mm1(lambda slot: (slot == yhs[1] * 4 + xs[1]) & jnp.logical_not(far_hidden(slot)))
    core_took(3, 1)
    mm1(lambda slot: (slot == yhs[1] * 4 + xs[3]) & jnp.logical_not(far_hidden(slot)))
    b_took(("r", 2), 2, 1, rest)
    b_took("g+", 2, 1, ring[0])
    b_took("g-", 2, 1, ring[1])
    a["g+"].wait_recv()
    a["g-"].wait_recv()
    mm1(lambda slot: far_hidden(slot) & jnp.logical_not(far_head(slot)))
    mm1_part(yhs[1] * 4 + xs[2], c)
    core_took(2, 1)
    mm1_part(yhs[1] * 4 + xs[2], 1 - c)

    def pool(base, length, weight, k, side, first):
        rows = pl.ds(pl.multiple_of(base + k * length, 8), length)
        for n in range(first, first + W // 2, 256):
            cols = pl.ds(n, 256)
            high = jnp.maximum(acc[rows, cols], 0.0)
            act = jnp.log1p(high)
            square = act * act
            totals[side, pl.ds(k, 1), cols] = jnp.sum(
                square * square * weight, axis=0, keepdims=True
            )

    def slope(base, length, weight, k):
        rows = pl.ds(pl.multiple_of(base + k * length, 8), length)
        for n in range(0, W, 256):
            cols = pl.ds(n, 256)
            high = jnp.maximum(acc[rows, cols], 0.0)
            act = jnp.log1p(high)
            acc[rows, cols] = weight * (act * act * act) / (1.0 + high)

    def line_weight(k):
        line = mp_ref[pl.ds(k, 1), :].astype(F32)
        shape = (LP, LP)
        eye = lax.broadcasted_iota(jnp.int32, shape, 0) == lax.broadcasted_iota(jnp.int32, shape, 1)
        return jnp.sum(jnp.where(eye, jnp.broadcast_to(line, shape), 0.0), axis=1, keepdims=True)

    def query_weight(k):
        shape = (LQ, G)
        here = lax.broadcasted_iota(jnp.int32, shape, 1) == k
        return jnp.sum(jnp.where(here, mq_ref[...].astype(F32), 0.0), axis=1, keepdims=True)

    def fourth_root(t):
        return jnp.sqrt(jnp.sqrt(t))

    def spread(ref, cols):
        mine = ref.at[r, :, cols]
        copies = [send(mine, device(z, yl, yhs[e], xs[d], c)) for d, e in RELATIVE]
        copies.append(send(mine, cdev))
        return copies

    def hand_on(ref, cols, copies):
        handed = []
        for (d, e), copy in zip(RELATIVE, copies):
            copy.wait_recv()
            came = (yhs[e] * 4 + xs[(4 - d) % 4]) * 2 + c
            handed.append(send(ref.at[came, :, cols], cdev))
        return handed

    spread_p = []
    for first in (0, W // 2):
        cols = pl.ds(first, W // 2)

        @pl.loop(0, G)
        def _(k):
            pool(0, LP, line_weight(k), k, 0, first)

        allp[r, :, cols] = (fourth_root(totals[0, :, cols] + 1.0) - 1.0).astype(BF)
        spread_p.append((cols, spread(allp, cols)))

    @pl.loop(0, G)
    def _(k):
        pool(PR, LQ, query_weight(k), k, 1, 0)
        pool(PR, LQ, query_weight(k), k, 1, W // 2)

    whole = pl.ds(0, W)
    allq[r] = (fourth_root(totals[1] + 1.0) - 1.0).astype(BF)

    @pl.loop(0, G)
    def _(k):
        slope(0, LP, line_weight(k), k)

    spread_q = spread(allq, whole)
    handed_p = []
    for cols, copies in spread_p:
        handed_p += hand_on(allp, cols, copies)
        handed_p.append(copies[7])
    for copy in handed_p:
        copy.wait_recv()

    every_pass = allp[...].reshape(ROWS * PAD, W)
    sbuf[v] = lax.dot_general(
        allq[r], every_pass, (((1,), (1,)), ((), ())), preferred_element_type=F32
    )
    shared = [send(sbuf.at[v], device(zs[d], yls[e], yh, x, c)) for d, e in RELATIVE]

    @pl.loop(0, G)
    def _(k):
        slope(PR, LQ, query_weight(k), k)

    row_at = lax.broadcasted_iota(jnp.int32, (PAD, ROWS * PAD), 0)
    col_at = lax.broadcasted_iota(jnp.int32, (PAD, ROWS * PAD), 1)
    passage = (col_at // PAD) * G + col_at % PAD
    real = (col_at % PAD < G) & (row_at < G)
    label = jnp.full((PAD, ROWS * PAD), -1, jnp.int32)
    for q in range(G):
        label = jnp.where(row_at == q, lab_ref[q], label)
    chosen = (label == passage) & real
    for copy in shared:
        copy.wait_recv()
    scores = sbuf[0]
    for k in range(1, VOCAB):
        scores = scores + sbuf[k]
    scores = scores * SCALING
    onehot = jnp.where(chosen, 1.0, 0.0)
    positive = jnp.sum(scores * onehot, axis=1, keepdims=True)
    weights = jnp.where(
        real & jnp.logical_not(chosen), jax.nn.sigmoid(MARGIN + scores - positive), 0.0
    )
    score_grad = (
        (weights - onehot * jnp.sum(weights, axis=1, keepdims=True)) * SCALING
    ).astype(BF)
    gbuf[r] = score_grad
    group = [send(gbuf.at[r], device(z, yl, yhs[e], xs[d], cs[f])) for d, e in RELATIVE for f in (0, 1)]
    group.append(send(gbuf.at[r], cdev))
    handed_q = hand_on(allq, whole, spread_q)

    def tail(t):
        root = jnp.sqrt(t)
        return 1.0 / (root * jnp.sqrt(root))

    query_grad = jnp.dot(score_grad, every_pass, preferred_element_type=F32)
    factor[1] = query_grad * tail(totals[1] + 1.0)

    @pl.loop(0, G // 2)
    def _(k):
        rows = pl.ds(pl.multiple_of(PR + k * 2 * LQ, 2 * LQ), 2 * LQ)
        upper = lax.broadcasted_iota(jnp.int32, (2 * LQ, W), 0) < LQ
        gain = jnp.where(
            upper,
            jnp.broadcast_to(factor[1, pl.ds(2 * k, 1), :], (2 * LQ, W)),
            jnp.broadcast_to(factor[1, pl.ds(2 * k + 1, 1), :], (2 * LQ, W)),
        )
        slopes[rows, :] = (acc[rows, :] * gain).astype(BF)

    for copy in tok_sent:
        copy.wait_send()

    def part(dz, dy, lo, n):
        return tok.at[zs[dz] * 2 + yls[dy], pl.ds(lo, n)]

    def mm2(dz, dy):
        slot = zs[dz] * 2 + yls[dy]

        @pl.loop(0, F // 256)
        def _(n):
            cols = pl.ds(pl.multiple_of(n * 256, 256), 256)
            tok[slot, :, cols] = lax.dot_general(
                slopes[...],
                head[slot, cols, :],
                (((1,), (1,)), ((), ())),
                preferred_element_type=F32,
            ).astype(BF)

    def mm2_pass(dz, dy):
        slot = zs[dz] * 2 + yls[dy]

        @pl.loop(0, F // 256)
        def _(n):
            cols = pl.ds(pl.multiple_of(n * 256, 256), 256)
            tok[slot, pl.ds(0, PR), cols] = lax.dot_general(
                slopes[pl.ds(0, PR), :],
                head[slot, cols, :],
                (((1,), (1,)), ((), ())),
                preferred_element_type=F32,
            ).astype(BF)

    def mm2_rows(dz, dy, lo, n):
        slot = zs[dz] * 2 + yls[dy]
        rows = pl.ds(lo, n)
        tok[slot, rows, :] = lax.dot_general(
            slopes[rows, :],
            head[slot],
            (((1,), (1,)), ((), ())),
            preferred_element_type=F32,
        ).astype(BF)

    def add_into(dz, dy, lo, size, *others):
        slot = zs[dz] * 2 + yls[dy]

        @pl.loop(0, size // 16)
        def _(k):
            rows = pl.ds(pl.multiple_of(lo + k * 16, 16), 16)
            total = tok[slot, rows, :].astype(F32)
            for other in others:
                total = total + other[rows, :].astype(F32)
            tok[slot, rows, :] = total.astype(BF)

    def out(src, dst, dev):
        copy = remote(src, dst, dev)
        sent.append(copy)
        return copy

    def to_ring(dz, dy, lo, n, ref):
        dev = zdev[1] if ref == 0 else zdev[3]
        return out(part(dz, dy, lo, n), rfull.at[dy, ref, pl.ds(lo, n)], dev)

    def to_half(dy, lo, n, ref):
        dev = zdev[1] if ref == 0 else zdev[3]
        return out(part(2, dy, lo, n), rhalf.at[dy, ref, pl.ds(lo, n)], dev)

    def to_pair(dz, lo, n):
        return out(part(dz, 1, lo, n), yb.at[dz, pl.ds(lo - ZR, n)], yldev)

    pair = {0: [], 1: [], 2: [], 3: []}
    for dz in (2, 1):
        mm2_rows(dz, 1, PR, QR)
        pair[dz].append(to_pair(dz, PR, QR))

    spread_q[7].wait_recv()
    for copy in handed_q:
        copy.wait_recv()
    for copy in group:
        copy.wait_recv()
    pick = jnp.where(
        lax.broadcasted_iota(jnp.int32, (ROWS * PAD, PAD), 0)
        == r * PAD + lax.broadcasted_iota(jnp.int32, (ROWS * PAD, PAD), 1),
        1.0,
        0.0,
    ).astype(BF)
    mine = jnp.dot(
        gbuf[...].reshape(ROWS * PAD, ROWS * PAD), pick, preferred_element_type=F32
    ).astype(BF)
    pass_grad = lax.dot_general(
        mine,
        allq[...].reshape(ROWS * PAD, W),
        (((0,), (0,)), ((), ())),
        preferred_element_type=F32,
    )
    factor[0] = pass_grad * tail(totals[0] + 1.0)

    def pass_slopes(lo, n):
        @pl.loop(lo // 16, (lo + n) // 16)
        def _(k):
            rows = pl.ds(pl.multiple_of(k * 16, 16), 16)
            slopes[rows, :] = (acc[rows, :] * factor[0, pl.ds(k // (LP // 16), 1), :]).astype(BF)

    pass_slopes(*ZH[0])
    mm2_rows(2, 1, *ZH[0])
    up = to_half(1, *ZH[0], 0)
    pass_slopes(*ZH[1])
    mm2_rows(2, 1, *ZH[1])
    down = to_half(1, *ZH[1], 1)
    pass_slopes(ZR, PR - ZR)
    mm2_rows(2, 1, ZR, PR - ZR)
    pair[2].append(to_pair(2, ZR, PR - ZR))
    mm2_pass(1, 1)
    other_plane = [to_ring(1, 1, *ZH[1], 0)]
    pair[1].append(to_pair(1, ZR, PR - ZR))
    mm2(3, 1)
    other_plane.append(to_ring(3, 1, *ZH[0], 1))
    pair[3].append(to_pair(3, ZR, YR))
    up.wait_recv()
    add_into(1, 1, *ZH[0], rhalf.at[1, 0])
    other_plane.append(to_ring(1, 1, *ZH[0], 0))
    down.wait_recv()
    add_into(3, 1, *ZH[1], rhalf.at[1, 1])
    other_plane.append(to_ring(3, 1, *ZH[1], 1))
    mm2(0, 1)
    last = [out(part(0, 1, ZR, YR), ybuf.at[pl.ds(ZR, YR)], yldev)]

    def add_pair(dz):
        slot = zs[dz] * 2 + yl
        for copy in pair[dz]:
            copy.wait_recv()

        @pl.loop(0, YR // 16)
        def _(k):
            rows = pl.ds(pl.multiple_of(ZR + k * 16, 16), 16)
            some = pl.ds(pl.multiple_of(k * 16, 16), 16)
            tok[slot, rows, :] = (
                tok[slot, rows, :].astype(F32) + yb[dz, some, :].astype(F32)
            ).astype(BF)

    mm2(2, 0)
    up = to_half(0, *ZH[0], 0)
    down = to_half(0, *ZH[1], 1)
    add_pair(2)
    up_y = to_half(0, *YH[0], 0)
    down_y = to_half(0, *YH[1], 1)
    mm2(1, 0)
    last.append(to_ring(1, 0, *ZH[1], 0))
    mm2(3, 0)
    last.append(to_ring(3, 0, *ZH[0], 1))
    for copy in other_plane:
        copy.wait_recv()
    add_into(0, 1, 0, ZR, rfull.at[1, 0], rfull.at[1, 1])
    last.append(out(part(0, 1, 0, ZR), ybuf.at[pl.ds(0, ZR)], yldev))
    up.wait_recv()
    add_into(1, 0, *ZH[0], rhalf.at[0, 0])
    last.append(to_ring(1, 0, *ZH[0], 0))
    down.wait_recv()
    add_into(3, 0, *ZH[1], rhalf.at[0, 1])
    last.append(to_ring(3, 0, *ZH[1], 1))
    add_pair(1)
    last.append(to_ring(1, 0, *YH[1], 0))
    add_pair(3)
    last.append(to_ring(3, 0, *YH[0], 1))
    mm2(0, 0)
    up_y.wait_recv()
    add_into(1, 0, *YH[0], rhalf.at[0, 0])
    last.append(to_ring(1, 0, *YH[0], 0))
    down_y.wait_recv()
    add_into(3, 0, *YH[1], rhalf.at[0, 1])
    last.append(to_ring(3, 0, *YH[1], 1))
    for copy in last:
        copy.wait_recv()

    def total(rows):
        return (
            tok[v, rows, :].astype(F32)
            + rfull[0, 0, rows, :].astype(F32)
            + rfull[0, 1, rows, :].astype(F32)
            + ybuf[rows, :].astype(F32)
        ).astype(BF)

    @pl.loop(0, PR // 48)
    def _(k):
        rows = pl.ds(pl.multiple_of(k * 48, 16), 48)
        gp_ref[rows, :] = total(rows)

    for k in range(QR // 48):
        gq_ref[pl.ds(k * 48, 48), :] = total(pl.ds(PR + k * 48, 48))

    for copy in sent:
        copy.wait_send()


COPIES = 192


def shards(hidden_pass, hidden_query, mask_pass, mask_query, labels, head_weight):
    hbm = pl.BlockSpec(memory_space=pltpu.HBM)
    vmem = pl.BlockSpec(memory_space=pltpu.VMEM)
    grad_pass, grad_query = pl.pallas_call(
        kernel,
        out_shape=(
            jax.ShapeDtypeStruct((PR, F), BF),
            jax.ShapeDtypeStruct((QR, F), BF),
        ),
        in_specs=[hbm] * 6,
        out_specs=(vmem, vmem),
        scratch_shapes=[
            pltpu.VMEM((VOCAB, R, F), BF),
            pltpu.VMEM((VOCAB, 2 * HD, W), BF),
            pltpu.VMEM((R, W), F32),
            pltpu.VMEM((R, W), BF),
            pltpu.VMEM((2, PAD, W), F32),
            pltpu.VMEM((2, PAD, W), F32),
            pltpu.VMEM((ROWS, PAD, W), BF),
            pltpu.VMEM((ROWS, PAD, W), BF),
            pltpu.VMEM((VOCAB, PAD, ROWS * PAD), F32),
            pltpu.VMEM((ROWS, PAD, ROWS * PAD), BF),
            pltpu.VMEM((2, 2, R, F), BF),
            pltpu.VMEM((2, 2, R, F), BF),
            pltpu.VMEM((R, F), BF),
            pltpu.VMEM((4, YR, F), BF),
            pltpu.VMEM((G, LP), jnp.int32),
            pltpu.VMEM((LQ, G), jnp.int32),
            pltpu.SMEM((G,), jnp.int32),
            pltpu.SemaphoreType.DMA((6,)),
            pltpu.SemaphoreType.DMA((COPIES,)),
            pltpu.SemaphoreType.DMA((COPIES,)),
        ],
        compiler_params=pltpu.CompilerParams(
            collective_id=0, has_side_effects=True, vmem_limit_bytes=52 * 1024 * 1024
        ),
        name="step",
    )(
        *(
            pltpu.with_memory_space_constraint(x, pltpu.HBM)
            for x in (
                hidden_pass.reshape(PR, F),
                hidden_query.reshape(QR, F),
                mask_pass,
                mask_query.T,
                labels,
                head_weight,
            )
        )
    )
    return (
        grad_pass.reshape(G, LP, F),
        grad_query.reshape(G, LQ, F),
    )


def solution(mesh):
    return jax.shard_map(
        shards,
        mesh=mesh,
        in_specs=(
            P("rows", None, "vocab"),
            P("rows", None, "vocab"),
            P("rows", None),
            P("rows", None),
            P("rows"),
            P("rows", "vocab"),
        ),
        out_specs=(P("rows", None, "vocab"), P("rows", None, "vocab")),
        check_vma=False,
    )
```

```python
import jax
import jax.numpy as jnp
from jax import lax
from jax.experimental import pallas as pl
from jax.experimental.pallas import tpu as pltpu
from jax.sharding import PartitionSpec as P

MESH = pl.DeviceIdType.MESH
MARGIN = 1.0
SHARPNESS = 16.0
V = 16384
SCALING = SHARPNESS * V ** (-0.5)

G = 12
LP = 64
LQ = 8
PR = G * LP
QR = G * LQ
R = PR + QR
RH = R // 2
ZR = 448
ZH = ((0, 256), (256, 192))
YR = R - ZR
YH = ((448, 208), (656, 208))
F = 512
W = 2048
HD = 256
HH = HD // 2
HY = 96
HX = HD - 2 * HY
LANES = 256
PAD = 16
ROWS = 16
VOCAB = 8
BF = jnp.bfloat16
F32 = jnp.float32

RELATIVE = [(1, 0), (3, 0), (2, 0), (0, 1), (1, 1), (3, 1), (2, 1)]


def where_am_i():
    v = lax.axis_index("vocab")
    r = lax.axis_index("rows")
    return v // 2, v % 2, r // 8, (r // 2) % 4, r % 2


def device(z, yl, yh, x, c):
    return (z * 2 + yl, (yh * 4 + x) * 2 + c)


def kernel(
    hp_ref,
    hq_ref,
    mp_hbm,
    mq_hbm,
    lab_hbm,
    hw_ref,
    gp_ref,
    gq_ref,
    tok,
    head,
    acc,
    slopes,
    totals,
    factor,
    allp,
    allq,
    sbuf,
    gbuf,
    rhalf,
    rfull,
    ybuf,
    yb,
    mp_ref,
    mq_ref,
    lab_ref,
    mask,
    lsem,
    ssem,
    rsem,
):
    z, yl, yh, x, c = where_am_i()
    v = z * 2 + yl
    r = (yh * 4 + x) * 2 + c
    zs = [z, (z + 1) % 4, (z + 2) % 4, (z + 3) % 4]
    xs = [x, (x + 1) % 4, (x + 2) % 4, (x + 3) % 4]
    yls = [yl, 1 - yl]
    yhs = [yh, 1 - yh]
    cs = [c, 1 - c]
    zdev = [device(k, yl, yh, x, c) for k in zs]
    xdev = [device(z, yl, yh, k, c) for k in xs]
    yldev = device(z, 1 - yl, yh, x, c)
    yhdev = device(z, yl, 1 - yh, x, c)
    cdev = device(z, yl, yh, x, 1 - c)

    own_head = yh * 4 + x
    local = [
        pltpu.make_async_copy(hp_ref, tok.at[v, pl.ds(0, PR)], lsem.at[0]),
        pltpu.make_async_copy(hq_ref, tok.at[v, pl.ds(PR, QR)], lsem.at[1]),
        pltpu.make_async_copy(hw_ref, head.at[own_head, pl.ds(c * HD, HD)], lsem.at[2]),
        pltpu.make_async_copy(mp_hbm, mp_ref, lsem.at[3]),
        pltpu.make_async_copy(mq_hbm, mq_ref, lsem.at[4]),
        pltpu.make_async_copy(lab_hbm, lab_ref, lsem.at[5]),
    ]
    for copy in local:
        copy.start()

    peers = [zdev[1], zdev[3], yldev, xdev[1], xdev[3], yhdev, cdev]
    barrier = pltpu.get_barrier_semaphore()
    for peer in peers:
        pl.semaphore_signal(barrier, inc=1, device_id=peer, device_id_type=MESH)
    for copy in local:
        copy.wait()
    pl.semaphore_wait(barrier, len(peers))

    counter = [0]
    sent = []

    def remote(src, dst, dev):
        k = counter[0]
        counter[0] += 1
        copy = pltpu.make_async_remote_copy(
            src_ref=src,
            dst_ref=dst,
            send_sem=ssem.at[k],
            recv_sem=rsem.at[k],
            device_id=dev,
            device_id_type=MESH,
        )
        copy.start()
        return copy

    def send(ref, dev):
        copy = remote(ref, ref, dev)
        sent.append(copy)
        return copy

    def hid(dz, dy, h):
        return tok.at[zs[dz] * 2 + yls[dy], pl.ds(h * RH, RH)]

    def hed(dx, dy, lo, n):
        return head.at[yhs[dy] * 4 + xs[dx], pl.ds(c * HD + lo, n)]

    halves = ((0, HH), (HH, HH))
    ring = ((0, HY), (HY, HY))
    rest = (2 * HY, HX)
    a, b, s = {}, {}, {}
    tok_sent = []

    def a_send(key, ref, dev):
        copy = remote(ref, ref, dev)
        a[key] = copy
        tok_sent.append(copy)

    def b_send(key, dx, dy, part, dev):
        b[key] = send(hed(dx, dy, *part), dev)

    def to_core(dx, dy, part):
        s.setdefault((dx, dy), []).append(send(hed(dx, dy, *part), cdev))

    def b_took(key, dx, dy, part):
        b[key].wait_recv()
        to_core(dx, dy, part)

    a_send(("y", 0), hid(0, 0, 0), yldev)
    a_send(("+", 0), hid(0, 0, 0), zdev[1])
    a_send(("-", 1), hid(0, 0, 1), zdev[3])
    b_send(("+", 0), 0, 0, halves[0], xdev[1])
    b_send(("-", 1), 0, 0, halves[1], xdev[3])
    a_send(("y", 1), hid(0, 0, 1), yldev)
    b_send(("y", 0), 0, 0, ring[0], yhdev)
    b_send(("y", 1), 0, 0, ring[1], yhdev)
    a_send(("+", 1), hid(0, 0, 1), zdev[1])
    a_send(("-", 0), hid(0, 0, 0), zdev[3])
    b_send(("+", 1), 0, 0, halves[1], xdev[1])
    b_send(("-", 0), 0, 0, halves[0], xdev[3])
    b_send(("r", 0), 0, 0, rest, yhdev)
    to_core(0, 0, halves[0])
    to_core(0, 0, halves[1])

    acc[...] = jnp.zeros_like(acc)
    totals[...] = jnp.zeros_like(totals)

    @pl.loop(0, G)
    def _(k):
        line = mp_ref[pl.ds(k, 1), :].astype(F32)
        shape = (LP, LP)
        eye = lax.broadcasted_iota(jnp.int32, shape, 0) == lax.broadcasted_iota(jnp.int32, shape, 1)
        column = jnp.sum(jnp.where(eye, jnp.broadcast_to(line, shape), 0.0), axis=1, keepdims=True)
        mask[pl.ds(pl.multiple_of(k * LP, LP), LP), :] = jnp.broadcast_to(column, (LP, LANES))
        here = lax.broadcasted_iota(jnp.int32, (LQ, G), 1) == k
        column = jnp.sum(jnp.where(here, mq_ref[...].astype(F32), 0.0), axis=1, keepdims=True)
        mask[pl.ds(pl.multiple_of(PR + k * LQ, LQ), LQ), :] = jnp.broadcast_to(column, (LQ, LANES))

    a[("+", 0)].wait_recv()
    a_send("f+", hid(3, 0, 0), zdev[1])
    a[("-", 1)].wait_recv()
    a_send("f-", hid(1, 0, 1), zdev[3])
    b[("+", 0)].wait_recv()
    b_send("f+", 3, 0, halves[0], xdev[1])
    b[("-", 1)].wait_recv()
    b_send("f-", 1, 0, halves[1], xdev[3])
    b_send(("r", 1), 1, 0, rest, yhdev)
    to_core(3, 0, halves[0])
    to_core(1, 0, halves[1])

    a[("y", 0)].wait_recv()
    a_send(("o+", 0), hid(0, 1, 0), zdev[1])
    b_took(("+", 1), 3, 0, halves[1])
    b_send(("r", 3), 3, 0, rest, yhdev)
    b_took(("-", 0), 1, 0, halves[0])
    a[("y", 1)].wait_recv()
    a_send(("o-", 1), hid(0, 1, 1), zdev[3])
    a_send(("o-", 0), hid(0, 1, 0), zdev[3])
    a_send(("o+", 1), hid(0, 1, 1), zdev[1])
    b[("y", 0)].wait_recv()
    b_send(("o+", 0), 0, 1, ring[0], xdev[1])
    b_send(("o-", 0), 0, 1, (0, HY // 2), xdev[3])
    b[("y", 1)].wait_recv()
    b_send(("o-", 1), 0, 1, ring[1], xdev[3])
    b_send(("o-", 2), 0, 1, (HY // 2, HY // 2), xdev[3])
    b_send(("o+", 1), 0, 1, ring[1], xdev[1])
    to_core(0, 1, ring[0])
    to_core(0, 1, ring[1])
    b_took("f+", 2, 0, halves[0])
    b_took("f-", 2, 0, halves[1])
    b_send(("r", 2), 2, 0, rest, yhdev)

    def core_took(dx, dy):
        for copy in s[(dx, dy)]:
            copy.wait_recv()

    def mm1_part(slot, half):
        feats = pl.ds(pl.multiple_of(half * HD, HD), HD)

        @pl.loop(0, 2)
        def _(n):
            cols = pl.ds(pl.multiple_of(n * (W // 2), W // 2), W // 2)
            acc[:, cols] += jnp.dot(
                tok[slot, :, feats], head[slot, feats, cols], preferred_element_type=F32
            )

    def mm1(ready):
        @pl.loop(0, VOCAB)
        def _(slot):
            @pl.when(ready(slot))
            def _():
                @pl.loop(0, 2)
                def _(n):
                    cols = pl.ds(pl.multiple_of(n * (W // 2), W // 2), W // 2)
                    acc[:, cols] += jnp.dot(
                        tok[slot], head[slot, :, cols], preferred_element_type=F32
                    )

    def near_head(slot):
        return slot // 4 == yh

    def near_hidden(slot):
        return slot % 2 == yl

    def early(slot):
        return near_hidden(slot) | (slot // 2 == z)

    def far_head(slot):
        return slot == yhs[1] * 4 + xs[2]

    def far_hidden(slot):
        return jnp.logical_not(near_hidden(slot)) & (slot // 2 == zs[2])

    for key in [("+", 1), ("-", 0), "f+", "f-"]:
        a[key].wait_recv()
    for dx in range(4):
        core_took(dx, 0)
    mm1(lambda slot: near_head(slot) & early(slot))
    a[("o+", 0)].wait_recv()
    a_send("g+", hid(3, 1, 0), zdev[1])
    a[("o-", 1)].wait_recv()
    a_send("g-", hid(1, 1, 1), zdev[3])
    b[("o+", 0)].wait_recv()
    b_send("g+", 3, 1, ring[0], xdev[1])
    to_core(3, 1, ring[0])
    b_took(("r", 0), 0, 1, rest)
    b_took(("o-", 0), 1, 1, (0, HY // 2))
    core_took(0, 1)
    mm1(lambda slot: (slot == yhs[1] * 4 + x) & early(slot))
    b[("o-", 1)].wait_recv()
    b_send("g-", 1, 1, ring[1], xdev[3])
    to_core(1, 1, ring[1])
    a[("o+", 1)].wait_recv()
    a[("o-", 0)].wait_recv()
    mm1(
        lambda slot: (near_head(slot) | (slot == yhs[1] * 4 + x))
        & jnp.logical_not(early(slot))
        & jnp.logical_not(far_hidden(slot))
    )
    b_took(("r", 1), 1, 1, rest)
    b_took(("o-", 2), 1, 1, (HY // 2, HY // 2))
    b_took(("o+", 1), 3, 1, ring[1])
    b_took(("r", 3), 3, 1, rest)
    core_took(1, 1)
    mm1(lambda slot: (slot == yhs[1] * 4 + xs[1]) & jnp.logical_not(far_hidden(slot)))
    core_took(3, 1)
    mm1(lambda slot: (slot == yhs[1] * 4 + xs[3]) & jnp.logical_not(far_hidden(slot)))
    b_took(("r", 2), 2, 1, rest)
    b_took("g+", 2, 1, ring[0])
    b_took("g-", 2, 1, ring[1])
    a["g+"].wait_recv()
    a["g-"].wait_recv()
    mm1(lambda slot: far_hidden(slot) & jnp.logical_not(far_head(slot)))
    mm1_part(yhs[1] * 4 + xs[2], c)
    core_took(2, 1)
    mm1_part(yhs[1] * 4 + xs[2], 1 - c)

    def pool(base, length, k, side, first):
        rows = pl.ds(pl.multiple_of(base + k * length, 8), length)
        weight = mask[rows, :]
        for n in range(first, first + W // 2, LANES):
            cols = pl.ds(n, LANES)
            act = jnp.log1p(jnp.maximum(acc[rows, cols], 0.0))
            square = act * act
            totals[side, pl.ds(k, 1), cols] = jnp.sum(
                square * square * weight, axis=0, keepdims=True
            )

    def slope(base, length, k):
        rows = pl.ds(pl.multiple_of(base + k * length, 8), length)
        weight = mask[rows, :]
        for n in range(0, W, LANES):
            cols = pl.ds(n, LANES)
            high = jnp.maximum(acc[rows, cols], 0.0)
            act = jnp.log1p(high)
            acc[rows, cols] = weight * (act * act * act) / (1.0 + high)

    def fourth_root(t):
        return jnp.sqrt(jnp.sqrt(t))

    def spread(ref, cols):
        mine = ref.at[r, :, cols]
        copies = [send(mine, device(z, yl, yhs[e], xs[d], c)) for d, e in RELATIVE]
        copies.append(send(mine, cdev))
        return copies

    def hand_on(ref, cols, copies):
        handed = []
        for (d, e), copy in zip(RELATIVE, copies):
            copy.wait_recv()
            came = (yhs[e] * 4 + xs[(4 - d) % 4]) * 2 + c
            handed.append(send(ref.at[came, :, cols], cdev))
        return handed

    spread_p = []
    for first in (0, W // 2):
        cols = pl.ds(first, W // 2)

        @pl.loop(0, G)
        def _(k):
            pool(0, LP, k, 0, first)

        allp[r, :, cols] = (fourth_root(totals[0, :, cols] + 1.0) - 1.0).astype(BF)
        spread_p.append((cols, spread(allp, cols)))

    @pl.loop(0, G)
    def _(k):
        pool(PR, LQ, k, 1, 0)
        pool(PR, LQ, k, 1, W // 2)

    whole = pl.ds(0, W)
    allq[r] = (fourth_root(totals[1] + 1.0) - 1.0).astype(BF)

    spread_q = spread(allq, whole)

    @pl.loop(0, G)
    def _(k):
        slope(0, LP, k)

    handed_p = []
    for cols, copies in spread_p:
        handed_p += hand_on(allp, cols, copies)
        handed_p.append(copies[7])
    for copy in handed_p:
        copy.wait_recv()

    every_pass = allp[...].reshape(ROWS * PAD, W)
    sbuf[v] = lax.dot_general(
        allq[r], every_pass, (((1,), (1,)), ((), ())), preferred_element_type=F32
    )
    shared = [send(sbuf.at[v], device(zs[d], yls[e], yh, x, c)) for d, e in RELATIVE]

    @pl.loop(0, G)
    def _(k):
        slope(PR, LQ, k)

    row_at = lax.broadcasted_iota(jnp.int32, (PAD, ROWS * PAD), 0)
    col_at = lax.broadcasted_iota(jnp.int32, (PAD, ROWS * PAD), 1)
    passage = (col_at // PAD) * G + col_at % PAD
    real = (col_at % PAD < G) & (row_at < G)
    label = jnp.full((PAD, ROWS * PAD), -1, jnp.int32)
    for q in range(G):
        label = jnp.where(row_at == q, lab_ref[q], label)
    chosen = (label == passage) & real
    for copy in shared:
        copy.wait_recv()
    scores = sbuf[0]
    for k in range(1, VOCAB):
        scores = scores + sbuf[k]
    scores = scores * SCALING
    onehot = jnp.where(chosen, 1.0, 0.0)
    positive = jnp.sum(scores * onehot, axis=1, keepdims=True)
    weights = jnp.where(
        real & jnp.logical_not(chosen), jax.nn.sigmoid(MARGIN + scores - positive), 0.0
    )
    score_grad = (
        (weights - onehot * jnp.sum(weights, axis=1, keepdims=True)) * SCALING
    ).astype(BF)
    gbuf[r] = score_grad
    group = [send(gbuf.at[r], device(z, yl, yhs[e], xs[d], cs[f])) for d, e in RELATIVE for f in (0, 1)]
    group.append(send(gbuf.at[r], cdev))
    handed_q = hand_on(allq, whole, spread_q)

    def tail(t):
        root = jnp.sqrt(t)
        return 1.0 / (root * jnp.sqrt(root))

    query_grad = jnp.dot(score_grad, every_pass, preferred_element_type=F32)
    factor[1] = query_grad * tail(totals[1] + 1.0)

    @pl.loop(0, G // 2)
    def _(k):
        rows = pl.ds(pl.multiple_of(PR + k * 2 * LQ, 2 * LQ), 2 * LQ)
        upper = lax.broadcasted_iota(jnp.int32, (2 * LQ, W), 0) < LQ
        gain = jnp.where(
            upper,
            jnp.broadcast_to(factor[1, pl.ds(2 * k, 1), :], (2 * LQ, W)),
            jnp.broadcast_to(factor[1, pl.ds(2 * k + 1, 1), :], (2 * LQ, W)),
        )
        slopes[rows, :] = (acc[rows, :] * gain).astype(BF)

    for copy in tok_sent:
        copy.wait_send()

    def part(dz, dy, lo, n):
        return tok.at[zs[dz] * 2 + yls[dy], pl.ds(lo, n)]

    def mm2(dz, dy):
        slot = zs[dz] * 2 + yls[dy]

        @pl.loop(0, F // 256)
        def _(n):
            cols = pl.ds(pl.multiple_of(n * 256, 256), 256)
            tok[slot, :, cols] = lax.dot_general(
                slopes[...],
                head[slot, cols, :],
                (((1,), (1,)), ((), ())),
                preferred_element_type=F32,
            ).astype(BF)

    def mm2_pass(dz, dy):
        slot = zs[dz] * 2 + yls[dy]

        @pl.loop(0, F // 256)
        def _(n):
            cols = pl.ds(pl.multiple_of(n * 256, 256), 256)
            tok[slot, pl.ds(0, PR), cols] = lax.dot_general(
                slopes[pl.ds(0, PR), :],
                head[slot, cols, :],
                (((1,), (1,)), ((), ())),
                preferred_element_type=F32,
            ).astype(BF)

    def mm2_rows(dz, dy, lo, n):
        slot = zs[dz] * 2 + yls[dy]
        rows = pl.ds(lo, n)
        tok[slot, rows, :] = lax.dot_general(
            slopes[rows, :],
            head[slot],
            (((1,), (1,)), ((), ())),
            preferred_element_type=F32,
        ).astype(BF)

    def add_into(dz, dy, lo, size, *others):
        slot = zs[dz] * 2 + yls[dy]

        @pl.loop(0, size // 16)
        def _(k):
            rows = pl.ds(pl.multiple_of(lo + k * 16, 16), 16)
            total = tok[slot, rows, :].astype(F32)
            for other in others:
                total = total + other[rows, :].astype(F32)
            tok[slot, rows, :] = total.astype(BF)

    def out(src, dst, dev):
        copy = remote(src, dst, dev)
        sent.append(copy)
        return copy

    def to_ring(dz, dy, lo, n, ref):
        dev = zdev[1] if ref == 0 else zdev[3]
        return out(part(dz, dy, lo, n), rfull.at[dy, ref, pl.ds(lo, n)], dev)

    def to_half(dy, lo, n, ref):
        dev = zdev[1] if ref == 0 else zdev[3]
        return out(part(2, dy, lo, n), rhalf.at[dy, ref, pl.ds(lo, n)], dev)

    def to_pair(dz, lo, n):
        return out(part(dz, 1, lo, n), yb.at[dz, pl.ds(lo - ZR, n)], yldev)

    pair = {0: [], 1: [], 2: [], 3: []}
    for dz in (2, 1):
        mm2_rows(dz, 1, PR, QR)
        pair[dz].append(to_pair(dz, PR, QR))

    factor[0] = tail(totals[0] + 1.0)
    pick = jnp.where(
        lax.broadcasted_iota(jnp.int32, (ROWS * PAD, PAD), 0)
        == r * PAD + lax.broadcasted_iota(jnp.int32, (ROWS * PAD, PAD), 1),
        1.0,
        0.0,
    ).astype(BF)
    spread_q[7].wait_recv()
    for copy in handed_q:
        copy.wait_recv()
    for copy in group:
        copy.wait_recv()
    mine = jnp.dot(
        gbuf[...].reshape(ROWS * PAD, ROWS * PAD), pick, preferred_element_type=F32
    ).astype(BF)
    pass_grad = lax.dot_general(
        mine,
        allq[...].reshape(ROWS * PAD, W),
        (((0,), (0,)), ((), ())),
        preferred_element_type=F32,
    )
    factor[0] = pass_grad * factor[0]

    def pass_slopes(lo, n):
        @pl.loop(lo // LP, (lo + n) // LP)
        def _(k):
            rows = pl.ds(pl.multiple_of(k * LP, LP), LP)
            for m in range(0, W, 512):
                cols = pl.ds(m, 512)
                slopes[rows, cols] = (acc[rows, cols] * factor[0, pl.ds(k, 1), cols]).astype(BF)

    pass_slopes(*ZH[0])
    mm2_rows(2, 1, *ZH[0])
    up = to_half(1, *ZH[0], 0)
    pass_slopes(*ZH[1])
    mm2_rows(2, 1, *ZH[1])
    down = to_half(1, *ZH[1], 1)
    pass_slopes(ZR, PR - ZR)
    mm2_rows(2, 1, ZR, PR - ZR)
    pair[2].append(to_pair(2, ZR, PR - ZR))
    mm2_pass(1, 1)
    other_plane = [to_ring(1, 1, *ZH[1], 0)]
    pair[1].append(to_pair(1, ZR, PR - ZR))
    mm2(3, 1)
    other_plane.append(to_ring(3, 1, *ZH[0], 1))
    pair[3].append(to_pair(3, ZR, YR))
    up.wait_recv()
    add_into(1, 1, *ZH[0], rhalf.at[1, 0])
    other_plane.append(to_ring(1, 1, *ZH[0], 0))
    down.wait_recv()
    add_into(3, 1, *ZH[1], rhalf.at[1, 1])
    other_plane.append(to_ring(3, 1, *ZH[1], 1))
    mm2(0, 1)
    last_z = []
    last_y = [out(part(0, 1, ZR, YR), ybuf.at[pl.ds(ZR, YR)], yldev)]

    def add_pair(dz):
        slot = zs[dz] * 2 + yl
        for copy in pair[dz]:
            copy.wait_recv()

        @pl.loop(0, YR // 16)
        def _(k):
            rows = pl.ds(pl.multiple_of(ZR + k * 16, 16), 16)
            some = pl.ds(pl.multiple_of(k * 16, 16), 16)
            tok[slot, rows, :] = (
                tok[slot, rows, :].astype(F32) + yb[dz, some, :].astype(F32)
            ).astype(BF)

    mm2(2, 0)
    up = to_half(0, *ZH[0], 0)
    down = to_half(0, *ZH[1], 1)
    add_pair(2)
    up_y = to_half(0, *YH[0], 0)
    down_y = to_half(0, *YH[1], 1)
    mm2(1, 0)
    last_z.append(to_ring(1, 0, *ZH[1], 0))
    mm2(3, 0)
    last_z.append(to_ring(3, 0, *ZH[0], 1))
    for copy in other_plane:
        copy.wait_recv()
    add_into(0, 1, 0, ZR, rfull.at[1, 0], rfull.at[1, 1])
    last_z.append(out(part(0, 1, 0, ZR), ybuf.at[pl.ds(0, ZR)], yldev))
    up.wait_recv()
    add_into(1, 0, *ZH[0], rhalf.at[0, 0])
    last_z.append(to_ring(1, 0, *ZH[0], 0))
    down.wait_recv()
    add_into(3, 0, *ZH[1], rhalf.at[0, 1])
    last_z.append(to_ring(3, 0, *ZH[1], 1))
    add_pair(1)
    last_y.append(to_ring(1, 0, *YH[1], 0))
    add_pair(3)
    last_y.append(to_ring(3, 0, *YH[0], 1))
    mm2(0, 0)
    up_y.wait_recv()
    add_into(1, 0, *YH[0], rhalf.at[0, 0])
    last_y.append(to_ring(1, 0, *YH[0], 0))
    down_y.wait_recv()
    add_into(3, 0, *YH[1], rhalf.at[0, 1])
    last_y.append(to_ring(3, 0, *YH[1], 1))
    def total(rows):
        return (
            tok[v, rows, :].astype(F32)
            + rfull[0, 0, rows, :].astype(F32)
            + rfull[0, 1, rows, :].astype(F32)
            + ybuf[rows, :].astype(F32)
        ).astype(BF)

    def finish(lo, n):
        @pl.loop(0, n // 64)
        def _(k):
            rows = pl.ds(pl.multiple_of(lo + k * 64, 16), 64)
            gp_ref[rows, :] = total(rows)

    for copy in last_z:
        copy.wait_recv()
    finish(0, ZR)
    for copy in last_y:
        copy.wait_recv()
    finish(ZR, PR - ZR)
    for k in range(QR // 48):
        gq_ref[pl.ds(k * 48, 48), :] = total(pl.ds(PR + k * 48, 48))

    for copy in sent:
        copy.wait_send()


COPIES = 192


def shards(hidden_pass, hidden_query, mask_pass, mask_query, labels, head_weight):
    hbm = pl.BlockSpec(memory_space=pltpu.HBM)
    vmem = pl.BlockSpec(memory_space=pltpu.VMEM)
    grad_pass, grad_query = pl.pallas_call(
        kernel,
        out_shape=(
            jax.ShapeDtypeStruct((PR, F), BF),
            jax.ShapeDtypeStruct((QR, F), BF),
        ),
        in_specs=[hbm] * 6,
        out_specs=(vmem, vmem),
        scratch_shapes=[
            pltpu.VMEM((VOCAB, R, F), BF),
            pltpu.VMEM((VOCAB, 2 * HD, W), BF),
            pltpu.VMEM((R, W), F32),
            pltpu.VMEM((R, W), BF),
            pltpu.VMEM((2, PAD, W), F32),
            pltpu.VMEM((2, PAD, W), F32),
            pltpu.VMEM((ROWS, PAD, W), BF),
            pltpu.VMEM((ROWS, PAD, W), BF),
            pltpu.VMEM((VOCAB, PAD, ROWS * PAD), F32),
            pltpu.VMEM((ROWS, PAD, ROWS * PAD), BF),
            pltpu.VMEM((2, 2, R, F), BF),
            pltpu.VMEM((2, 2, R, F), BF),
            pltpu.VMEM((R, F), BF),
            pltpu.VMEM((4, YR, F), BF),
            pltpu.VMEM((G, LP), jnp.int32),
            pltpu.VMEM((LQ, G), jnp.int32),
            pltpu.SMEM((G,), jnp.int32),
            pltpu.VMEM((R, LANES), F32),
            pltpu.SemaphoreType.DMA((6,)),
            pltpu.SemaphoreType.DMA((COPIES,)),
            pltpu.SemaphoreType.DMA((COPIES,)),
        ],
        compiler_params=pltpu.CompilerParams(
            collective_id=0, has_side_effects=True, vmem_limit_bytes=52 * 1024 * 1024
        ),
        name="step",
    )(
        *(
            pltpu.with_memory_space_constraint(x, pltpu.HBM)
            for x in (
                hidden_pass.reshape(PR, F),
                hidden_query.reshape(QR, F),
                mask_pass,
                mask_query.T,
                labels,
                head_weight,
            )
        )
    )
    return (
        grad_pass.reshape(G, LP, F),
        grad_query.reshape(G, LQ, F),
    )


def solution(mesh):
    return jax.shard_map(
        shards,
        mesh=mesh,
        in_specs=(
            P("rows", None, "vocab"),
            P("rows", None, "vocab"),
            P("rows", None),
            P("rows", None),
            P("rows"),
            P("rows", "vocab"),
        ),
        out_specs=(P("rows", None, "vocab"), P("rows", None, "vocab")),
        check_vma=False,
    )
```

```python
import jax
import jax.numpy as jnp
from jax import lax
from jax.experimental import pallas as pl
from jax.experimental.pallas import tpu as pltpu
from jax.sharding import PartitionSpec as P

MESH = pl.DeviceIdType.MESH
MARGIN = 1.0
SHARPNESS = 16.0
V = 16384
SCALING = SHARPNESS * V ** (-0.5)

G = 12
LP = 64
LQ = 8
PR = G * LP
QR = G * LQ
R = PR + QR
RH = R // 2
ZR = 448
ZH = ((0, 256), (256, 192))
YR = R - ZR
YH = ((448, 208), (656, 208))
F = 512
W = 2048
HD = 256
HH = HD // 2
HY = 96
HX = HD - 2 * HY
LANES = 256
PAD = 16
ROWS = 16
VOCAB = 8
BF = jnp.bfloat16
F32 = jnp.float32

RELATIVE = [(1, 0), (3, 0), (2, 0), (0, 1), (1, 1), (3, 1), (2, 1)]


def where_am_i():
    v = lax.axis_index("vocab")
    r = lax.axis_index("rows")
    return v // 2, v % 2, r // 8, (r // 2) % 4, r % 2


def device(z, yl, yh, x, c):
    return (z * 2 + yl, (yh * 4 + x) * 2 + c)


def kernel(
    hp_ref,
    hq_ref,
    mp_hbm,
    mq_hbm,
    lab_hbm,
    hw_ref,
    gp_ref,
    gq_ref,
    tok,
    head,
    acc,
    slopes,
    totals,
    factor,
    allp,
    allq,
    sbuf,
    gbuf,
    rhalf,
    rfull,
    ybuf,
    yb,
    mp_ref,
    mq_ref,
    lab_ref,
    mask,
    lsem,
    ssem,
    rsem,
):
    z, yl, yh, x, c = where_am_i()
    v = z * 2 + yl
    r = (yh * 4 + x) * 2 + c
    zs = [z, (z + 1) % 4, (z + 2) % 4, (z + 3) % 4]
    xs = [x, (x + 1) % 4, (x + 2) % 4, (x + 3) % 4]
    yls = [yl, 1 - yl]
    yhs = [yh, 1 - yh]
    cs = [c, 1 - c]
    zdev = [device(k, yl, yh, x, c) for k in zs]
    xdev = [device(z, yl, yh, k, c) for k in xs]
    yldev = device(z, 1 - yl, yh, x, c)
    yhdev = device(z, yl, 1 - yh, x, c)
    cdev = device(z, yl, yh, x, 1 - c)

    own_head = yh * 4 + x
    local = [
        pltpu.make_async_copy(hp_ref, tok.at[v, pl.ds(0, PR)], lsem.at[0]),
        pltpu.make_async_copy(hq_ref, tok.at[v, pl.ds(PR, QR)], lsem.at[1]),
        pltpu.make_async_copy(hw_ref, head.at[own_head, pl.ds(c * HD, HD)], lsem.at[2]),
        pltpu.make_async_copy(mp_hbm, mp_ref, lsem.at[3]),
        pltpu.make_async_copy(mq_hbm, mq_ref, lsem.at[4]),
        pltpu.make_async_copy(lab_hbm, lab_ref, lsem.at[5]),
    ]
    for copy in local:
        copy.start()

    peers = [zdev[1], zdev[3], yldev, xdev[1], xdev[3], yhdev, cdev]
    barrier = pltpu.get_barrier_semaphore()
    for peer in peers:
        pl.semaphore_signal(barrier, inc=1, device_id=peer, device_id_type=MESH)
    for copy in local:
        copy.wait()
    pl.semaphore_wait(barrier, len(peers))

    counter = [0]
    sent = []

    def remote(src, dst, dev):
        k = counter[0]
        counter[0] += 1
        copy = pltpu.make_async_remote_copy(
            src_ref=src,
            dst_ref=dst,
            send_sem=ssem.at[k],
            recv_sem=rsem.at[k],
            device_id=dev,
            device_id_type=MESH,
        )
        copy.start()
        return copy

    def send(ref, dev):
        copy = remote(ref, ref, dev)
        sent.append(copy)
        return copy

    def hid(dz, dy, h):
        return tok.at[zs[dz] * 2 + yls[dy], pl.ds(h * RH, RH)]

    def hed(dx, dy, lo, n):
        return head.at[yhs[dy] * 4 + xs[dx], pl.ds(c * HD + lo, n)]

    halves = ((0, HH), (HH, HH))
    ring = ((0, HY), (HY, HY))
    rest = (2 * HY, HX)
    a, b, s = {}, {}, {}
    tok_sent = []

    def a_send(key, ref, dev):
        copy = remote(ref, ref, dev)
        a[key] = copy
        tok_sent.append(copy)

    def b_send(key, dx, dy, part, dev):
        b[key] = send(hed(dx, dy, *part), dev)

    def to_core(dx, dy, part):
        s.setdefault((dx, dy), []).append(send(hed(dx, dy, *part), cdev))

    def b_took(key, dx, dy, part):
        b[key].wait_recv()
        to_core(dx, dy, part)

    a_send(("y", 0), hid(0, 0, 0), yldev)
    a_send(("+", 0), hid(0, 0, 0), zdev[1])
    a_send(("-", 1), hid(0, 0, 1), zdev[3])
    b_send(("+", 0), 0, 0, halves[0], xdev[1])
    b_send(("-", 1), 0, 0, halves[1], xdev[3])
    a_send(("y", 1), hid(0, 0, 1), yldev)
    b_send(("y", 0), 0, 0, ring[0], yhdev)
    b_send(("y", 1), 0, 0, ring[1], yhdev)
    a_send(("+", 1), hid(0, 0, 1), zdev[1])
    a_send(("-", 0), hid(0, 0, 0), zdev[3])
    b_send(("+", 1), 0, 0, halves[1], xdev[1])
    b_send(("-", 0), 0, 0, halves[0], xdev[3])
    b_send(("r", 0), 0, 0, rest, yhdev)
    to_core(0, 0, halves[0])
    to_core(0, 0, halves[1])

    acc[...] = jnp.zeros_like(acc)
    totals[...] = jnp.zeros_like(totals)

    @pl.loop(0, G)
    def _(k):
        line = mp_ref[pl.ds(k, 1), :].astype(F32)
        shape = (LP, LP)
        eye = lax.broadcasted_iota(jnp.int32, shape, 0) == lax.broadcasted_iota(jnp.int32, shape, 1)
        column = jnp.sum(jnp.where(eye, jnp.broadcast_to(line, shape), 0.0), axis=1, keepdims=True)
        mask[pl.ds(pl.multiple_of(k * LP, LP), LP), :] = jnp.broadcast_to(column, (LP, LANES))
        here = lax.broadcasted_iota(jnp.int32, (LQ, G), 1) == k
        column = jnp.sum(jnp.where(here, mq_ref[...].astype(F32), 0.0), axis=1, keepdims=True)
        mask[pl.ds(pl.multiple_of(PR + k * LQ, LQ), LQ), :] = jnp.broadcast_to(column, (LQ, LANES))

    a[("+", 0)].wait_recv()
    a_send("f+", hid(3, 0, 0), zdev[1])
    a[("-", 1)].wait_recv()
    a_send("f-", hid(1, 0, 1), zdev[3])
    b[("+", 0)].wait_recv()
    b_send("f+", 3, 0, halves[0], xdev[1])
    b[("-", 1)].wait_recv()
    b_send("f-", 1, 0, halves[1], xdev[3])
    b_send(("r", 1), 1, 0, rest, yhdev)
    to_core(3, 0, halves[0])
    to_core(1, 0, halves[1])

    a[("y", 0)].wait_recv()
    a_send(("o+", 0), hid(0, 1, 0), zdev[1])
    b_took(("+", 1), 3, 0, halves[1])
    b_send(("r", 3), 3, 0, rest, yhdev)
    b_took(("-", 0), 1, 0, halves[0])
    a[("y", 1)].wait_recv()
    a_send(("o-", 1), hid(0, 1, 1), zdev[3])
    a_send(("o-", 0), hid(0, 1, 0), zdev[3])
    a_send(("o+", 1), hid(0, 1, 1), zdev[1])
    b[("y", 0)].wait_recv()
    b_send(("o+", 0), 0, 1, ring[0], xdev[1])
    b_send(("o-", 0), 0, 1, (0, HY // 2), xdev[3])
    b[("y", 1)].wait_recv()
    b_send(("o-", 1), 0, 1, ring[1], xdev[3])
    b_send(("o-", 2), 0, 1, (HY // 2, HY // 2), xdev[3])
    b_send(("o+", 1), 0, 1, ring[1], xdev[1])
    to_core(0, 1, ring[0])
    to_core(0, 1, ring[1])
    b_took("f+", 2, 0, halves[0])
    b_took("f-", 2, 0, halves[1])
    b_send(("r", 2), 2, 0, rest, yhdev)

    def core_took(dx, dy):
        for copy in s[(dx, dy)]:
            copy.wait_recv()

    def mm1_part(slot, half):
        feats = pl.ds(pl.multiple_of(half * HD, HD), HD)

        @pl.loop(0, 2)
        def _(n):
            cols = pl.ds(pl.multiple_of(n * (W // 2), W // 2), W // 2)
            acc[:, cols] += jnp.dot(
                tok[slot, :, feats], head[slot, feats, cols], preferred_element_type=F32
            )

    def mm1(ready):
        @pl.loop(0, VOCAB)
        def _(slot):
            @pl.when(ready(slot))
            def _():
                @pl.loop(0, 2)
                def _(n):
                    cols = pl.ds(pl.multiple_of(n * (W // 2), W // 2), W // 2)
                    acc[:, cols] += jnp.dot(
                        tok[slot], head[slot, :, cols], preferred_element_type=F32
                    )

    def near_head(slot):
        return slot // 4 == yh

    def near_hidden(slot):
        return slot % 2 == yl

    def early(slot):
        return near_hidden(slot) | (slot // 2 == z)

    def far_head(slot):
        return slot == yhs[1] * 4 + xs[2]

    def far_hidden(slot):
        return jnp.logical_not(near_hidden(slot)) & (slot // 2 == zs[2])

    for key in [("+", 1), ("-", 0), "f+", "f-"]:
        a[key].wait_recv()
    for dx in range(4):
        core_took(dx, 0)
    mm1(lambda slot: near_head(slot) & early(slot))
    a[("o+", 0)].wait_recv()
    a_send("g+", hid(3, 1, 0), zdev[1])
    a[("o-", 1)].wait_recv()
    a_send("g-", hid(1, 1, 1), zdev[3])
    b[("o+", 0)].wait_recv()
    b_send("g+", 3, 1, ring[0], xdev[1])
    to_core(3, 1, ring[0])
    b_took(("r", 0), 0, 1, rest)
    b_took(("o-", 0), 1, 1, (0, HY // 2))
    core_took(0, 1)
    mm1(lambda slot: (slot == yhs[1] * 4 + x) & early(slot))
    b[("o-", 1)].wait_recv()
    b_send("g-", 1, 1, ring[1], xdev[3])
    to_core(1, 1, ring[1])
    a[("o+", 1)].wait_recv()
    a[("o-", 0)].wait_recv()
    mm1(
        lambda slot: (near_head(slot) | (slot == yhs[1] * 4 + x))
        & jnp.logical_not(early(slot))
        & jnp.logical_not(far_hidden(slot))
    )
    b_took(("r", 1), 1, 1, rest)
    b_took(("o-", 2), 1, 1, (HY // 2, HY // 2))
    b_took(("o+", 1), 3, 1, ring[1])
    b_took(("r", 3), 3, 1, rest)
    core_took(1, 1)
    mm1(lambda slot: (slot == yhs[1] * 4 + xs[1]) & jnp.logical_not(far_hidden(slot)))
    core_took(3, 1)
    mm1(lambda slot: (slot == yhs[1] * 4 + xs[3]) & jnp.logical_not(far_hidden(slot)))
    b_took(("r", 2), 2, 1, rest)
    b_took("g+", 2, 1, ring[0])
    b_took("g-", 2, 1, ring[1])
    a["g+"].wait_recv()
    a["g-"].wait_recv()
    mm1(lambda slot: far_hidden(slot) & jnp.logical_not(far_head(slot)))
    mm1_part(yhs[1] * 4 + xs[2], c)
    core_took(2, 1)
    mm1_part(yhs[1] * 4 + xs[2], 1 - c)

    def pool(base, length, k, side, first):
        rows = pl.ds(pl.multiple_of(base + k * length, 8), length)
        weight = mask[rows, :]
        for n in range(first, first + W // 2, LANES):
            cols = pl.ds(n, LANES)
            act = jnp.log1p(jnp.maximum(acc[rows, cols], 0.0))
            square = act * act
            totals[side, pl.ds(k, 1), cols] = jnp.sum(
                square * square * weight, axis=0, keepdims=True
            )

    def slope(base, length, k):
        rows = pl.ds(pl.multiple_of(base + k * length, 8), length)
        weight = mask[rows, :]
        for n in range(0, W, LANES):
            cols = pl.ds(n, LANES)
            high = jnp.maximum(acc[rows, cols], 0.0)
            act = jnp.log1p(high)
            acc[rows, cols] = weight * (act * act * act) / (1.0 + high)

    def fourth_root(t):
        return jnp.sqrt(jnp.sqrt(t))

    def spread(ref, cols):
        mine = ref.at[r, :, cols]
        copies = [send(mine, device(z, yl, yhs[e], xs[d], c)) for d, e in RELATIVE]
        copies.append(send(mine, cdev))
        return copies

    def hand_on(ref, cols, copies):
        handed = []
        for (d, e), copy in zip(RELATIVE, copies):
            copy.wait_recv()
            came = (yhs[e] * 4 + xs[(4 - d) % 4]) * 2 + c
            handed.append(send(ref.at[came, :, cols], cdev))
        return handed

    spread_p = []
    for first in (0, W // 2):
        cols = pl.ds(first, W // 2)

        @pl.loop(0, G)
        def _(k):
            pool(0, LP, k, 0, first)

        allp[r, :, cols] = (fourth_root(totals[0, :, cols] + 1.0) - 1.0).astype(BF)
        spread_p.append((cols, spread(allp, cols)))

    @pl.loop(0, G)
    def _(k):
        pool(PR, LQ, k, 1, 0)
        pool(PR, LQ, k, 1, W // 2)

    whole = pl.ds(0, W)
    allq[r] = (fourth_root(totals[1] + 1.0) - 1.0).astype(BF)

    spread_q = spread(allq, whole)

    @pl.loop(0, G)
    def _(k):
        slope(0, LP, k)

    handed_p = []
    for cols, copies in spread_p:
        handed_p += hand_on(allp, cols, copies)
        handed_p.append(copies[7])
    for copy in handed_p:
        copy.wait_recv()

    every_pass = allp[...].reshape(ROWS * PAD, W)
    sbuf[v] = lax.dot_general(
        allq[r], every_pass, (((1,), (1,)), ((), ())), preferred_element_type=F32
    )
    shared = [send(sbuf.at[v], device(zs[d], yls[e], yh, x, c)) for d, e in RELATIVE]

    @pl.loop(0, G)
    def _(k):
        slope(PR, LQ, k)

    row_at = lax.broadcasted_iota(jnp.int32, (PAD, ROWS * PAD), 0)
    col_at = lax.broadcasted_iota(jnp.int32, (PAD, ROWS * PAD), 1)
    passage = (col_at // PAD) * G + col_at % PAD
    real = (col_at % PAD < G) & (row_at < G)
    label = jnp.full((PAD, ROWS * PAD), -1, jnp.int32)
    for q in range(G):
        label = jnp.where(row_at == q, lab_ref[q], label)
    chosen = (label == passage) & real
    for copy in shared:
        copy.wait_recv()
    scores = sbuf[0]
    for k in range(1, VOCAB):
        scores = scores + sbuf[k]
    scores = scores * SCALING
    onehot = jnp.where(chosen, 1.0, 0.0)
    positive = jnp.sum(scores * onehot, axis=1, keepdims=True)
    weights = jnp.where(
        real & jnp.logical_not(chosen), jax.nn.sigmoid(MARGIN + scores - positive), 0.0
    )
    score_grad = (
        (weights - onehot * jnp.sum(weights, axis=1, keepdims=True)) * SCALING
    ).astype(BF)
    gbuf[r] = score_grad
    group = [send(gbuf.at[r], device(z, yl, yhs[e], xs[d], cs[f])) for d, e in RELATIVE for f in (0, 1)]
    group.append(send(gbuf.at[r], cdev))
    handed_q = hand_on(allq, whole, spread_q)

    def tail(t):
        root = jnp.sqrt(t)
        return 1.0 / (root * jnp.sqrt(root))

    query_grad = jnp.dot(score_grad, every_pass, preferred_element_type=F32)
    factor[1] = query_grad * tail(totals[1] + 1.0)

    @pl.loop(0, G // 2)
    def _(k):
        rows = pl.ds(pl.multiple_of(PR + k * 2 * LQ, 2 * LQ), 2 * LQ)
        upper = lax.broadcasted_iota(jnp.int32, (2 * LQ, W), 0) < LQ
        gain = jnp.where(
            upper,
            jnp.broadcast_to(factor[1, pl.ds(2 * k, 1), :], (2 * LQ, W)),
            jnp.broadcast_to(factor[1, pl.ds(2 * k + 1, 1), :], (2 * LQ, W)),
        )
        slopes[rows, :] = (acc[rows, :] * gain).astype(BF)

    for copy in tok_sent:
        copy.wait_send()

    def part(dz, dy, lo, n):
        return tok.at[zs[dz] * 2 + yls[dy], pl.ds(lo, n)]

    def mm2(dz, dy):
        slot = zs[dz] * 2 + yls[dy]

        @pl.loop(0, F // 256)
        def _(n):
            cols = pl.ds(pl.multiple_of(n * 256, 256), 256)
            tok[slot, :, cols] = lax.dot_general(
                slopes[...],
                head[slot, cols, :],
                (((1,), (1,)), ((), ())),
                preferred_element_type=F32,
            ).astype(BF)

    def mm2_pass(dz, dy):
        slot = zs[dz] * 2 + yls[dy]

        @pl.loop(0, F // 256)
        def _(n):
            cols = pl.ds(pl.multiple_of(n * 256, 256), 256)
            tok[slot, pl.ds(0, PR), cols] = lax.dot_general(
                slopes[pl.ds(0, PR), :],
                head[slot, cols, :],
                (((1,), (1,)), ((), ())),
                preferred_element_type=F32,
            ).astype(BF)

    def mm2_rows(dz, dy, lo, n):
        slot = zs[dz] * 2 + yls[dy]
        rows = pl.ds(lo, n)
        tok[slot, rows, :] = lax.dot_general(
            slopes[rows, :],
            head[slot],
            (((1,), (1,)), ((), ())),
            preferred_element_type=F32,
        ).astype(BF)

    def add_into(dz, dy, lo, size, *others):
        slot = zs[dz] * 2 + yls[dy]

        block = 64 if size % 64 == 0 else 16

        @pl.loop(0, size // block)
        def _(k):
            rows = pl.ds(pl.multiple_of(lo + k * block, 16), block)
            total = tok[slot, rows, :].astype(F32)
            for other in others:
                total = total + other[rows, :].astype(F32)
            tok[slot, rows, :] = total.astype(BF)

    def out(src, dst, dev):
        copy = remote(src, dst, dev)
        sent.append(copy)
        return copy

    def to_ring(dz, dy, lo, n, ref):
        dev = zdev[1] if ref == 0 else zdev[3]
        return out(part(dz, dy, lo, n), rfull.at[dy, ref, pl.ds(lo, n)], dev)

    def to_half(dy, lo, n, ref):
        dev = zdev[1] if ref == 0 else zdev[3]
        return out(part(2, dy, lo, n), rhalf.at[dy, ref, pl.ds(lo, n)], dev)

    def to_pair(dz, lo, n):
        return out(part(dz, 1, lo, n), yb.at[dz, pl.ds(lo - ZR, n)], yldev)

    pair = {0: [], 1: [], 2: [], 3: []}
    for dz in (2, 1):
        mm2_rows(dz, 1, PR, QR)
        pair[dz].append(to_pair(dz, PR, QR))

    factor[0] = tail(totals[0] + 1.0)
    pick = jnp.where(
        lax.broadcasted_iota(jnp.int32, (ROWS * PAD, PAD), 0)
        == r * PAD + lax.broadcasted_iota(jnp.int32, (ROWS * PAD, PAD), 1),
        1.0,
        0.0,
    ).astype(BF)
    spread_q[7].wait_recv()
    for copy in handed_q:
        copy.wait_recv()
    for copy in group:
        copy.wait_recv()
    mine = jnp.dot(
        gbuf[...].reshape(ROWS * PAD, ROWS * PAD), pick, preferred_element_type=F32
    ).astype(BF)
    pass_grad = lax.dot_general(
        mine,
        allq[...].reshape(ROWS * PAD, W),
        (((0,), (0,)), ((), ())),
        preferred_element_type=F32,
    )
    factor[0] = pass_grad * factor[0]

    def pass_slopes(lo, n):
        @pl.loop(lo // LP, (lo + n) // LP)
        def _(k):
            rows = pl.ds(pl.multiple_of(k * LP, LP), LP)
            for m in range(0, W, 512):
                cols = pl.ds(m, 512)
                slopes[rows, cols] = (acc[rows, cols] * factor[0, pl.ds(k, 1), cols]).astype(BF)

    pass_slopes(*ZH[0])
    mm2_rows(2, 1, *ZH[0])
    up = to_half(1, *ZH[0], 0)
    pass_slopes(*ZH[1])
    mm2_rows(2, 1, *ZH[1])
    down = to_half(1, *ZH[1], 1)
    pass_slopes(ZR, PR - ZR)
    mm2_rows(2, 1, ZR, PR - ZR)
    pair[2].append(to_pair(2, ZR, PR - ZR))
    mm2_pass(1, 1)
    other_plane = [to_ring(1, 1, *ZH[1], 0)]
    pair[1].append(to_pair(1, ZR, PR - ZR))
    mm2(3, 1)
    other_plane.append(to_ring(3, 1, *ZH[0], 1))
    pair[3].append(to_pair(3, ZR, YR))
    up.wait_recv()
    add_into(1, 1, *ZH[0], rhalf.at[1, 0])
    other_plane.append(to_ring(1, 1, *ZH[0], 0))
    down.wait_recv()
    add_into(3, 1, *ZH[1], rhalf.at[1, 1])
    other_plane.append(to_ring(3, 1, *ZH[1], 1))
    mm2(0, 1)
    last_z = []
    last_y = [out(part(0, 1, ZR, YR), ybuf.at[pl.ds(ZR, YR)], yldev)]

    def add_pair(dz):
        slot = zs[dz] * 2 + yl
        for copy in pair[dz]:
            copy.wait_recv()

        @pl.loop(0, YR // 16)
        def _(k):
            rows = pl.ds(pl.multiple_of(ZR + k * 16, 16), 16)
            some = pl.ds(pl.multiple_of(k * 16, 16), 16)
            tok[slot, rows, :] = (
                tok[slot, rows, :].astype(F32) + yb[dz, some, :].astype(F32)
            ).astype(BF)

    mm2(2, 0)
    up = to_half(0, *ZH[0], 0)
    down = to_half(0, *ZH[1], 1)
    add_pair(2)
    up_y = to_half(0, *YH[0], 0)
    down_y = to_half(0, *YH[1], 1)
    mm2(1, 0)
    last_z.append(to_ring(1, 0, *ZH[1], 0))
    mm2(3, 0)
    last_z.append(to_ring(3, 0, *ZH[0], 1))
    for copy in other_plane:
        copy.wait_recv()
    add_into(0, 1, 0, ZR, rfull.at[1, 0], rfull.at[1, 1])
    last_z.append(out(part(0, 1, 0, ZR), ybuf.at[pl.ds(0, ZR)], yldev))
    up.wait_recv()
    add_into(1, 0, *ZH[0], rhalf.at[0, 0])
    last_z.append(to_ring(1, 0, *ZH[0], 0))
    down.wait_recv()
    add_into(3, 0, *ZH[1], rhalf.at[0, 1])
    last_z.append(to_ring(3, 0, *ZH[1], 1))
    add_pair(1)
    last_y.append(to_ring(1, 0, *YH[1], 0))
    add_pair(3)
    last_y.append(to_ring(3, 0, *YH[0], 1))
    mm2(0, 0)
    up_y.wait_recv()
    add_into(1, 0, *YH[0], rhalf.at[0, 0])
    last_y.append(to_ring(1, 0, *YH[0], 0))
    down_y.wait_recv()
    add_into(3, 0, *YH[1], rhalf.at[0, 1])
    last_y.append(to_ring(3, 0, *YH[1], 1))
    def total(rows):
        return (
            tok[v, rows, :].astype(F32)
            + rfull[0, 0, rows, :].astype(F32)
            + rfull[0, 1, rows, :].astype(F32)
            + ybuf[rows, :].astype(F32)
        ).astype(BF)

    def finish(lo, n):
        @pl.loop(0, n // 64)
        def _(k):
            rows = pl.ds(pl.multiple_of(lo + k * 64, 16), 64)
            gp_ref[rows, :] = total(rows)

    for copy in last_z:
        copy.wait_recv()
    finish(0, ZR)
    for copy in last_y:
        copy.wait_recv()
    finish(ZR, PR - ZR)
    for k in range(QR // 48):
        gq_ref[pl.ds(k * 48, 48), :] = total(pl.ds(PR + k * 48, 48))

    for copy in sent:
        copy.wait_send()


COPIES = 192


def shards(hidden_pass, hidden_query, mask_pass, mask_query, labels, head_weight):
    hbm = pl.BlockSpec(memory_space=pltpu.HBM)
    vmem = pl.BlockSpec(memory_space=pltpu.VMEM)
    grad_pass, grad_query = pl.pallas_call(
        kernel,
        out_shape=(
            jax.ShapeDtypeStruct((PR, F), BF),
            jax.ShapeDtypeStruct((QR, F), BF),
        ),
        in_specs=[hbm] * 6,
        out_specs=(vmem, vmem),
        scratch_shapes=[
            pltpu.VMEM((VOCAB, R, F), BF),
            pltpu.VMEM((VOCAB, 2 * HD, W), BF),
            pltpu.VMEM((R, W), F32),
            pltpu.VMEM((R, W), BF),
            pltpu.VMEM((2, PAD, W), F32),
            pltpu.VMEM((2, PAD, W), F32),
            pltpu.VMEM((ROWS, PAD, W), BF),
            pltpu.VMEM((ROWS, PAD, W), BF),
            pltpu.VMEM((VOCAB, PAD, ROWS * PAD), F32),
            pltpu.VMEM((ROWS, PAD, ROWS * PAD), BF),
            pltpu.VMEM((2, 2, R, F), BF),
            pltpu.VMEM((2, 2, R, F), BF),
            pltpu.VMEM((R, F), BF),
            pltpu.VMEM((4, YR, F), BF),
            pltpu.VMEM((G, LP), jnp.int32),
            pltpu.VMEM((LQ, G), jnp.int32),
            pltpu.SMEM((G,), jnp.int32),
            pltpu.VMEM((R, LANES), F32),
            pltpu.SemaphoreType.DMA((6,)),
            pltpu.SemaphoreType.DMA((COPIES,)),
            pltpu.SemaphoreType.DMA((COPIES,)),
        ],
        compiler_params=pltpu.CompilerParams(
            collective_id=0, has_side_effects=True, vmem_limit_bytes=52 * 1024 * 1024
        ),
        name="step",
    )(
        *(
            pltpu.with_memory_space_constraint(x, pltpu.HBM)
            for x in (
                hidden_pass.reshape(PR, F),
                hidden_query.reshape(QR, F),
                mask_pass,
                mask_query.T,
                labels,
                head_weight,
            )
        )
    )
    return (
        grad_pass.reshape(G, LP, F),
        grad_query.reshape(G, LQ, F),
    )


def solution(mesh):
    return jax.shard_map(
        shards,
        mesh=mesh,
        in_specs=(
            P("rows", None, "vocab"),
            P("rows", None, "vocab"),
            P("rows", None),
            P("rows", None),
            P("rows"),
            P("rows", "vocab"),
        ),
        out_specs=(P("rows", None, "vocab"), P("rows", None, "vocab")),
        check_vma=False,
    )
```
